32 devices in a mesh: dp: 8 (over z, x), fsdp: 4 (over y, core).
Axes of the slice: x: 2, y: 2, z: 4, core: 2. Of those that a mesh axis runs over, the one named last changes fastest.
Arguments:
- patches: bfloat16 [25088, 768], P(('dp', 'fsdp')), may hold values from -6 to 6
- lengths: int32 [32, 4], P(('dp', 'fsdp')), may hold values from 0 to 784, as said below
- cotangent: bfloat16 [25088, 768], P(('dp', 'fsdp')), may hold values from -6 to 6
- owners: int32 [432], replicated, may hold values from 0 to 447, as said below
- master: float32 [448, 128, 128], P(('dp', 'fsdp')), as said below
- first_moment: float32 [448, 128, 128], P(('dp', 'fsdp')), may hold values from -3 to 3
- second_moment: float32 [448, 128, 128], P(('dp', 'fsdp')), may hold values from 0.25 to 1
- left_basis: float32 [448, 128, 128], P(('dp', 'fsdp')), as said below
- right_basis: float32 [448, 128, 128], P(('dp', 'fsdp')), as said below
- vectors: float32 [12, 768], replicated, as said below
- vector_first: float32 [12, 768], replicated, may hold values from -3 to 3
- vector_second: float32 [12, 768], replicated, may hold values from 0.25 to 1
Outputs:
- result: bfloat16 [25088, 768], P(('dp', 'fsdp'))
- grad_input: bfloat16 [25088, 768], P(('dp', 'fsdp'))
- clip_norm: float32 [], replicated
- new_master: float32 [448, 128, 128], P(('dp', 'fsdp'))
- new_first: float32 [448, 128, 128], P(('dp', 'fsdp'))
- new_second: float32 [448, 128, 128], P(('dp', 'fsdp'))
- new_vectors: float32 [12, 768], replicated
- new_vector_first: float32 [12, 768], replicated
- new_vector_second: float32 [12, 768], replicated
The draws below stay inside these ranges and needn't reach their ends.
Inputs may be any that keep to these rules, and one draw needn't show every extreme that they name: `lengths`: row d lists the patch counts of device d's images (devices in the order of dp+fsdp): each count is 0, 196 or 784, nonzero counts come first, and their sum lies between half of 784 and 784. Distinct slot numbers: block b of the stacked weight blocks lives in slot owners[b]; slot s belongs to device s // 14 in the order of dp+fsdp; other slots hold no weight. `master`: slots named in owners hold the layer's weight blocks. `left_basis`: each slot's matrix is orthogonal. `right_basis`: each slot's matrix is orthogonal. `vectors`: rows in the order of the steps: the two norms' gains near one, the rest biases.
All inputs are finite; a program needn't handle non-finite values.
Results may differ from the reference program's by a relative error of at most 0.012.
Values may be sent and summed in bfloat16 or wider, within the bound.
No kernel may reach another device: no remote copies, remote signals or barrier semaphores. Data moves between devices by JAX's collectives and lax.ppermute only.
A program may use at most 256 MiB of HBM per device.

```python
import math
import jax
import jax.numpy as jnp
from jax import lax

D = 768
HEADS = 12
HD = 64
FF = 3072
B = 128
P_SMALL = 196
P_LARGE = 784
ROWS_DEV = 784
STEP = 2
IMGS = 4
NBLK = 432
SLOTS = 448
ROWS = 25088
DEVICES = 32


def owner_list(key):
    base = jax.random.fold_in(key, 17)
    first, second = jax.random.split(base)
    inner = jax.random.permutation(first, SLOTS - 2)[:NBLK - 2].astype(jnp.int32) + 1
    listed = jnp.concatenate([jnp.array([0, SLOTS - 1], jnp.int32), inner])
    order = jax.random.permutation(second, NBLK)
    return listed[order].astype(jnp.int32)


def orthogonal_set(key):
    first, second, third, fourth = jax.random.split(key, 4)
    row_perm = jax.vmap(lambda sub: jax.random.permutation(sub, B))(jax.random.split(first, SLOTS))
    col_perm = jax.vmap(lambda sub: jax.random.permutation(sub, B))(jax.random.split(second, SLOTS))
    row_sign = (jax.random.randint(third, (SLOTS, B), 0, 2) * 2 - 1).astype(jnp.float32)
    col_sign = (jax.random.randint(fourth, (SLOTS, B), 0, 2) * 2 - 1).astype(jnp.float32)
    freq = row_perm[:, :, None].astype(jnp.float32)
    place = col_perm[:, None, :].astype(jnp.float32)
    weight = jnp.where(freq == 0.0, math.sqrt(1.0 / B), math.sqrt(2.0 / B))
    table = weight * jnp.cos(math.pi * (place + 0.5) * freq / B)
    return (table * row_sign[:, :, None] * col_sign[:, None, :]).astype(jnp.float32)


def draw_lengths(key, part):
    base = jax.random.fold_in(key, 41)
    first, second = jax.random.split(base)
    large = jax.random.randint(first, (DEVICES,), 0, ROWS_DEV // P_LARGE + 1)
    large = jnp.where(jnp.arange(DEVICES) == 0, jnp.maximum(large, 1), large)
    spare = ROWS_DEV - large * P_LARGE
    most = spare // P_SMALL
    least = jnp.maximum((ROWS_DEV // 2 - large * P_LARGE + P_SMALL - 1) // P_SMALL, 0)
    small = jax.random.randint(second, (DEVICES,), least, most + 1)
    column = jnp.arange(IMGS)[None, :]
    counts = jnp.where(column < large[:, None], P_LARGE, jnp.where(column < (large + small)[:, None], P_SMALL, 0))
    return counts.astype(jnp.int32)


def draw_owners(key, part):
    return owner_list(key)


def draw_master(key, part):
    owners = owner_list(key)
    side = D // B
    up_count = side * (FF // B)
    kinds = jnp.concatenate([jnp.full((3 * side * side,), 1.0, jnp.float32), jnp.full((side * side,), 8.0, jnp.float32), jnp.full((up_count,), 1.0, jnp.float32), jnp.full((up_count,), 0.5, jnp.float32)])
    scale = jnp.ones((SLOTS,), jnp.float32).at[owners].set(kinds) / math.sqrt(D)
    noise = jax.random.normal(jax.random.fold_in(key, 23), (SLOTS, B, B), jnp.float32)
    return noise * scale[:, None, None]


def draw_left_basis(key, part):
    return orthogonal_set(jax.random.fold_in(key, 31))


def draw_right_basis(key, part):
    return orthogonal_set(jax.random.fold_in(key, 37))


def draw_vectors(key, part):
    noise = jax.random.normal(jax.random.fold_in(key, 53), (12, D), jnp.float32)
    index = jnp.arange(12)[:, None]
    gains = (index == 0) | (index == 5)
    return jnp.where(gains, 1.0 + 0.1 * noise, 0.2 * noise).astype(jnp.float32)


def block_scale(rng, extent, cuts, low, largest):
    def one(dim, parts):
        steps = jax.random.uniform(jax.random.fold_in(jax.random.fold_in(rng, 6), dim), (parts,), jnp.float32, low / len(cuts), largest / len(cuts))
        return jnp.repeat(jnp.exp(steps), extent[dim] // parts).reshape((-1,) + (1,) * (len(extent) - dim - 1))

    level = one(*cuts[0])
    for cut in cuts[1:]:
        level = level * one(*cut)
    return level


def gaussian(rng, extent, spread, most, cuts=(), kind=jnp.bfloat16):
    level = block_scale(rng, extent, cuts, -0.22, 0.18) if cuts else 1.0
    result = jax.random.normal(rng, extent, jnp.float32) * spread * level
    return jnp.minimum(jnp.maximum(result, -most), most).astype(kind)


def setup_inputs(seed: int = 0) -> dict:
    arg_keys = jax.random.split(jax.random.key(seed), 13)
    patches = gaussian(arg_keys[0], (ROWS, D), 1.0, 6.0, ((0, 32),))
    lengths = draw_lengths(jax.random.fold_in(arg_keys[12], 71), 0)
    cotangent = gaussian(arg_keys[2], (ROWS, D), 1.0, 6.0, ((0, 32),))
    owners = draw_owners(jax.random.fold_in(arg_keys[12], 71), 0)
    master = draw_master(jax.random.fold_in(arg_keys[12], 71), 0)
    first_moment = gaussian(arg_keys[5], (SLOTS, B, B), 0.5, 3.0, ((0, 32),), jnp.float32)
    second_moment = jnp.clip(jnp.exp(math.log(1.0) - 1.3862944 * jax.random.uniform(arg_keys[6], (SLOTS, B, B), jnp.float32) ** block_scale(arg_keys[6], (SLOTS, B, B), ((0, 32),), -0.2, 0.2)), 0.25, 1.0)
    left_basis = draw_left_basis(jax.random.fold_in(arg_keys[12], 71), 0)
    right_basis = draw_right_basis(jax.random.fold_in(arg_keys[12], 71), 0)
    vectors = draw_vectors(jax.random.fold_in(arg_keys[12], 71), 0)
    vector_first = gaussian(arg_keys[10], (12, D), 0.5, 3.0, (), jnp.float32)
    vector_second = jnp.clip(jnp.exp(jax.random.uniform(arg_keys[11], (12, D), jnp.float32, math.log(0.25), math.log(1.0))), 0.25, 1.0)
    return dict(patches=patches, lengths=lengths, cotangent=cotangent, owners=owners, master=master, first_moment=first_moment, second_moment=second_moment, left_basis=left_basis, right_basis=right_basis, vectors=vectors, vector_first=vector_first, vector_second=vector_second)


@jax.custom_vjp
def low(v):
    return lax.optimization_barrier(v.astype(jnp.bfloat16)).astype(jnp.float32)

@jax.custom_vjp
def low_back(v):
    return v

def low_keep(v):
    return (low(v), None)

def low_pass(kept, grad):
    return (grad,)

def back_keep(v):
    return (v, None)

def back_low(kept, grad):
    return (low(grad),)
low.defvjp(low_keep, low_pass)
low_back.defvjp(back_keep, back_low)
masked_value = -1000000000.0
norm_eps = 1e-06
adam_eps = 1e-08
beta = 0.5
rate_matrix = 0.03
rate_vector = 0.05
decay_weight = 0.01
highest = lax.Precision.HIGHEST

def layer_norm(values, gain, shift):
    center = values - lax.optimization_barrier(jnp.mean(values, axis=-1, keepdims=True))
    factor = lax.rsqrt(lax.optimization_barrier(jnp.mean(center * center, axis=-1, keepdims=True)) + norm_eps)
    return center * factor * gain + shift

def layout(counts, rows):
    ends = jnp.cumsum(counts).astype(jnp.int32)
    places = jnp.arange(rows, dtype=jnp.int32)
    image = lax.optimization_barrier(jnp.sum((places[:, None] >= ends[None, :]).astype(jnp.int32), axis=1)).astype(jnp.int32)
    within = places < ends[-1]
    image = jnp.where(within, image, -1).astype(jnp.int32)
    return (image, within.astype(jnp.float32)[:, None])

def to_blocks(matrix, size):
    height, breadth = matrix.shape
    return matrix.reshape(height // size, size, breadth // size, size).transpose(0, 2, 1, 3).reshape(-1, size, size)

def from_blocks(blocks, height, breadth, size):
    return blocks.reshape(height // size, breadth // size, size, size).transpose(0, 2, 1, 3).reshape(height, breadth)

def split_blocks(blocks, width, hidden, size):
    side = width // size
    counts = [3 * side * side, side * side, side * (hidden // size), side * (hidden // size)]
    shapes = [(width, 3 * width), (width, width), (width, hidden), (hidden, width)]
    matrices = []
    begin = 0
    for count, shape in zip(counts, shapes):
        matrices.append(from_blocks(blocks[begin:begin + count], shape[0], shape[1], size))
        begin += count
    return matrices

def forward(weights, vectors, inputs, image, inside):
    w_attn, w_out, w_up, w_down = weights
    rows, width = inputs.shape
    normed = low(layer_norm(inputs, vectors[0], vectors[1]))
    bias_attn = jnp.concatenate([vectors[2], jnp.zeros_like(vectors[2]), vectors[3]])
    project = low_back(low(jnp.dot(normed, w_attn, precision=highest) + bias_attn))
    query = project[:, :width].reshape(rows, HEADS, HD)
    keys = project[:, width:2 * width].reshape(rows, HEADS, HD)
    values = project[:, 2 * width:].reshape(rows, HEADS, HD)
    scores = low_back(jnp.einsum('qhd,khd->hqk', query, keys, precision=highest) * HD ** (-0.5))
    same = image[:, None] == image[None, :]
    scores = jnp.where(same[None], scores, masked_value)
    peak = lax.optimization_barrier(jnp.max(scores, axis=-1, keepdims=True))
    expd = jnp.exp(scores - peak)
    probs = low(expd / lax.optimization_barrier(jnp.sum(expd, axis=-1, keepdims=True)))
    mixed = low_back(low(jnp.einsum('hqk,khd->qhd', probs, values, precision=highest).reshape(rows, width)))
    branch = low_back(jnp.dot(mixed, w_out, precision=highest) + vectors[4])
    middle = inputs + inside * branch
    second = low(layer_norm(middle, vectors[5], vectors[6]))
    pre = low_back(jnp.dot(second, w_up, precision=highest) + vectors[7:11].reshape(-1))
    active = low(jax.nn.gelu(pre, approximate=False))
    output = low_back(jnp.dot(active, w_down, precision=highest) + vectors[11])
    return middle + inside * output

def reference(patches, lengths, cotangent, owners, master, first_moment, second_moment, left_basis, right_basis, vectors, vector_first, vector_second):
    size = master.shape[1]
    width = patches.shape[1]
    hidden = 4 * width
    chosen = jnp.take(master, owners, axis=0)
    chosen = lax.optimization_barrier(chosen.astype(jnp.bfloat16)).astype(jnp.float32)
    weights = tuple(split_blocks(chosen, width, hidden, size))
    inputs = patches.reshape(DEVICES, ROWS_DEV, width)
    backs = cotangent.reshape(DEVICES, ROWS_DEV, width)

    def device(carry, item):
        part_in, part_count, part_back = item
        image, inside = layout(part_count, ROWS_DEV)

        def run(weights_in, vectors_in, inputs_in):
            return forward(weights_in, vectors_in, inputs_in, image, inside)
        outcome, pull = jax.vjp(run, weights, vectors, part_in.astype(jnp.float32))
        grad_w, grad_v, grad_x = pull(part_back.astype(jnp.float32))
        summed = tuple((old + new for old, new in zip(carry[0], grad_w)))
        return ((summed, carry[1] + grad_v), (outcome.astype(jnp.bfloat16), grad_x.astype(jnp.bfloat16)))
    start = (tuple((jnp.zeros_like(matrix) for matrix in weights)), jnp.zeros_like(vectors))
    (grad_w, grad_v), (outputs, grad_in) = lax.scan(device, start, (inputs, lengths, backs))
    grad_blocks = jnp.concatenate([to_blocks(matrix, size) for matrix in grad_w])
    clip_norm = jnp.sqrt(jnp.sum(grad_blocks * grad_blocks) + jnp.sum(grad_v * grad_v))
    count = grad_blocks.shape[0] * size * size + vectors.shape[0] * width
    factor = jnp.minimum(1.0, 0.5 * math.sqrt(count) / clip_norm)
    slot_grad = jnp.zeros_like(master).at[owners].set(grad_blocks)
    clipped = factor * slot_grad
    turned = jnp.einsum('sji,sjk->sik', left_basis, clipped, precision=highest)
    rotated = jnp.einsum('sik,skl->sil', turned, right_basis, precision=highest)
    new_first = beta * first_moment + (1.0 - beta) * rotated
    new_second = beta * second_moment + (1.0 - beta) * rotated * rotated
    correction = 1.0 - beta ** STEP
    direction = new_first / correction / (jnp.sqrt(new_second / correction) + adam_eps)
    back_turn = jnp.einsum('sij,sjk->sik', left_basis, direction, precision=highest)
    update = jnp.einsum('sik,slk->sil', back_turn, right_basis, precision=highest)
    new_master = master - rate_matrix * (update + decay_weight * master)
    vector_clip = factor * grad_v
    new_vector_first = beta * vector_first + (1.0 - beta) * vector_clip
    new_vector_second = beta * vector_second + (1.0 - beta) * vector_clip * vector_clip
    vector_step = new_vector_first / correction / (jnp.sqrt(new_vector_second / correction) + adam_eps)
    new_vectors = vectors - rate_vector * vector_step
    return (outputs.reshape(DEVICES * ROWS_DEV, width), grad_in.reshape(DEVICES * ROWS_DEV, width), clip_norm, new_master, new_first, new_second, new_vectors, new_vector_first, new_vector_second)
```

```python
import functools
import math

import jax
import jax.numpy as jnp
from jax import lax
from jax.experimental import pallas as pl
from jax.experimental.pallas import tpu as pltpu
from jax.sharding import PartitionSpec as P

HEADS = 12
STEP = 2
AXES = ("dp", "fsdp")

norm_eps = 1e-06
adam_eps = 1e-08
beta = 0.5
rate_matrix = 0.03
rate_vector = 0.05
decay_weight = 0.01
highest = lax.Precision.HIGHEST
far = 2.0**30
low = jnp.bfloat16
wide = jnp.float32

CHUNK = 512


def ring_order(dp, fsdp):
    if (dp, fsdp) != (8, 4):
        return None
    order = []
    for turn, (x, y) in enumerate(((0, 0), (1, 0), (1, 1), (0, 1))):
        places = range(4) if turn % 2 == 0 else range(3, -1, -1)
        for z in places:
            order += [(z * 2 + x) * 4 + y * 2 + core for core in (0, 1)]
    return order


def mm(a, b, ca, cb):
    return lax.dot_general(a, b, (((ca,), (cb,)), ((), ())), preferred_element_type=wide)


def normal_parts(values):
    center = values - jnp.mean(values, axis=-1, keepdims=True)
    factor = lax.rsqrt(jnp.mean(center * center, axis=-1, keepdims=True) + norm_eps)
    return center * factor, factor


def norm_back(grad, normal, factor, gain):
    inner = grad * gain
    return factor * (
        inner
        - jnp.mean(inner, axis=-1, keepdims=True)
        - normal * jnp.mean(inner * normal, axis=-1, keepdims=True)
    )


def start_blocks(place, whole, target, sem, first, across, row0, col0, height, breadth):
    def one(index, carry):
        r = index // breadth
        c = index % breadth
        slot = place[first + (row0 + r) * across + col0 + c]
        pltpu.make_async_copy(
            whole.at[slot],
            target.at[pl.ds(pl.multiple_of(r * 128, 128), 128), pl.ds(pl.multiple_of(c * 128, 128), 128)],
            sem,
        ).start()
        return carry

    lax.fori_loop(0, height * breadth, one, 0)


def store_blocks(place, source, buffer, sem, first, across, row0, col0, height, breadth):
    def one(index, carry):
        r = index // breadth
        c = index % breadth
        slot = place[first + (row0 + r) * across + col0 + c]
        pltpu.make_async_copy(
            source.at[pl.ds(pl.multiple_of(r * 128, 128), 128), pl.ds(pl.multiple_of(c * 128, 128), 128)],
            buffer.at[slot],
            sem,
        ).start()
        return carry

    lax.fori_loop(0, height * breadth, one, 0)


def await_bytes(ref, sem):
    pltpu.make_async_copy(ref, ref, sem).wait()


TILE = 112


def tiles(rows):
    return rows // TILE


def rows_of(t):
    return pl.ds(pl.multiple_of(t * TILE, 16), TILE)


def qkv_kernel(place, whole, patches, vectors, project, weight, normed, sems):
    rows, width = patches.shape
    side = width // 128
    for part in range(3):
        start_blocks(
            place, whole, weight.at[part], sems.at[part], 0, 3 * side, 0, part * side, side, side
        )

    def norm(t, carry):
        at = rows_of(t)
        normal, _ = normal_parts(patches[at, :].astype(wide))
        normed[at, :] = (normal * vectors[0:1, :] + vectors[1:2, :]).astype(low)
        return carry

    lax.fori_loop(0, tiles(rows), norm, 0)
    for part in range(3):
        await_bytes(weight.at[part], sems.at[part])
        out = mm(normed[...], weight[part], 1, 0)
        if part == 0:
            out = out + vectors[2:3, :]
        if part == 2:
            out = out + vectors[3:4, :]
        project[:, part * width : (part + 1) * width] = out.astype(low)


def attend_kernel(query, keys, values, image_query, image_keys, mixed, probs, scores):
    rows = query.shape[0]
    lane = lax.broadcasted_iota(jnp.int32, (rows, 128), 1)
    wide_keys = jnp.concatenate([keys[...], image_keys[...]], axis=1)
    scaled = query[...] * jnp.asarray(0.125, low)
    outs = []
    for h in range(2):
        part = jnp.where(lane // 64 == h, scaled, jnp.zeros_like(scaled))
        scores[h] = mm(jnp.concatenate([part, image_query[...]], axis=1), wide_keys, 1, 1)
    for h in range(2):
        for t in range(tiles(rows)):
            at = slice(t * TILE, (t + 1) * TILE)
            s = scores[h, at, :]
            e = jnp.exp(s - jnp.max(s, axis=-1, keepdims=True))
            total = jnp.sum(e, axis=-1, keepdims=True)
            probs[h, at, :] = (e * (1.0 / total)).astype(low)
        outs.append(mm(probs[h], values[...], 1, 0))
    mixed[...] = jnp.where(lane < 64, outs[0], outs[1]).astype(low)


def feed_kernel(
    place,
    whole,
    patches,
    cotangent,
    mixed,
    inside,
    vectors,
    bias_up,
    result,
    grad_middle,
    grad_mixed,
    sums,
    sums_up,
    buffer,
    w_out,
    w_up,
    w_down,
    middle,
    normal,
    factor,
    second,
    second_t,
    grad_two,
    out_sum,
    back_sum,
    stage_up,
    stage_down,
    stage_out,
    active,
    grad_pre,
    sems,
    out_sems,
):
    step = pl.program_id(0)
    steps = pl.num_programs(0)
    rows, width = patches.shape
    side = width // 128
    hidden = 4 * width
    high = hidden // 128
    per = CHUNK // 128
    first_out = 3 * side * side
    first_up = 4 * side * side
    first_down = first_up + side * high

    def fetch(index, slot):
        start_blocks(
            place, whole, w_up.at[slot], sems.at[slot], first_up, high, 0, index * per, side, per
        )
        start_blocks(
            place, whole, w_down.at[slot], sems.at[2 + slot], first_down, side, index * per, 0, per, side
        )

    @pl.when(step == 0)
    def _():
        start_blocks(place, whole, w_out, sems.at[4], first_out, side, 0, 0, side, side)
        fetch(0, 0)
        fetch(1, 1)
        await_bytes(w_out, sems.at[4])
        out_sum[...] = mm(mixed[...], w_out[...], 1, 0)

        def norm(t, total):
            at = rows_of(t)
            keep = inside[at, :]
            mid = patches[at, :].astype(wide) + keep * (out_sum[at, :] + vectors[4:5, :])
            middle[at, :] = mid
            scaled, q = normal_parts(mid)
            normal[at, :] = scaled
            factor[at, :] = q
            second[at, :] = (scaled * vectors[5:6, :] + vectors[6:7, :]).astype(low)
            two = (keep * cotangent[at, :].astype(wide)).astype(low)
            grad_two[at, :] = two
            return total + jnp.sum(two.astype(wide), axis=0, keepdims=True)

        sums[3:4, :] = lax.fori_loop(0, tiles(rows), norm, jnp.zeros((1, width), wide))
        second_t[...] = second[...].T

    slot = lax.rem(step, 2)
    await_bytes(w_up.at[slot], sems.at[slot])
    await_bytes(w_down.at[slot], sems.at[2 + slot])
    up = w_up[slot]
    down = w_down[slot]
    pre = mm(second[...], up, 1, 0) + bias_up[0]
    grad_active = mm(grad_two[...], down, 1, 1)
    half = 0.5 * (1.0 + lax.erf(pre * math.sqrt(0.5)))
    active[...] = (pre * half).astype(low)
    slope = half + pre * (jnp.exp(-0.5 * pre * pre) * (1.0 / math.sqrt(2.0 * math.pi)))
    back = (grad_active * slope).astype(low)
    grad_pre[...] = back
    sums_up[0] = jnp.sum(back.astype(wide), axis=0, keepdims=True)
    gone = mm(active[...], down, 1, 0)
    came = mm(grad_pre[...], up, 1, 1)

    @pl.when(step == 0)
    def _():
        out_sum[...] = gone
        back_sum[...] = came

    @pl.when(step > 0)
    def _():
        out_sum[...] += gone
        back_sum[...] += came

    @pl.when(step >= 2)
    def _():
        await_bytes(stage_up.at[slot], out_sems.at[slot])
        await_bytes(stage_down.at[slot], out_sems.at[2 + slot])

    stage_up[slot] = mm(second_t[...], grad_pre[...], 1, 0).astype(low)
    stage_down[slot] = mm(active[...], grad_two[...], 0, 0).astype(low)
    store_blocks(
        place, stage_up.at[slot], buffer, out_sems.at[slot], first_up, high, 0, step * per, side, per
    )
    store_blocks(
        place, stage_down.at[slot], buffer, out_sems.at[2 + slot], first_down, side, step * per, 0, per, side
    )

    @pl.when(step + 2 < steps)
    def _():
        fetch(step + 2, slot)

    @pl.when(step == steps - 1)
    def _():
        def finish(t, total):
            at = rows_of(t)
            keep = inside[at, :]
            result[at, :] = (middle[at, :] + keep * (out_sum[at, :] + vectors[11:12, :])).astype(low)
            grad = back_sum[at, :]
            scaled = normal[at, :]
            mid = cotangent[at, :].astype(wide) + norm_back(
                grad, scaled, factor[at, :], vectors[5:6, :]
            )
            grad_middle[at, :] = mid
            one = (keep * mid).astype(low)
            second[at, :] = one
            gain, shift, bias = total
            return (
                gain + jnp.sum(grad * scaled, axis=0, keepdims=True),
                shift + jnp.sum(grad, axis=0, keepdims=True),
                bias + jnp.sum(one.astype(wide), axis=0, keepdims=True),
            )

        empty = jnp.zeros((1, width), wide)
        gain, shift, bias = lax.fori_loop(0, tiles(rows), finish, (empty, empty, empty))
        sums[0:1, :] = bias
        sums[1:2, :] = gain
        sums[2:3, :] = shift
        sums[4:8, :] = jnp.zeros((4, width), wide)
        stage_out[...] = mm(mixed[...], second[...], 0, 0).astype(low)
        store_blocks(place, stage_out, buffer, out_sems.at[4], first_out, side, 0, 0, side, side)
        grad_mixed[...] = mm(second[...], w_out[...], 1, 1).astype(low)
        for other in range(2):
            await_bytes(stage_up.at[other], out_sems.at[other])
            await_bytes(stage_down.at[other], out_sems.at[2 + other])
        await_bytes(stage_out, out_sems.at[4])


def back_kernel(
    place,
    whole,
    held,
    query,
    keys,
    values,
    probs,
    grad_mixed,
    mixed,
    patches,
    grad_middle,
    vectors,
    grad_input,
    sums,
    buffer,
    weight,
    grad_project,
    grad_low,
    normed,
    grad_sum,
    stage,
    sems,
    out_sems,
):
    del held
    step = pl.program_id(0)
    steps = pl.num_programs(0)
    rows, width = patches.shape
    side = width // 128
    scale = 0.125

    @pl.when(step == 0)
    def _():
        for part in range(3):
            start_blocks(
                place, whole, weight.at[part], sems.at[part], 0, 3 * side, 0, part * side, side, side
            )

        def norm(t, carry):
            at = rows_of(t)
            normal, _ = normal_parts(patches[at, :].astype(wide))
            normed[at, :] = (normal * vectors[0:1, :] + vectors[1:2, :]).astype(low)
            return carry

        lax.fori_loop(0, tiles(rows), norm, 0)

    lane = lax.broadcasted_iota(jnp.int32, (rows, 128), 1)
    grad = grad_mixed[...]
    grad_t = grad.T
    query_t = query[...].T
    outer = grad.astype(wide) * mixed[...].astype(wide)
    turned_query = []
    turned_keys = []
    turned_values = []
    for h in range(2):
        mine = lane // 64 == h
        delta = jnp.sum(jnp.where(mine, outer, 0.0), axis=-1, keepdims=True)
        part = jnp.where(mine, grad, jnp.zeros_like(grad))
        grad_probs = mm(part, values[...], 1, 1)
        grad_low[h] = (probs[h].astype(wide) * (grad_probs - delta)).astype(low)
        turned_query.append(mm(grad_low[h], keys[...], 1, 0))
        turned_keys.append(mm(query_t[h * 64 : (h + 1) * 64, :], grad_low[h], 1, 0))
        turned_values.append(mm(grad_t[h * 64 : (h + 1) * 64, :], probs[h], 1, 0))
    grad_query = jnp.where(lane < 64, turned_query[0], turned_query[1]) * scale
    grad_keys = (jnp.concatenate(turned_keys, axis=0) * scale).T
    grad_values = jnp.concatenate(turned_values, axis=0).T
    at = pl.multiple_of(step * 128, 128)
    for part, value in enumerate((grad_query, grad_keys, grad_values)):
        grad_project[part, :, pl.ds(at, 128)] = value.astype(low)

    @pl.when(step == steps - 1)
    def _():
        for part in range(3):
            if part == 2:
                await_bytes(stage.at[0], out_sems.at[0])
            stage[part % 2] = mm(normed[...], grad_project[part], 0, 0).astype(low)
            store_blocks(
                place, stage.at[part % 2], buffer, out_sems.at[part % 2], 0, 3 * side, 0, part * side, side, side
            )
        for part in range(3):
            await_bytes(weight.at[part], sems.at[part])
        total = mm(grad_project[0], weight[0], 1, 1)
        total = total + mm(grad_project[1], weight[1], 1, 1)
        grad_sum[...] = total + mm(grad_project[2], weight[2], 1, 1)

        def finish(t, carry):
            at = rows_of(t)
            grad = grad_sum[at, :]
            normal, factor = normal_parts(patches[at, :].astype(wide))
            back = norm_back(grad, normal, factor, vectors[0:1, :])
            grad_input[at, :] = (grad_middle[at, :] + back).astype(low)
            gain, shift, bias_query, bias_value = carry
            return (
                gain + jnp.sum(grad * normal, axis=0, keepdims=True),
                shift + jnp.sum(grad, axis=0, keepdims=True),
                bias_query + jnp.sum(grad_project[0, at, :].astype(wide), axis=0, keepdims=True),
                bias_value + jnp.sum(grad_project[2, at, :].astype(wide), axis=0, keepdims=True),
            )

        empty = jnp.zeros((1, width), wide)
        found = lax.fori_loop(0, tiles(rows), finish, (empty, empty, empty, empty))
        for row in range(4):
            sums[row : row + 1, :] = found[row]
        sums[4:8, :] = jnp.zeros((4, width), wide)
        await_bytes(stage.at[1], out_sems.at[1])
        await_bytes(stage.at[0], out_sems.at[0])


VMEM_LIMIT = 60 * 1024 * 1024


def params(count=1):
    return pltpu.CompilerParams(
        dimension_semantics=("arbitrary",) * count, vmem_limit_bytes=VMEM_LIMIT
    )


def whole_spec():
    return pl.BlockSpec(memory_space=pl.ANY)


def full(shape):
    return pl.BlockSpec(shape, lambda *_: (0,) * len(shape))


def layer(whole, place, patches, cotangent, counts, vectors, slots):
    rows, width = patches.shape
    hidden = 4 * width
    side = width // 128
    pairs = width // 128
    shape = jax.ShapeDtypeStruct
    ends = jnp.cumsum(counts)
    places = jnp.arange(rows, dtype=jnp.int32)[:, None]
    image = jnp.sum((places >= ends[None, :]).astype(jnp.int32), axis=1, keepdims=True)
    within = places < ends[-1]
    image = jnp.where(within, image, 4)
    inside = within.astype(wide)
    lanes = jnp.arange(128, dtype=jnp.int32)[None, :]
    image_keys = (lanes == image).astype(low)
    image_query = jnp.where((lanes != image) & (lanes < 5), -far, 0.0).astype(low)

    project = pl.pallas_call(
        qkv_kernel,
        grid_spec=pltpu.PrefetchScalarGridSpec(
            num_scalar_prefetch=1,
            grid=(1,),
            in_specs=[whole_spec(), full((rows, width)), full((12, width))],
            out_specs=full((rows, 3 * width)),
            scratch_shapes=[
                pltpu.VMEM((3, width, width), low),
                pltpu.VMEM((rows, width), low),
                pltpu.SemaphoreType.DMA((3,)),
            ],
        ),
        out_shape=shape((rows, 3 * width), low),
        compiler_params=params(),
        name="qkv",
    )(place, whole, patches, vectors)

    def column(offset):
        return pl.BlockSpec((rows, 128), lambda j, *_: (0, j + offset))

    mixed, probs = pl.pallas_call(
        attend_kernel,
        grid=(pairs,),
        in_specs=[
            column(0),
            column(pairs),
            column(2 * pairs),
            full((rows, 128)),
            full((rows, 128)),
        ],
        out_specs=[column(0), pl.BlockSpec((2, rows, rows), lambda j: (j, 0, 0))],
        out_shape=[shape((rows, width), low), shape((HEADS, rows, rows), low)],
        scratch_shapes=[pltpu.VMEM((2, rows, rows), wide)],
        compiler_params=params(),
        name="attend",
    )(project, project, project, image_query, image_keys)

    steps = hidden // CHUNK
    result, grad_middle, grad_mixed, sums_two, sums_up, buffer = pl.pallas_call(
        feed_kernel,
        grid_spec=pltpu.PrefetchScalarGridSpec(
            num_scalar_prefetch=1,
            grid=(steps,),
            in_specs=[
                whole_spec(),
                full((rows, width)),
                full((rows, width)),
                full((rows, width)),
                full((rows, 1)),
                full((12, width)),
                pl.BlockSpec((1, 1, CHUNK), lambda c, *_: (c, 0, 0)),
            ],
            out_specs=[
                full((rows, width)),
                full((rows, width)),
                full((rows, width)),
                full((8, width)),
                pl.BlockSpec((1, 1, CHUNK), lambda c, *_: (c, 0, 0)),
                whole_spec(),
            ],
            scratch_shapes=[
                pltpu.VMEM((width, width), low),
                pltpu.VMEM((2, width, CHUNK), low),
                pltpu.VMEM((2, CHUNK, width), low),
                pltpu.VMEM((rows, width), wide),
                pltpu.VMEM((rows, width), wide),
                pltpu.VMEM((rows, 1), wide),
                pltpu.VMEM((rows, width), low),
                pltpu.VMEM((width, rows), low),
                pltpu.VMEM((rows, width), low),
                pltpu.VMEM((rows, width), wide),
                pltpu.VMEM((rows, width), wide),
                pltpu.VMEM((2, width, CHUNK), low),
                pltpu.VMEM((2, CHUNK, width), low),
                pltpu.VMEM((width, width), low),
                pltpu.VMEM((rows, CHUNK), low),
                pltpu.VMEM((rows, CHUNK), low),
                pltpu.SemaphoreType.DMA((5,)),
                pltpu.SemaphoreType.DMA((5,)),
            ],
        ),
        out_shape=[
            shape((rows, width), low),
            shape((rows, width), wide),
            shape((rows, width), low),
            shape((8, width), wide),
            shape((steps, 1, CHUNK), wide),
            shape((slots, 128, 128), low),
        ],
        compiler_params=params(),
        name="feed",
    )(
        place,
        whole,
        patches,
        cotangent,
        mixed,
        inside,
        vectors,
        vectors[7:11].reshape(steps, 1, CHUNK),
    )

    grad_input, sums_one, buffer = pl.pallas_call(
        back_kernel,
        grid_spec=pltpu.PrefetchScalarGridSpec(
            num_scalar_prefetch=1,
            grid=(pairs,),
            in_specs=[
                whole_spec(),
                whole_spec(),
                column(0),
                column(pairs),
                column(2 * pairs),
                pl.BlockSpec((2, rows, rows), lambda j, *_: (j, 0, 0)),
                column(0),
                column(0),
                full((rows, width)),
                full((rows, width)),
                full((12, width)),
            ],
            out_specs=[full((rows, width)), full((8, width)), whole_spec()],
            scratch_shapes=[
                pltpu.VMEM((3, width, width), low),
                pltpu.VMEM((3, rows, width), low),
                pltpu.VMEM((2, rows, rows), low),
                pltpu.VMEM((rows, width), low),
                pltpu.VMEM((rows, width), wide),
                pltpu.VMEM((2, width, width), low),
                pltpu.SemaphoreType.DMA((3,)),
                pltpu.SemaphoreType.DMA((2,)),
            ],
        ),
        out_shape=[
            shape((rows, width), low),
            shape((8, width), wide),
            shape((slots, 128, 128), low),
        ],
        input_output_aliases={2: 2},
        compiler_params=params(),
        name="back",
    )(
        place,
        whole,
        buffer,
        project,
        project,
        project,
        probs,
        grad_mixed,
        mixed,
        patches,
        grad_middle,
        vectors,
    )
    del side
    vector_grad = jnp.concatenate(
        [sums_one[0:4], sums_two[0:3], sums_up.reshape(4, width), sums_two[3:4]], axis=0
    )
    return result, grad_input, vector_grad, buffer


def shards(
    sizes,
    patches,
    lengths,
    cotangent,
    owners,
    master,
    first_moment,
    second_moment,
    left_basis,
    right_basis,
    vectors,
    vector_first,
    vector_second,
):
    dp, fsdp = sizes
    devices = dp * fsdp
    width = patches.shape[1]
    held, size = master.shape[0], master.shape[1]
    slots = held * devices
    order = ring_order(dp, fsdp)
    me = lax.axis_index(AXES)
    if order is None:
        groups = None
        place = owners
    else:
        groups = [order]
        rank = [0] * devices
        for spot, device in enumerate(order):
            rank[device] = spot
        device = owners // held
        spot = jnp.sum(
            jnp.where(
                device[:, None] == jnp.arange(devices, dtype=jnp.int32)[None, :],
                jnp.array(rank, jnp.int32)[None, :],
                0,
            ),
            axis=1,
        )
        place = spot * held + owners % held
    mine = me * held + jnp.arange(held, dtype=jnp.int32)
    named = jnp.any(mine[:, None] == owners[None, :], axis=1)

    whole = lax.all_gather(
        master.astype(low), AXES, axis=0, tiled=True, axis_index_groups=groups
    )
    result, grad_input, vector_grad, buffer = layer(
        whole, place, patches, cotangent, lengths[0], vectors, slots
    )

    def everywhere(value):
        step = 1
        while step < devices:
            value = value + lax.ppermute(value, AXES, [(d, d ^ step) for d in range(devices)])
            step *= 2
        return value

    vector_sum = everywhere(vector_grad)
    owned = lax.psum_scatter(
        buffer, AXES, scatter_dimension=0, tiled=True, axis_index_groups=groups
    )
    owned = jnp.where(named[:, None, None], owned.astype(wide), 0.0)
    total_blocks = everywhere(jnp.broadcast_to(jnp.sum(owned * owned), (8, 128)))[0, 0]
    clip_norm = jnp.sqrt(total_blocks + jnp.sum(vector_sum * vector_sum))
    count = owners.shape[0] * size * size + vectors.shape[0] * width
    factor = jnp.minimum(1.0, 0.5 * math.sqrt(count) / clip_norm)
    turned = jnp.einsum("sji,sjk->sik", left_basis, owned, precision=highest)
    rotated = factor * jnp.einsum("sik,skl->sil", turned, right_basis, precision=highest)
    new_first = beta * first_moment + (1.0 - beta) * rotated
    new_second = beta * second_moment + (1.0 - beta) * rotated * rotated
    correction = 1.0 - beta**STEP
    direction = new_first / correction / (jnp.sqrt(new_second / correction) + adam_eps)
    back_turn = jnp.einsum("sij,sjk->sik", left_basis, direction, precision=highest)
    update = jnp.einsum("sik,slk->sil", back_turn, right_basis, precision=highest)
    new_master = master - rate_matrix * (update + decay_weight * master)
    vector_clip = factor * vector_sum
    new_vector_first = beta * vector_first + (1.0 - beta) * vector_clip
    new_vector_second = beta * vector_second + (1.0 - beta) * vector_clip * vector_clip
    vector_step = (
        new_vector_first / correction / (jnp.sqrt(new_vector_second / correction) + adam_eps)
    )
    new_vectors = vectors - rate_vector * vector_step
    return (
        result,
        grad_input,
        clip_norm,
        new_master,
        new_first,
        new_second,
        new_vectors,
        new_vector_first,
        new_vector_second,
    )


def solution(mesh):
    sizes = (mesh.shape["dp"], mesh.shape["fsdp"])
    rows = P(AXES, None)
    blocks = P(AXES, None, None)
    return jax.shard_map(
        functools.partial(shards, sizes),
        mesh=mesh,
        in_specs=(rows, rows, rows, P(), blocks, blocks, blocks, blocks, blocks, P(), P(), P()),
        out_specs=(rows, rows, P(), blocks, blocks, blocks, P(), P(), P()),
        check_vma=False,
    )
```

```python
import functools
import math

import jax
import jax.numpy as jnp
from jax import lax
from jax.experimental import pallas as pl
from jax.experimental.pallas import tpu as pltpu
from jax.sharding import PartitionSpec as P

HEADS = 12
STEP = 2
AXES = ("dp", "fsdp")

norm_eps = 1e-06
adam_eps = 1e-08
beta = 0.5
rate_matrix = 0.03
rate_vector = 0.05
decay_weight = 0.01
highest = lax.Precision.HIGHEST
far = 2.0**30
low = jnp.bfloat16
wide = jnp.float32

CHUNK = 512


def ring_order(dp, fsdp):
    if (dp, fsdp) != (8, 4):
        return None
    order = []
    for turn, (x, y) in enumerate(((0, 0), (1, 0), (1, 1), (0, 1))):
        places = range(4) if turn % 2 == 0 else range(3, -1, -1)
        for z in places:
            order += [(z * 2 + x) * 4 + y * 2 + core for core in (0, 1)]
    return order


def mm(a, b, ca, cb):
    return lax.dot_general(a, b, (((ca,), (cb,)), ((), ())), preferred_element_type=wide)


def normal_parts(values):
    center = values - jnp.mean(values, axis=-1, keepdims=True)
    factor = lax.rsqrt(jnp.mean(center * center, axis=-1, keepdims=True) + norm_eps)
    return center * factor, factor


def norm_back(grad, normal, factor, gain):
    inner = grad * gain
    return factor * (
        inner
        - jnp.mean(inner, axis=-1, keepdims=True)
        - normal * jnp.mean(inner * normal, axis=-1, keepdims=True)
    )


def start_blocks(place, whole, target, sem, first, across, row0, col0, height, breadth):
    def one(index, carry):
        r = index // breadth
        c = index % breadth
        slot = place[first + (row0 + r) * across + col0 + c]
        pltpu.make_async_copy(
            whole.at[slot],
            target.at[pl.ds(pl.multiple_of(r * 128, 128), 128), pl.ds(pl.multiple_of(c * 128, 128), 128)],
            sem,
        ).start()
        return carry

    lax.fori_loop(0, height * breadth, one, 0)


def store_blocks(place, source, buffer, sem, first, across, row0, col0, height, breadth):
    def one(index, carry):
        r = index // breadth
        c = index % breadth
        slot = place[first + (row0 + r) * across + col0 + c]
        pltpu.make_async_copy(
            source.at[pl.ds(pl.multiple_of(r * 128, 128), 128), pl.ds(pl.multiple_of(c * 128, 128), 128)],
            buffer.at[slot],
            sem,
        ).start()
        return carry

    lax.fori_loop(0, height * breadth, one, 0)


def await_bytes(ref, sem):
    pltpu.make_async_copy(ref, ref, sem).wait()


TILE = 112


def tiles(rows):
    return rows // TILE


def rows_of(t):
    return pl.ds(pl.multiple_of(t * TILE, 16), TILE)


def qkv_kernel(place, whole, patches, vectors, project, weight, normed, sems):
    rows, width = patches.shape
    side = width // 128
    for part in range(3):
        start_blocks(
            place, whole, weight.at[part], sems.at[part], 0, 3 * side, 0, part * side, side, side
        )

    def norm(t, carry):
        at = rows_of(t)
        normal, _ = normal_parts(patches[at, :].astype(wide))
        normed[at, :] = (normal * vectors[0:1, :] + vectors[1:2, :]).astype(low)
        return carry

    lax.fori_loop(0, tiles(rows), norm, 0)
    for part in range(3):
        await_bytes(weight.at[part], sems.at[part])
        out = mm(normed[...], weight[part], 1, 0)
        if part == 0:
            out = out + vectors[2:3, :]
        if part == 2:
            out = out + vectors[3:4, :]
        project[:, part * width : (part + 1) * width] = out.astype(low)


def attend_kernel(query, keys, values, image_query, image_keys, mixed, probs, scores):
    rows = query.shape[0]
    lane = lax.broadcasted_iota(jnp.int32, (rows, 128), 1)
    wide_keys = jnp.concatenate([keys[...], image_keys[...]], axis=1)
    scaled = query[...] * jnp.asarray(0.125, low)
    outs = []
    for h in range(2):
        part = jnp.where(lane // 64 == h, scaled, jnp.zeros_like(scaled))
        scores[h] = mm(jnp.concatenate([part, image_query[...]], axis=1), wide_keys, 1, 1)
    for h in range(2):
        for t in range(tiles(rows)):
            at = slice(t * TILE, (t + 1) * TILE)
            s = scores[h, at, :]
            e = jnp.exp(s - jnp.max(s, axis=-1, keepdims=True))
            total = jnp.sum(e, axis=-1, keepdims=True)
            probs[h, at, :] = (e * (1.0 / total)).astype(low)
        outs.append(mm(probs[h], values[...], 1, 0))
    mixed[...] = jnp.where(lane < 64, outs[0], outs[1]).astype(low)


def feed_kernel(
    place,
    whole,
    patches,
    cotangent,
    mixed,
    inside,
    vectors,
    bias_up,
    result,
    grad_middle,
    grad_mixed,
    sums,
    sums_up,
    buffer,
    w_out,
    w_up,
    w_down,
    middle,
    normal,
    factor,
    second,
    second_t,
    grad_two,
    out_sum,
    back_sum,
    stage_up,
    stage_down,
    stage_out,
    active,
    grad_pre,
    sems,
    out_sems,
):
    step = pl.program_id(0)
    steps = pl.num_programs(0)
    rows, width = patches.shape
    side = width // 128
    hidden = 4 * width
    high = hidden // 128
    per = CHUNK // 128
    first_out = 3 * side * side
    first_up = 4 * side * side
    first_down = first_up + side * high

    def fetch(index, slot):
        start_blocks(
            place, whole, w_up.at[slot], sems.at[slot], first_up, high, 0, index * per, side, per
        )
        start_blocks(
            place, whole, w_down.at[slot], sems.at[2 + slot], first_down, side, index * per, 0, per, side
        )

    @pl.when(step == 0)
    def _():
        start_blocks(place, whole, w_out, sems.at[4], first_out, side, 0, 0, side, side)
        fetch(0, 0)
        fetch(1, 1)
        await_bytes(w_out, sems.at[4])
        out_sum[...] = mm(mixed[...], w_out[...], 1, 0)

        def norm(t, total):
            at = rows_of(t)
            keep = inside[at, :]
            mid = patches[at, :].astype(wide) + keep * (out_sum[at, :] + vectors[4:5, :])
            middle[at, :] = mid
            scaled, q = normal_parts(mid)
            normal[at, :] = scaled
            factor[at, :] = q
            second[at, :] = (scaled * vectors[5:6, :] + vectors[6:7, :]).astype(low)
            two = (keep * cotangent[at, :].astype(wide)).astype(low)
            grad_two[at, :] = two
            return total + jnp.sum(two.astype(wide), axis=0, keepdims=True)

        sums[3:4, :] = lax.fori_loop(0, tiles(rows), norm, jnp.zeros((1, width), wide))
        second_t[...] = second[...].T

    slot = lax.rem(step, 2)
    await_bytes(w_up.at[slot], sems.at[slot])
    await_bytes(w_down.at[slot], sems.at[2 + slot])
    up = w_up[slot]
    down = w_down[slot]
    pre = mm(second[...], up, 1, 0) + bias_up[0]
    grad_active = mm(grad_two[...], down, 1, 1)
    half = 0.5 * (1.0 + lax.erf(pre * math.sqrt(0.5)))
    active[...] = (pre * half).astype(low)
    slope = half + pre * (jnp.exp(-0.5 * pre * pre) * (1.0 / math.sqrt(2.0 * math.pi)))
    back = (grad_active * slope).astype(low)
    grad_pre[...] = back
    sums_up[0] = jnp.sum(back.astype(wide), axis=0, keepdims=True)
    gone = mm(active[...], down, 1, 0)
    came = mm(grad_pre[...], up, 1, 1)

    @pl.when(step == 0)
    def _():
        out_sum[...] = gone
        back_sum[...] = came

    @pl.when(step > 0)
    def _():
        out_sum[...] += gone
        back_sum[...] += came

    @pl.when(step >= 2)
    def _():
        await_bytes(stage_up.at[slot], out_sems.at[slot])
        await_bytes(stage_down.at[slot], out_sems.at[2 + slot])

    stage_up[slot] = mm(second_t[...], grad_pre[...], 1, 0).astype(low)
    stage_down[slot] = mm(active[...], grad_two[...], 0, 0).astype(low)
    store_blocks(
        place, stage_up.at[slot], buffer, out_sems.at[slot], first_up, high, 0, step * per, side, per
    )
    store_blocks(
        place, stage_down.at[slot], buffer, out_sems.at[2 + slot], first_down, side, step * per, 0, per, side
    )

    @pl.when(step + 2 < steps)
    def _():
        fetch(step + 2, slot)

    @pl.when(step == steps - 1)
    def _():
        def finish(t, total):
            at = rows_of(t)
            keep = inside[at, :]
            result[at, :] = (middle[at, :] + keep * (out_sum[at, :] + vectors[11:12, :])).astype(low)
            grad = back_sum[at, :]
            scaled = normal[at, :]
            mid = cotangent[at, :].astype(wide) + norm_back(
                grad, scaled, factor[at, :], vectors[5:6, :]
            )
            grad_middle[at, :] = mid
            one = (keep * mid).astype(low)
            second[at, :] = one
            gain, shift, bias = total
            return (
                gain + jnp.sum(grad * scaled, axis=0, keepdims=True),
                shift + jnp.sum(grad, axis=0, keepdims=True),
                bias + jnp.sum(one.astype(wide), axis=0, keepdims=True),
            )

        empty = jnp.zeros((1, width), wide)
        gain, shift, bias = lax.fori_loop(0, tiles(rows), finish, (empty, empty, empty))
        sums[0:1, :] = bias
        sums[1:2, :] = gain
        sums[2:3, :] = shift
        sums[4:8, :] = jnp.zeros((4, width), wide)
        stage_out[...] = mm(mixed[...], second[...], 0, 0).astype(low)
        store_blocks(place, stage_out, buffer, out_sems.at[4], first_out, side, 0, 0, side, side)
        grad_mixed[...] = mm(second[...], w_out[...], 1, 1).astype(low)
        for other in range(2):
            await_bytes(stage_up.at[other], out_sems.at[other])
            await_bytes(stage_down.at[other], out_sems.at[2 + other])
        await_bytes(stage_out, out_sems.at[4])


def back_kernel(
    place,
    held,
    query,
    keys,
    values,
    probs,
    grad_mixed,
    mixed,
    patches,
    vectors,
    grad_project,
    buffer,
    grad_low,
    normed,
    stage,
    out_sems,
):
    del held
    step = pl.program_id(0)
    steps = pl.num_programs(0)
    rows, width = patches.shape
    side = width // 128
    scale = 0.125

    @pl.when(step == 0)
    def _():
        def norm(t, carry):
            at = rows_of(t)
            normal, _ = normal_parts(patches[at, :].astype(wide))
            normed[at, :] = (normal * vectors[0:1, :] + vectors[1:2, :]).astype(low)
            return carry

        lax.fori_loop(0, tiles(rows), norm, 0)

    lane = lax.broadcasted_iota(jnp.int32, (rows, 128), 1)
    grad = grad_mixed[...]
    grad_t = grad.T
    query_t = query[...].T
    outer = grad.astype(wide) * mixed[...].astype(wide)
    turned_query = []
    turned_keys = []
    turned_values = []
    for h in range(2):
        mine = lane // 64 == h
        delta = jnp.sum(jnp.where(mine, outer, 0.0), axis=-1, keepdims=True)
        part = jnp.where(mine, grad, jnp.zeros_like(grad))
        grad_probs = mm(part, values[...], 1, 1)
        grad_low[h] = (probs[h].astype(wide) * (grad_probs - delta)).astype(low)
        turned_query.append(mm(grad_low[h], keys[...], 1, 0))
        turned_keys.append(mm(query_t[h * 64 : (h + 1) * 64, :], grad_low[h], 1, 0))
        turned_values.append(mm(grad_t[h * 64 : (h + 1) * 64, :], probs[h], 1, 0))
    grad_query = jnp.where(lane < 64, turned_query[0], turned_query[1]) * scale
    grad_keys = (jnp.concatenate(turned_keys, axis=0) * scale).T
    grad_values = jnp.concatenate(turned_values, axis=0).T
    at = pl.multiple_of(step * 128, 128)
    for part, value in enumerate((grad_query, grad_keys, grad_values)):
        grad_project[part, :, pl.ds(at, 128)] = value.astype(low)

    @pl.when(step == steps - 1)
    def _():
        for part in range(3):
            if part == 2:
                await_bytes(stage.at[0], out_sems.at[0])
            stage[part % 2] = mm(normed[...], grad_project[part], 0, 0).astype(low)
            store_blocks(
                place,
                stage.at[part % 2],
                buffer,
                out_sems.at[part % 2],
                0,
                3 * side,
                0,
                part * side,
                side,
                side,
            )
        await_bytes(stage.at[1], out_sems.at[1])
        await_bytes(stage.at[0], out_sems.at[0])


def input_kernel(
    place, whole, grad_project, patches, grad_middle, vectors, grad_input, sums, weight, grad_sum, sems
):
    rows, width = patches.shape
    side = width // 128
    for part in range(3):
        start_blocks(
            place, whole, weight.at[part], sems.at[part], 0, 3 * side, 0, part * side, side, side
        )
    for part in range(3):
        await_bytes(weight.at[part], sems.at[part])
    total = mm(grad_project[0], weight[0], 1, 1)
    total = total + mm(grad_project[1], weight[1], 1, 1)
    grad_sum[...] = total + mm(grad_project[2], weight[2], 1, 1)

    def finish(t, carry):
        at = rows_of(t)
        grad = grad_sum[at, :]
        normal, factor = normal_parts(patches[at, :].astype(wide))
        back = norm_back(grad, normal, factor, vectors[0:1, :])
        grad_input[at, :] = (grad_middle[at, :] + back).astype(low)
        gain, shift, bias_query, bias_value = carry
        return (
            gain + jnp.sum(grad * normal, axis=0, keepdims=True),
            shift + jnp.sum(grad, axis=0, keepdims=True),
            bias_query + jnp.sum(grad_project[0, at, :].astype(wide), axis=0, keepdims=True),
            bias_value + jnp.sum(grad_project[2, at, :].astype(wide), axis=0, keepdims=True),
        )

    empty = jnp.zeros((1, width), wide)
    found = lax.fori_loop(0, tiles(rows), finish, (empty, empty, empty, empty))
    for row in range(4):
        sums[row : row + 1, :] = found[row]
    sums[4:8, :] = jnp.zeros((4, width), wide)


def full_dot(a, b, ca, cb):
    return lax.dot_general(
        a, b, (((ca,), (cb,)), ((), ())), precision=highest, preferred_element_type=wide
    )


def turn_kernel(named, grads, left, right, rotated, total):
    s = pl.program_id(0)
    block = jnp.where(named[s] > 0, grads[0].astype(wide), 0.0)
    rotated[0] = full_dot(full_dot(left[0], block, 0, 0), right[0], 1, 0)

    @pl.when(s == 0)
    def _():
        total[...] = jnp.zeros_like(total)

    total[...] += jnp.sum(block * block)


def adam_parts(gradient, first, second):
    correction = 1.0 - beta**STEP
    new_first = beta * first + (1.0 - beta) * gradient
    new_second = beta * second + (1.0 - beta) * gradient * gradient
    direction = new_first / correction / (jnp.sqrt(new_second / correction) + adam_eps)
    return new_first, new_second, direction


def adam_kernel(
    count,
    total,
    rotated,
    master,
    first,
    second,
    left,
    right,
    vector_sum,
    vectors,
    vector_first,
    vector_second,
    new_master,
    new_first,
    new_second,
    clip,
    new_vectors,
    new_vector_first,
    new_vector_second,
    factor,
):
    @pl.when(pl.program_id(0) == 0)
    def _():
        grads = vector_sum[...]
        norm = jnp.sqrt(total[0:1, 0:1] + jnp.sum(grads * grads))
        clip[...] = norm
        factor[...] = jnp.minimum(1.0, 0.5 * math.sqrt(count) / norm)
        ahead, squares, way = adam_parts(
            factor[...] * grads, vector_first[...], vector_second[...]
        )
        new_vector_first[...] = ahead
        new_vector_second[...] = squares
        new_vectors[...] = vectors[...] - rate_vector * way

    ahead, squares, way = adam_parts(factor[...] * rotated[0], first[0], second[0])
    new_first[0] = ahead
    new_second[0] = squares
    update = full_dot(full_dot(left[0], way, 1, 0), right[0], 1, 1)
    new_master[0] = master[0] - rate_matrix * (update + decay_weight * master[0])


VMEM_LIMIT = 60 * 1024 * 1024


def params(count=1):
    return pltpu.CompilerParams(
        dimension_semantics=("arbitrary",) * count, vmem_limit_bytes=VMEM_LIMIT
    )


def whole_spec():
    return pl.BlockSpec(memory_space=pl.ANY)


def full(shape):
    return pl.BlockSpec(shape, lambda *_: (0,) * len(shape))


def shards(
    sizes,
    patches,
    lengths,
    cotangent,
    owners,
    master,
    first_moment,
    second_moment,
    left_basis,
    right_basis,
    vectors,
    vector_first,
    vector_second,
):
    dp, fsdp = sizes
    devices = dp * fsdp
    rows, width = patches.shape
    hidden = 4 * width
    side = width // 128
    pairs = width // 128
    held, size = master.shape[0], master.shape[1]
    slots = held * devices
    shape = jax.ShapeDtypeStruct
    me = lax.axis_index(AXES)
    order = ring_order(dp, fsdp)
    groups = None if order is None else [order]

    def gather(value):
        return lax.all_gather(value, AXES, axis=0, tiled=True, axis_index_groups=groups)

    def scatter(value):
        return lax.psum_scatter(
            value, AXES, scatter_dimension=0, tiled=True, axis_index_groups=groups
        )

    def everywhere(value):
        step = 1
        while step < devices:
            value = value + lax.ppermute(value, AXES, [(d, d ^ step) for d in range(devices)])
            step *= 2
        return value

    whole = gather(master.astype(low))
    if order is None:
        place = owners
    else:
        rank = [0] * devices
        for spot, device in enumerate(order):
            rank[device] = spot
        device = owners // held
        spot = jnp.sum(
            jnp.where(
                device[:, None] == jnp.arange(devices, dtype=jnp.int32)[None, :],
                jnp.array(rank, jnp.int32)[None, :],
                0,
            ),
            axis=1,
        )
        place = spot * held + owners % held
    mine = me * held + jnp.arange(held, dtype=jnp.int32)
    named = jnp.any(mine[:, None] == owners[None, :], axis=1).astype(jnp.int32)

    counts = lengths[0]
    ends = jnp.cumsum(counts)
    places = jnp.arange(rows, dtype=jnp.int32)[:, None]
    image = jnp.sum((places >= ends[None, :]).astype(jnp.int32), axis=1, keepdims=True)
    within = places < ends[-1]
    image = jnp.where(within, image, 4)
    inside = within.astype(wide)
    lanes = jnp.arange(128, dtype=jnp.int32)[None, :]
    image_keys = (lanes == image).astype(low)
    image_query = jnp.where((lanes != image) & (lanes < 5), -far, 0.0).astype(low)

    project = pl.pallas_call(
        qkv_kernel,
        grid_spec=pltpu.PrefetchScalarGridSpec(
            num_scalar_prefetch=1,
            grid=(1,),
            in_specs=[whole_spec(), full((rows, width)), full((12, width))],
            out_specs=full((rows, 3 * width)),
            scratch_shapes=[
                pltpu.VMEM((3, width, width), low),
                pltpu.VMEM((rows, width), low),
                pltpu.SemaphoreType.DMA((3,)),
            ],
        ),
        out_shape=shape((rows, 3 * width), low),
        compiler_params=params(),
        name="qkv",
    )(place, whole, patches, vectors)

    def column(offset):
        return pl.BlockSpec((rows, 128), lambda j, *_: (0, j + offset))

    mixed, probs = pl.pallas_call(
        attend_kernel,
        grid=(pairs,),
        in_specs=[
            column(0),
            column(pairs),
            column(2 * pairs),
            full((rows, 128)),
            full((rows, 128)),
        ],
        out_specs=[column(0), pl.BlockSpec((2, rows, rows), lambda j: (j, 0, 0))],
        out_shape=[shape((rows, width), low), shape((HEADS, rows, rows), low)],
        scratch_shapes=[pltpu.VMEM((2, rows, rows), wide)],
        compiler_params=params(),
        name="attend",
    )(project, project, project, image_query, image_keys)

    steps = hidden // CHUNK
    result, grad_middle, grad_mixed, sums_two, sums_up, buffer = pl.pallas_call(
        feed_kernel,
        grid_spec=pltpu.PrefetchScalarGridSpec(
            num_scalar_prefetch=1,
            grid=(steps,),
            in_specs=[
                whole_spec(),
                full((rows, width)),
                full((rows, width)),
                full((rows, width)),
                full((rows, 1)),
                full((12, width)),
                pl.BlockSpec((1, 1, CHUNK), lambda c, *_: (c, 0, 0)),
            ],
            out_specs=[
                full((rows, width)),
                full((rows, width)),
                full((rows, width)),
                full((8, width)),
                pl.BlockSpec((1, 1, CHUNK), lambda c, *_: (c, 0, 0)),
                whole_spec(),
            ],
            scratch_shapes=[
                pltpu.VMEM((width, width), low),
                pltpu.VMEM((2, width, CHUNK), low),
                pltpu.VMEM((2, CHUNK, width), low),
                pltpu.VMEM((rows, width), wide),
                pltpu.VMEM((rows, width), wide),
                pltpu.VMEM((rows, 1), wide),
                pltpu.VMEM((rows, width), low),
                pltpu.VMEM((width, rows), low),
                pltpu.VMEM((rows, width), low),
                pltpu.VMEM((rows, width), wide),
                pltpu.VMEM((rows, width), wide),
                pltpu.VMEM((2, width, CHUNK), low),
                pltpu.VMEM((2, CHUNK, width), low),
                pltpu.VMEM((width, width), low),
                pltpu.VMEM((rows, CHUNK), low),
                pltpu.VMEM((rows, CHUNK), low),
                pltpu.SemaphoreType.DMA((5,)),
                pltpu.SemaphoreType.DMA((5,)),
            ],
        ),
        out_shape=[
            shape((rows, width), low),
            shape((rows, width), wide),
            shape((rows, width), low),
            shape((8, width), wide),
            shape((steps, 1, CHUNK), wide),
            shape((slots, size, size), low),
        ],
        compiler_params=params(),
        name="feed",
    )(
        place,
        whole,
        patches,
        cotangent,
        mixed,
        inside,
        vectors,
        vectors[7:11].reshape(steps, 1, CHUNK),
    )

    grad_project, buffer = pl.pallas_call(
        back_kernel,
        grid_spec=pltpu.PrefetchScalarGridSpec(
            num_scalar_prefetch=1,
            grid=(pairs,),
            in_specs=[
                whole_spec(),
                column(0),
                column(pairs),
                column(2 * pairs),
                pl.BlockSpec((2, rows, rows), lambda j, *_: (j, 0, 0)),
                column(0),
                column(0),
                full((rows, width)),
                full((12, width)),
            ],
            out_specs=[full((3, rows, width)), whole_spec()],
            scratch_shapes=[
                pltpu.VMEM((2, rows, rows), low),
                pltpu.VMEM((rows, width), low),
                pltpu.VMEM((2, width, width), low),
                pltpu.SemaphoreType.DMA((2,)),
            ],
        ),
        out_shape=[
            shape((3, rows, width), low),
            shape((slots, size, size), low),
        ],
        input_output_aliases={1: 1},
        compiler_params=params(),
        name="back",
    )(
        place,
        buffer,
        project,
        project,
        project,
        probs,
        grad_mixed,
        mixed,
        patches,
        vectors,
    )
    owned = scatter(buffer)

    grad_input, sums_one = pl.pallas_call(
        input_kernel,
        grid_spec=pltpu.PrefetchScalarGridSpec(
            num_scalar_prefetch=1,
            grid=(1,),
            in_specs=[
                whole_spec(),
                full((3, rows, width)),
                full((rows, width)),
                full((rows, width)),
                full((12, width)),
            ],
            out_specs=[full((rows, width)), full((8, width))],
            scratch_shapes=[
                pltpu.VMEM((3, width, width), low),
                pltpu.VMEM((rows, width), wide),
                pltpu.SemaphoreType.DMA((3,)),
            ],
        ),
        out_shape=[shape((rows, width), low), shape((8, width), wide)],
        compiler_params=params(),
        name="input",
    )(place, whole, grad_project, patches, grad_middle, vectors)
    vector_grad = jnp.concatenate(
        [sums_one[0:4], sums_two[0:3], sums_up.reshape(4, width), sums_two[3:4]], axis=0
    )
    vector_sum = everywhere(vector_grad)

    owned, vector_sum = lax.optimization_barrier((owned, vector_sum))

    def block():
        return pl.BlockSpec((1, size, size), lambda s, *_: (s, 0, 0))

    rotated, total = pl.pallas_call(
        turn_kernel,
        grid_spec=pltpu.PrefetchScalarGridSpec(
            num_scalar_prefetch=1,
            grid=(held,),
            in_specs=[block(), block(), block()],
            out_specs=[block(), full((8, 128))],
        ),
        out_shape=[shape((held, size, size), wide), shape((8, 128), wide)],
        compiler_params=params(),
        name="turn",
    )(named, owned, left_basis, right_basis)
    total = everywhere(total)

    count = owners.shape[0] * size * size + vectors.shape[0] * width
    small = full((12, width))
    new_master, new_first, new_second, clip, new_vectors, new_vector_first, new_vector_second = (
        pl.pallas_call(
            functools.partial(adam_kernel, count),
            grid=(held,),
            in_specs=[full((8, 128))] + [block() for _ in range(6)] + [small] * 4,
            out_specs=[block(), block(), block(), full((1, 1)), small, small, small],
            out_shape=[shape((held, size, size), wide)] * 3
            + [shape((1, 1), wide)]
            + [shape((12, width), wide)] * 3,
            scratch_shapes=[pltpu.VMEM((1, 1), wide)],
            compiler_params=params(),
            name="adam",
        )(
            total,
            rotated,
            master,
            first_moment,
            second_moment,
            left_basis,
            right_basis,
            vector_sum,
            vectors,
            vector_first,
            vector_second,
        )
    )
    return (
        result,
        grad_input,
        clip.reshape(()),
        new_master,
        new_first,
        new_second,
        new_vectors,
        new_vector_first,
        new_vector_second,
    )


def solution(mesh):
    sizes = (mesh.shape["dp"], mesh.shape["fsdp"])
    rows = P(AXES, None)
    blocks = P(AXES, None, None)
    return jax.shard_map(
        functools.partial(shards, sizes),
        mesh=mesh,
        in_specs=(rows, rows, rows, P(), blocks, blocks, blocks, blocks, blocks, P(), P(), P()),
        out_specs=(rows, rows, P(), blocks, blocks, blocks, P(), P(), P()),
        check_vma=False,
    )
```

```python
import functools
import math

import jax
import jax.numpy as jnp
from jax import lax
from jax.experimental import pallas as pl
from jax.experimental.pallas import tpu as pltpu
from jax.sharding import PartitionSpec as P

HEADS = 12
STEP = 2
AXES = ("dp", "fsdp")

norm_eps = 1e-06
adam_eps = 1e-08
beta = 0.5
rate_matrix = 0.03
rate_vector = 0.05
decay_weight = 0.01
highest = lax.Precision.HIGHEST
far = 2.0**30
low = jnp.bfloat16
wide = jnp.float32

CHUNK = 512


def ring_order(dp, fsdp):
    if (dp, fsdp) != (8, 4):
        return None
    order = []
    for turn, (x, y) in enumerate(((0, 0), (1, 0), (1, 1), (0, 1))):
        places = range(4) if turn % 2 == 0 else range(3, -1, -1)
        for z in places:
            order += [(z * 2 + x) * 4 + y * 2 + core for core in (0, 1)]
    return order


def mm(a, b, ca, cb):
    return lax.dot_general(a, b, (((ca,), (cb,)), ((), ())), preferred_element_type=wide)


def normal_parts(values):
    center = values - jnp.mean(values, axis=-1, keepdims=True)
    factor = lax.rsqrt(jnp.mean(center * center, axis=-1, keepdims=True) + norm_eps)
    return center * factor, factor


def norm_back(grad, normal, factor, gain):
    inner = grad * gain
    return factor * (
        inner
        - jnp.mean(inner, axis=-1, keepdims=True)
        - normal * jnp.mean(inner * normal, axis=-1, keepdims=True)
    )


def start_blocks(place, whole, target, sem, first, across, row0, col0, height, breadth):
    def one(index, carry):
        r = index // breadth
        c = index % breadth
        slot = place[first + (row0 + r) * across + col0 + c]
        pltpu.make_async_copy(
            whole.at[slot],
            target.at[pl.ds(pl.multiple_of(r * 128, 128), 128), pl.ds(pl.multiple_of(c * 128, 128), 128)],
            sem,
        ).start()
        return carry

    lax.fori_loop(0, height * breadth, one, 0)


def store_blocks(place, source, buffer, sem, first, across, row0, col0, height, breadth):
    def one(index, carry):
        r = index // breadth
        c = index % breadth
        slot = place[first + (row0 + r) * across + col0 + c]
        pltpu.make_async_copy(
            source.at[pl.ds(pl.multiple_of(r * 128, 128), 128), pl.ds(pl.multiple_of(c * 128, 128), 128)],
            buffer.at[slot],
            sem,
        ).start()
        return carry

    lax.fori_loop(0, height * breadth, one, 0)


def await_bytes(ref, sem):
    pltpu.make_async_copy(ref, ref, sem).wait()


TILE = 112


def tiles(rows):
    return rows // TILE


def rows_of(t):
    return pl.ds(pl.multiple_of(t * TILE, 16), TILE)


def qkv_kernel(place, whole, patches, vectors, project, weight, normed, sems):
    rows, width = patches.shape
    side = width // 128
    for part in range(3):
        start_blocks(
            place, whole, weight.at[part], sems.at[part], 0, 3 * side, 0, part * side, side, side
        )

    def norm(t, carry):
        at = rows_of(t)
        normal, _ = normal_parts(patches[at, :].astype(wide))
        normed[at, :] = (normal * vectors[0:1, :] + vectors[1:2, :]).astype(low)
        return carry

    lax.fori_loop(0, tiles(rows), norm, 0)
    for part in range(3):
        await_bytes(weight.at[part], sems.at[part])
        out = mm(normed[...], weight[part], 1, 0)
        if part == 0:
            out = out + vectors[2:3, :]
        if part == 2:
            out = out + vectors[3:4, :]
        project[:, part * width : (part + 1) * width] = out.astype(low)


def attend_kernel(query, keys, values, image_query, image_keys, mixed, probs, scores):
    rows = query.shape[0]
    lane = lax.broadcasted_iota(jnp.int32, (rows, 128), 1)
    wide_keys = jnp.concatenate([keys[...], image_keys[...]], axis=1)
    scaled = query[...] * jnp.asarray(0.125, low)
    outs = []
    for h in range(2):
        part = jnp.where(lane // 64 == h, scaled, jnp.zeros_like(scaled))
        scores[h] = mm(jnp.concatenate([part, image_query[...]], axis=1), wide_keys, 1, 1)
    for h in range(2):
        for t in range(tiles(rows)):
            at = slice(t * TILE, (t + 1) * TILE)
            s = scores[h, at, :]
            e = jnp.exp(s - jnp.max(s, axis=-1, keepdims=True))
            total = jnp.sum(e, axis=-1, keepdims=True)
            probs[h, at, :] = (e * (1.0 / total)).astype(low)
        outs.append(mm(probs[h], values[...], 1, 0))
    mixed[...] = jnp.where(lane < 64, outs[0], outs[1]).astype(low)


def feed_kernel(
    place,
    whole,
    patches,
    cotangent,
    mixed,
    inside,
    vectors,
    bias_up,
    middle,
    active,
    grad_middle,
    grad_mixed,
    sums,
    sums_up,
    buffer,
    w_out,
    w_up,
    w_down,
    normal,
    factor,
    second,
    second_t,
    grad_two,
    out_sum,
    back_sum,
    stage_up,
    stage_down,
    stage_out,
    grad_pre,
    sems,
    out_sems,
):
    step = pl.program_id(0)
    steps = pl.num_programs(0)
    rows, width = patches.shape
    side = width // 128
    hidden = 4 * width
    high = hidden // 128
    per = CHUNK // 128
    first_out = 3 * side * side
    first_up = 4 * side * side
    first_down = first_up + side * high

    def fetch(index, slot):
        start_blocks(
            place, whole, w_up.at[slot], sems.at[slot], first_up, high, 0, index * per, side, per
        )
        start_blocks(
            place, whole, w_down.at[slot], sems.at[2 + slot], first_down, side, index * per, 0, per, side
        )

    @pl.when(step == 0)
    def _():
        start_blocks(place, whole, w_out, sems.at[4], first_out, side, 0, 0, side, side)
        fetch(0, 0)
        fetch(1, 1)
        await_bytes(w_out, sems.at[4])
        out_sum[...] = mm(mixed[...], w_out[...], 1, 0)

        def norm(t, total):
            at = rows_of(t)
            keep = inside[at, :]
            mid = patches[at, :].astype(wide) + keep * (out_sum[at, :] + vectors[4:5, :])
            middle[at, :] = mid
            scaled, q = normal_parts(mid)
            normal[at, :] = scaled
            factor[at, :] = q
            second[at, :] = (scaled * vectors[5:6, :] + vectors[6:7, :]).astype(low)
            two = (keep * cotangent[at, :].astype(wide)).astype(low)
            grad_two[at, :] = two
            return total + jnp.sum(two.astype(wide), axis=0, keepdims=True)

        sums[3:4, :] = lax.fori_loop(0, tiles(rows), norm, jnp.zeros((1, width), wide))
        second_t[...] = second[...].T

    slot = lax.rem(step, 2)
    await_bytes(w_up.at[slot], sems.at[slot])
    await_bytes(w_down.at[slot], sems.at[2 + slot])
    up = w_up[slot]
    down = w_down[slot]
    pre = mm(second[...], up, 1, 0) + bias_up[0]
    grad_active = mm(grad_two[...], down, 1, 1)
    half = 0.5 * (1.0 + lax.erf(pre * math.sqrt(0.5)))
    active[...] = (pre * half).astype(low)
    slope = half + pre * (jnp.exp(-0.5 * pre * pre) * (1.0 / math.sqrt(2.0 * math.pi)))
    back = (grad_active * slope).astype(low)
    grad_pre[...] = back
    sums_up[0] = jnp.sum(back.astype(wide), axis=0, keepdims=True)
    came = mm(grad_pre[...], up, 1, 1)

    @pl.when(step == 0)
    def _():
        back_sum[...] = came

    @pl.when(step > 0)
    def _():
        back_sum[...] += came

    @pl.when(step >= 2)
    def _():
        await_bytes(stage_up.at[slot], out_sems.at[slot])
        await_bytes(stage_down.at[slot], out_sems.at[2 + slot])

    stage_up[slot] = mm(second_t[...], grad_pre[...], 1, 0).astype(low)
    stage_down[slot] = mm(active[...], grad_two[...], 0, 0).astype(low)
    store_blocks(
        place, stage_up.at[slot], buffer, out_sems.at[slot], first_up, high, 0, step * per, side, per
    )
    store_blocks(
        place, stage_down.at[slot], buffer, out_sems.at[2 + slot], first_down, side, step * per, 0, per, side
    )

    @pl.when(step + 2 < steps)
    def _():
        fetch(step + 2, slot)

    @pl.when(step == steps - 1)
    def _():
        def finish(t, total):
            at = rows_of(t)
            keep = inside[at, :]
            grad = back_sum[at, :]
            scaled = normal[at, :]
            mid = cotangent[at, :].astype(wide) + norm_back(
                grad, scaled, factor[at, :], vectors[5:6, :]
            )
            grad_middle[at, :] = mid
            one = (keep * mid).astype(low)
            second[at, :] = one
            gain, shift, bias = total
            return (
                gain + jnp.sum(grad * scaled, axis=0, keepdims=True),
                shift + jnp.sum(grad, axis=0, keepdims=True),
                bias + jnp.sum(one.astype(wide), axis=0, keepdims=True),
            )

        empty = jnp.zeros((1, width), wide)
        gain, shift, bias = lax.fori_loop(0, tiles(rows), finish, (empty, empty, empty))
        sums[0:1, :] = bias
        sums[1:2, :] = gain
        sums[2:3, :] = shift
        sums[4:8, :] = jnp.zeros((4, width), wide)
        stage_out[...] = mm(mixed[...], second[...], 0, 0).astype(low)
        store_blocks(place, stage_out, buffer, out_sems.at[4], first_out, side, 0, 0, side, side)
        grad_mixed[...] = mm(second[...], w_out[...], 1, 1).astype(low)
        for other in range(2):
            await_bytes(stage_up.at[other], out_sems.at[other])
            await_bytes(stage_down.at[other], out_sems.at[2 + other])
        await_bytes(stage_out, out_sems.at[4])


def back_kernel(
    place,
    held,
    query,
    keys,
    values,
    probs,
    grad_mixed,
    mixed,
    patches,
    vectors,
    grad_project,
    buffer,
    grad_low,
    normed,
    stage,
    out_sems,
):
    del held
    step = pl.program_id(0)
    steps = pl.num_programs(0)
    rows, width = patches.shape
    side = width // 128
    scale = 0.125

    @pl.when(step == 0)
    def _():
        def norm(t, carry):
            at = rows_of(t)
            normal, _ = normal_parts(patches[at, :].astype(wide))
            normed[at, :] = (normal * vectors[0:1, :] + vectors[1:2, :]).astype(low)
            return carry

        lax.fori_loop(0, tiles(rows), norm, 0)

    lane = lax.broadcasted_iota(jnp.int32, (rows, 128), 1)
    grad = grad_mixed[...]
    grad_t = grad.T
    query_t = query[...].T
    outer = grad.astype(wide) * mixed[...].astype(wide)
    turned_query = []
    turned_keys = []
    turned_values = []
    for h in range(2):
        mine = lane // 64 == h
        delta = jnp.sum(jnp.where(mine, outer, 0.0), axis=-1, keepdims=True)
        part = jnp.where(mine, grad, jnp.zeros_like(grad))
        grad_probs = mm(part, values[...], 1, 1)
        grad_low[h] = (probs[h].astype(wide) * (grad_probs - delta)).astype(low)
        turned_query.append(mm(grad_low[h], keys[...], 1, 0))
        turned_keys.append(mm(query_t[h * 64 : (h + 1) * 64, :], grad_low[h], 1, 0))
        turned_values.append(mm(grad_t[h * 64 : (h + 1) * 64, :], probs[h], 1, 0))
    grad_query = jnp.where(lane < 64, turned_query[0], turned_query[1]) * scale
    grad_keys = (jnp.concatenate(turned_keys, axis=0) * scale).T
    grad_values = jnp.concatenate(turned_values, axis=0).T
    at = pl.multiple_of(step * 128, 128)
    for part, value in enumerate((grad_query, grad_keys, grad_values)):
        grad_project[part, :, pl.ds(at, 128)] = value.astype(low)

    @pl.when(step == steps - 1)
    def _():
        for part in range(3):
            if part == 2:
                await_bytes(stage.at[0], out_sems.at[0])
            stage[part % 2] = mm(normed[...], grad_project[part], 0, 0).astype(low)
            store_blocks(
                place,
                stage.at[part % 2],
                buffer,
                out_sems.at[part % 2],
                0,
                3 * side,
                0,
                part * side,
                side,
                side,
            )
        await_bytes(stage.at[1], out_sems.at[1])
        await_bytes(stage.at[0], out_sems.at[0])


def result_kernel(place, whole, active, middle, inside, vectors, result, w_down, total, sems):
    step = pl.program_id(0)
    steps = pl.num_programs(0)
    rows, width = middle.shape
    side = width // 128
    high = 4 * side
    per = CHUNK // 128
    first_down = 4 * side * side + side * high

    def fetch(index, slot):
        start_blocks(
            place, whole, w_down.at[slot], sems.at[slot], first_down, side, index * per, 0, per, side
        )

    @pl.when(step == 0)
    def _():
        total[...] = jnp.zeros_like(total)
        fetch(0, 0)
        fetch(1, 1)

    slot = lax.rem(step, 2)
    await_bytes(w_down.at[slot], sems.at[slot])
    total[...] += mm(active[...], w_down[slot], 1, 0)

    @pl.when(step + 2 < steps)
    def _():
        fetch(step + 2, slot)

    @pl.when(step == steps - 1)
    def _():
        def finish(t, carry):
            at = rows_of(t)
            result[at, :] = (
                middle[at, :] + inside[at, :] * (total[at, :] + vectors[11:12, :])
            ).astype(low)
            return carry

        lax.fori_loop(0, tiles(rows), finish, 0)


def input_kernel(
    place, whole, grad_project, patches, grad_middle, vectors, grad_input, sums, weight, grad_sum, sems
):
    rows, width = patches.shape
    side = width // 128
    for part in range(3):
        start_blocks(
            place, whole, weight.at[part], sems.at[part], 0, 3 * side, 0, part * side, side, side
        )
    for part in range(3):
        await_bytes(weight.at[part], sems.at[part])
    total = mm(grad_project[0], weight[0], 1, 1)
    total = total + mm(grad_project[1], weight[1], 1, 1)
    grad_sum[...] = total + mm(grad_project[2], weight[2], 1, 1)

    def finish(t, carry):
        at = rows_of(t)
        grad = grad_sum[at, :]
        normal, factor = normal_parts(patches[at, :].astype(wide))
        back = norm_back(grad, normal, factor, vectors[0:1, :])
        grad_input[at, :] = (grad_middle[at, :] + back).astype(low)
        gain, shift, bias_query, bias_value = carry
        return (
            gain + jnp.sum(grad * normal, axis=0, keepdims=True),
            shift + jnp.sum(grad, axis=0, keepdims=True),
            bias_query + jnp.sum(grad_project[0, at, :].astype(wide), axis=0, keepdims=True),
            bias_value + jnp.sum(grad_project[2, at, :].astype(wide), axis=0, keepdims=True),
        )

    empty = jnp.zeros((1, width), wide)
    found = lax.fori_loop(0, tiles(rows), finish, (empty, empty, empty, empty))
    for row in range(4):
        sums[row : row + 1, :] = found[row]
    sums[4:8, :] = jnp.zeros((4, width), wide)


VMEM_LIMIT = 60 * 1024 * 1024


def params(count=1):
    return pltpu.CompilerParams(
        dimension_semantics=("arbitrary",) * count, vmem_limit_bytes=VMEM_LIMIT
    )


def whole_spec():
    return pl.BlockSpec(memory_space=pl.ANY)


def full(shape):
    return pl.BlockSpec(shape, lambda *_: (0,) * len(shape))


def shards(
    sizes,
    patches,
    lengths,
    cotangent,
    owners,
    master,
    first_moment,
    second_moment,
    left_basis,
    right_basis,
    vectors,
    vector_first,
    vector_second,
):
    dp, fsdp = sizes
    devices = dp * fsdp
    rows, width = patches.shape
    hidden = 4 * width
    side = width // 128
    pairs = width // 128
    held, size = master.shape[0], master.shape[1]
    slots = held * devices
    shape = jax.ShapeDtypeStruct
    me = lax.axis_index(AXES)
    order = ring_order(dp, fsdp)
    groups = None if order is None else [order]

    def gather(value):
        return lax.all_gather(value, AXES, axis=0, tiled=True, axis_index_groups=groups)

    def scatter(value):
        return lax.psum_scatter(
            value, AXES, scatter_dimension=0, tiled=True, axis_index_groups=groups
        )

    def everywhere(value):
        step = 1
        while step < devices:
            value = value + lax.ppermute(value, AXES, [(d, d ^ step) for d in range(devices)])
            step *= 2
        return value

    whole = gather(master.astype(low))
    if order is None:
        place = owners
    else:
        rank = [0] * devices
        for spot, device in enumerate(order):
            rank[device] = spot
        device = owners // held
        spot = jnp.sum(
            jnp.where(
                device[:, None] == jnp.arange(devices, dtype=jnp.int32)[None, :],
                jnp.array(rank, jnp.int32)[None, :],
                0,
            ),
            axis=1,
        )
        place = spot * held + owners % held
    mine = me * held + jnp.arange(held, dtype=jnp.int32)
    named = jnp.any(mine[:, None] == owners[None, :], axis=1)

    counts = lengths[0]
    ends = jnp.cumsum(counts)
    places = jnp.arange(rows, dtype=jnp.int32)[:, None]
    image = jnp.sum((places >= ends[None, :]).astype(jnp.int32), axis=1, keepdims=True)
    within = places < ends[-1]
    image = jnp.where(within, image, 4)
    inside = within.astype(wide)
    lanes = jnp.arange(128, dtype=jnp.int32)[None, :]
    image_keys = (lanes == image).astype(low)
    image_query = jnp.where((lanes != image) & (lanes < 5), -far, 0.0).astype(low)

    project = pl.pallas_call(
        qkv_kernel,
        grid_spec=pltpu.PrefetchScalarGridSpec(
            num_scalar_prefetch=1,
            grid=(1,),
            in_specs=[whole_spec(), full((rows, width)), full((12, width))],
            out_specs=full((rows, 3 * width)),
            scratch_shapes=[
                pltpu.VMEM((3, width, width), low),
                pltpu.VMEM((rows, width), low),
                pltpu.SemaphoreType.DMA((3,)),
            ],
        ),
        out_shape=shape((rows, 3 * width), low),
        compiler_params=params(),
        name="qkv",
    )(place, whole, patches, vectors)

    def column(offset):
        return pl.BlockSpec((rows, 128), lambda j, *_: (0, j + offset))

    mixed, probs = pl.pallas_call(
        attend_kernel,
        grid=(pairs,),
        in_specs=[
            column(0),
            column(pairs),
            column(2 * pairs),
            full((rows, 128)),
            full((rows, 128)),
        ],
        out_specs=[column(0), pl.BlockSpec((2, rows, rows), lambda j: (j, 0, 0))],
        out_shape=[shape((rows, width), low), shape((HEADS, rows, rows), low)],
        scratch_shapes=[pltpu.VMEM((2, rows, rows), wide)],
        compiler_params=params(),
        name="attend",
    )(project, project, project, image_query, image_keys)

    steps = hidden // CHUNK
    middle, active, grad_middle, grad_mixed, sums_two, sums_up, buffer = pl.pallas_call(
        feed_kernel,
        grid_spec=pltpu.PrefetchScalarGridSpec(
            num_scalar_prefetch=1,
            grid=(steps,),
            in_specs=[
                whole_spec(),
                full((rows, width)),
                full((rows, width)),
                full((rows, width)),
                full((rows, 1)),
                full((12, width)),
                pl.BlockSpec((1, 1, CHUNK), lambda c, *_: (c, 0, 0)),
            ],
            out_specs=[
                full((rows, width)),
                pl.BlockSpec((rows, CHUNK), lambda c, *_: (0, c)),
                full((rows, width)),
                full((rows, width)),
                full((8, width)),
                pl.BlockSpec((1, 1, CHUNK), lambda c, *_: (c, 0, 0)),
                whole_spec(),
            ],
            scratch_shapes=[
                pltpu.VMEM((width, width), low),
                pltpu.VMEM((2, width, CHUNK), low),
                pltpu.VMEM((2, CHUNK, width), low),
                pltpu.VMEM((rows, width), wide),
                pltpu.VMEM((rows, 1), wide),
                pltpu.VMEM((rows, width), low),
                pltpu.VMEM((width, rows), low),
                pltpu.VMEM((rows, width), low),
                pltpu.VMEM((rows, width), wide),
                pltpu.VMEM((rows, width), wide),
                pltpu.VMEM((2, width, CHUNK), low),
                pltpu.VMEM((2, CHUNK, width), low),
                pltpu.VMEM((width, width), low),
                pltpu.VMEM((rows, CHUNK), low),
                pltpu.SemaphoreType.DMA((5,)),
                pltpu.SemaphoreType.DMA((5,)),
            ],
        ),
        out_shape=[
            shape((rows, width), wide),
            shape((rows, hidden), low),
            shape((rows, width), wide),
            shape((rows, width), low),
            shape((8, width), wide),
            shape((steps, 1, CHUNK), wide),
            shape((slots, size, size), low),
        ],
        compiler_params=params(),
        name="feed",
    )(
        place,
        whole,
        patches,
        cotangent,
        mixed,
        inside,
        vectors,
        vectors[7:11].reshape(steps, 1, CHUNK),
    )

    grad_project, buffer = pl.pallas_call(
        back_kernel,
        grid_spec=pltpu.PrefetchScalarGridSpec(
            num_scalar_prefetch=1,
            grid=(pairs,),
            in_specs=[
                whole_spec(),
                column(0),
                column(pairs),
                column(2 * pairs),
                pl.BlockSpec((2, rows, rows), lambda j, *_: (j, 0, 0)),
                column(0),
                column(0),
                full((rows, width)),
                full((12, width)),
            ],
            out_specs=[full((3, rows, width)), whole_spec()],
            scratch_shapes=[
                pltpu.VMEM((2, rows, rows), low),
                pltpu.VMEM((rows, width), low),
                pltpu.VMEM((2, width, width), low),
                pltpu.SemaphoreType.DMA((2,)),
            ],
        ),
        out_shape=[
            shape((3, rows, width), low),
            shape((slots, size, size), low),
        ],
        input_output_aliases={1: 1},
        compiler_params=params(),
        name="back",
    )(
        place,
        buffer,
        project,
        project,
        project,
        probs,
        grad_mixed,
        mixed,
        patches,
        vectors,
    )
    owned = scatter(buffer)

    grad_input, sums_one = pl.pallas_call(
        input_kernel,
        grid_spec=pltpu.PrefetchScalarGridSpec(
            num_scalar_prefetch=1,
            grid=(1,),
            in_specs=[
                whole_spec(),
                full((3, rows, width)),
                full((rows, width)),
                full((rows, width)),
                full((12, width)),
            ],
            out_specs=[full((rows, width)), full((8, width))],
            scratch_shapes=[
                pltpu.VMEM((3, width, width), low),
                pltpu.VMEM((rows, width), wide),
                pltpu.SemaphoreType.DMA((3,)),
            ],
        ),
        out_shape=[shape((rows, width), low), shape((8, width), wide)],
        compiler_params=params(),
        name="input",
    )(place, whole, grad_project, patches, grad_middle, vectors)
    result = pl.pallas_call(
        result_kernel,
        grid_spec=pltpu.PrefetchScalarGridSpec(
            num_scalar_prefetch=1,
            grid=(steps,),
            in_specs=[
                whole_spec(),
                pl.BlockSpec((rows, CHUNK), lambda c, *_: (0, c)),
                full((rows, width)),
                full((rows, 1)),
                full((12, width)),
            ],
            out_specs=full((rows, width)),
            scratch_shapes=[
                pltpu.VMEM((2, CHUNK, width), low),
                pltpu.VMEM((rows, width), wide),
                pltpu.SemaphoreType.DMA((2,)),
            ],
        ),
        out_shape=shape((rows, width), low),
        compiler_params=params(),
        name="result",
    )(place, whole, active, middle, inside, vectors)
    vector_grad = jnp.concatenate(
        [sums_one[0:4], sums_two[0:3], sums_up.reshape(4, width), sums_two[3:4]], axis=0
    )
    vector_sum = everywhere(vector_grad)

    owned, vector_sum, result = lax.optimization_barrier((owned, vector_sum, result))

    owned = jnp.where(named[:, None, None], owned.astype(wide), 0.0)
    total_blocks = everywhere(jnp.broadcast_to(jnp.sum(owned * owned), (8, 128)))[0, 0]
    clip_norm = jnp.sqrt(total_blocks + jnp.sum(vector_sum * vector_sum))
    count = owners.shape[0] * size * size + vectors.shape[0] * width
    factor = jnp.minimum(1.0, 0.5 * math.sqrt(count) / clip_norm)
    turned = jnp.einsum("sji,sjk->sik", left_basis, owned, precision=highest)
    rotated = factor * jnp.einsum("sik,skl->sil", turned, right_basis, precision=highest)
    new_first = beta * first_moment + (1.0 - beta) * rotated
    new_second = beta * second_moment + (1.0 - beta) * rotated * rotated
    correction = 1.0 - beta**STEP
    direction = new_first / correction / (jnp.sqrt(new_second / correction) + adam_eps)
    back_turn = jnp.einsum("sij,sjk->sik", left_basis, direction, precision=highest)
    update = jnp.einsum("sik,slk->sil", back_turn, right_basis, precision=highest)
    new_master = master - rate_matrix * (update + decay_weight * master)
    vector_clip = factor * vector_sum
    new_vector_first = beta * vector_first + (1.0 - beta) * vector_clip
    new_vector_second = beta * vector_second + (1.0 - beta) * vector_clip * vector_clip
    vector_step = (
        new_vector_first / correction / (jnp.sqrt(new_vector_second / correction) + adam_eps)
    )
    new_vectors = vectors - rate_vector * vector_step
    return (
        result,
        grad_input,
        clip_norm,
        new_master,
        new_first,
        new_second,
        new_vectors,
        new_vector_first,
        new_vector_second,
    )


def solution(mesh):
    sizes = (mesh.shape["dp"], mesh.shape["fsdp"])
    rows = P(AXES, None)
    blocks = P(AXES, None, None)
    return jax.shard_map(
        functools.partial(shards, sizes),
        mesh=mesh,
        in_specs=(rows, rows, rows, P(), blocks, blocks, blocks, blocks, blocks, P(), P(), P()),
        out_specs=(rows, rows, P(), blocks, blocks, blocks, P(), P(), P()),
        check_vma=False,
    )
```

```python
import functools
import math

import jax
import jax.numpy as jnp
from jax import lax
from jax.experimental import pallas as pl
from jax.experimental.pallas import tpu as pltpu
from jax.sharding import PartitionSpec as P

HEADS = 12
STEP = 2
AXES = ("dp", "fsdp")

norm_eps = 1e-06
adam_eps = 1e-08
beta = 0.5
rate_matrix = 0.03
rate_vector = 0.05
decay_weight = 0.01
highest = lax.Precision.HIGHEST
far = 2.0**30
low = jnp.bfloat16
wide = jnp.float32

CHUNK = 512


def ring_order(dp, fsdp):
    if (dp, fsdp) != (8, 4):
        return None
    order = []
    for turn, (x, y) in enumerate(((0, 0), (1, 0), (1, 1), (0, 1))):
        places = range(4) if turn % 2 == 0 else range(3, -1, -1)
        for z in places:
            order += [(z * 2 + x) * 4 + y * 2 + core for core in (0, 1)]
    return order


def mm(a, b, ca, cb):
    return lax.dot_general(a, b, (((ca,), (cb,)), ((), ())), preferred_element_type=wide)


def normal_parts(values):
    center = values - jnp.mean(values, axis=-1, keepdims=True)
    factor = lax.rsqrt(jnp.mean(center * center, axis=-1, keepdims=True) + norm_eps)
    return center * factor, factor


def norm_back(grad, normal, factor, gain):
    inner = grad * gain
    return factor * (
        inner
        - jnp.mean(inner, axis=-1, keepdims=True)
        - normal * jnp.mean(inner * normal, axis=-1, keepdims=True)
    )


def start_blocks(place, whole, target, sem, first, across, row0, col0, height, breadth):
    def one(r, carry):
        at = first + (row0 + r) * across + col0
        down = pl.ds(pl.multiple_of(r * 128, 128), 128)
        for c in range(breadth):
            pltpu.make_async_copy(
                whole.at[place[at + c]], target.at[down, pl.ds(c * 128, 128)], sem
            ).start()
        return carry

    lax.fori_loop(0, height, one, 0)


def store_blocks(place, source, buffer, sem, first, across, row0, col0, height, breadth):
    def one(r, carry):
        at = first + (row0 + r) * across + col0
        down = pl.ds(pl.multiple_of(r * 128, 128), 128)
        for c in range(breadth):
            pltpu.make_async_copy(
                source.at[down, pl.ds(c * 128, 128)], buffer.at[place[at + c]], sem
            ).start()
        return carry

    lax.fori_loop(0, height, one, 0)


def await_bytes(ref, sem):
    pltpu.make_async_copy(ref, ref, sem).wait()


TILE = 112


def tiles(rows):
    return rows // TILE


def rows_of(t):
    return pl.ds(pl.multiple_of(t * TILE, 16), TILE)


def qkv_kernel(place, whole, patches, vectors, project, weight, normed, sems):
    rows, width = patches.shape
    side = width // 128
    for part in range(3):
        start_blocks(
            place, whole, weight.at[part], sems.at[part], 0, 3 * side, 0, part * side, side, side
        )

    def norm(t, carry):
        at = rows_of(t)
        normal, _ = normal_parts(patches[at, :].astype(wide))
        normed[at, :] = (normal * vectors[0:1, :] + vectors[1:2, :]).astype(low)
        return carry

    lax.fori_loop(0, tiles(rows), norm, 0)
    for part in range(3):
        await_bytes(weight.at[part], sems.at[part])
        out = mm(normed[...], weight[part], 1, 0)
        if part == 0:
            out = out + vectors[2:3, :]
        if part == 2:
            out = out + vectors[3:4, :]
        project[:, part * width : (part + 1) * width] = out.astype(low)


def attend_kernel(query, keys, values, image_query, image_keys, mixed, probs, scores):
    rows = query.shape[0]
    lane = lax.broadcasted_iota(jnp.int32, (rows, 128), 1)
    wide_keys = jnp.concatenate([keys[...], image_keys[...]], axis=1)
    scaled = query[...] * jnp.asarray(0.125, low)
    outs = []
    for h in range(2):
        part = jnp.where(lane // 64 == h, scaled, jnp.zeros_like(scaled))
        scores[h] = mm(jnp.concatenate([part, image_query[...]], axis=1), wide_keys, 1, 1)
    for h in range(2):
        for t in range(tiles(rows)):
            at = slice(t * TILE, (t + 1) * TILE)
            s = scores[h, at, :]
            e = jnp.exp(s - jnp.max(s, axis=-1, keepdims=True))
            total = jnp.sum(e, axis=-1, keepdims=True)
            probs[h, at, :] = (e * (1.0 / total)).astype(low)
        outs.append(mm(probs[h], values[...], 1, 0))
    mixed[...] = jnp.where(lane < 64, outs[0], outs[1]).astype(low)


def feed_kernel(
    place,
    whole,
    patches,
    cotangent,
    mixed,
    inside,
    vectors,
    bias_up,
    middle,
    active,
    grad_middle,
    grad_mixed,
    sums,
    sums_up,
    buffer,
    w_out,
    w_up,
    w_down,
    normal,
    factor,
    second,
    second_t,
    grad_two,
    out_sum,
    back_sum,
    stage_up,
    stage_down,
    stage_out,
    grad_pre,
    sems,
    out_sems,
):
    step = pl.program_id(0)
    steps = pl.num_programs(0)
    rows, width = patches.shape
    side = width // 128
    hidden = 4 * width
    high = hidden // 128
    per = CHUNK // 128
    first_out = 3 * side * side
    first_up = 4 * side * side
    first_down = first_up + side * high

    def fetch(index, slot):
        start_blocks(
            place, whole, w_up.at[slot], sems.at[slot], first_up, high, 0, index * per, side, per
        )
        start_blocks(
            place, whole, w_down.at[slot], sems.at[2 + slot], first_down, side, index * per, 0, per, side
        )

    @pl.when(step == 0)
    def _():
        start_blocks(place, whole, w_out, sems.at[4], first_out, side, 0, 0, side, side)
        fetch(0, 0)
        fetch(1, 1)
        await_bytes(w_out, sems.at[4])
        out_sum[...] = mm(mixed[...], w_out[...], 1, 0)

        def norm(t, total):
            at = rows_of(t)
            keep = inside[at, :]
            mid = patches[at, :].astype(wide) + keep * (out_sum[at, :] + vectors[4:5, :])
            middle[at, :] = mid
            scaled, q = normal_parts(mid)
            normal[at, :] = scaled
            factor[at, :] = q
            second[at, :] = (scaled * vectors[5:6, :] + vectors[6:7, :]).astype(low)
            two = (keep * cotangent[at, :].astype(wide)).astype(low)
            grad_two[at, :] = two
            return total + jnp.sum(two.astype(wide), axis=0, keepdims=True)

        sums[3:4, :] = lax.fori_loop(0, tiles(rows), norm, jnp.zeros((1, width), wide))
        second_t[...] = second[...].T
        back_sum[...] = jnp.zeros_like(back_sum)

    slot = lax.rem(step, 2)
    await_bytes(w_up.at[slot], sems.at[slot])
    await_bytes(w_down.at[slot], sems.at[2 + slot])

    @pl.when(step >= 2)
    def _():
        await_bytes(stage_up.at[slot], out_sems.at[slot])
        await_bytes(stage_down.at[slot], out_sems.at[2 + slot])

    parts = [slice(h * (CHUNK // 2), (h + 1) * (CHUNK // 2)) for h in range(2)]
    pres = [mm(second[...], w_up[slot, :, p], 1, 0) + bias_up[0, :, p] for p in parts]
    grads = [mm(grad_two[...], w_down[slot, p, :], 1, 1) for p in parts]
    for p, pre, grad in zip(parts, pres, grads):
        half = 0.5 * (1.0 + lax.erf(pre * math.sqrt(0.5)))
        active[:, p] = (pre * half).astype(low)
        slope = half + pre * (jnp.exp(-0.5 * pre * pre) * (1.0 / math.sqrt(2.0 * math.pi)))
        back = (grad * slope).astype(low)
        grad_pre[:, p] = back
        sums_up[0, :, p] = jnp.sum(back.astype(wide), axis=0, keepdims=True)
        stage_up[slot, :, p] = mm(second_t[...], grad_pre[:, p], 1, 0).astype(low)
        stage_down[slot, p, :] = mm(active[:, p], grad_two[...], 0, 0).astype(low)
    back_sum[...] += mm(grad_pre[...], w_up[slot], 1, 1)
    store_blocks(
        place, stage_up.at[slot], buffer, out_sems.at[slot], first_up, high, 0, step * per, side, per
    )
    store_blocks(
        place, stage_down.at[slot], buffer, out_sems.at[2 + slot], first_down, side, step * per, 0, per, side
    )

    @pl.when(step + 2 < steps)
    def _():
        fetch(step + 2, slot)

    @pl.when(step == steps - 1)
    def _():
        def finish(t, total):
            at = rows_of(t)
            keep = inside[at, :]
            grad = back_sum[at, :]
            scaled = normal[at, :]
            mid = cotangent[at, :].astype(wide) + norm_back(
                grad, scaled, factor[at, :], vectors[5:6, :]
            )
            grad_middle[at, :] = mid
            one = (keep * mid).astype(low)
            second[at, :] = one
            gain, shift, bias = total
            return (
                gain + jnp.sum(grad * scaled, axis=0, keepdims=True),
                shift + jnp.sum(grad, axis=0, keepdims=True),
                bias + jnp.sum(one.astype(wide), axis=0, keepdims=True),
            )

        empty = jnp.zeros((1, width), wide)
        gain, shift, bias = lax.fori_loop(0, tiles(rows), finish, (empty, empty, empty))
        sums[0:1, :] = bias
        sums[1:2, :] = gain
        sums[2:3, :] = shift
        sums[4:8, :] = jnp.zeros((4, width), wide)
        stage_out[...] = mm(mixed[...], second[...], 0, 0).astype(low)
        store_blocks(place, stage_out, buffer, out_sems.at[4], first_out, side, 0, 0, side, side)
        grad_mixed[...] = mm(second[...], w_out[...], 1, 1).astype(low)
        for other in range(2):
            await_bytes(stage_up.at[other], out_sems.at[other])
            await_bytes(stage_down.at[other], out_sems.at[2 + other])
        await_bytes(stage_out, out_sems.at[4])


def back_kernel(
    place,
    held,
    query,
    keys,
    values,
    probs,
    grad_mixed,
    mixed,
    patches,
    vectors,
    grad_project,
    buffer,
    grad_low,
    normed,
    stage,
    out_sems,
):
    del held
    step = pl.program_id(0)
    steps = pl.num_programs(0)
    rows, width = patches.shape
    side = width // 128
    scale = 0.125

    @pl.when(step == 0)
    def _():
        def norm(t, carry):
            at = rows_of(t)
            normal, _ = normal_parts(patches[at, :].astype(wide))
            normed[at, :] = (normal * vectors[0:1, :] + vectors[1:2, :]).astype(low)
            return carry

        lax.fori_loop(0, tiles(rows), norm, 0)

    lane = lax.broadcasted_iota(jnp.int32, (rows, 128), 1)
    grad = grad_mixed[...]
    grad_t = grad.T
    query_t = query[...].T
    outer = grad.astype(wide) * mixed[...].astype(wide)
    turned_query = []
    turned_keys = []
    turned_values = []
    for h in range(2):
        mine = lane // 64 == h
        delta = jnp.sum(jnp.where(mine, outer, 0.0), axis=-1, keepdims=True)
        part = jnp.where(mine, grad, jnp.zeros_like(grad))
        grad_probs = mm(part, values[...], 1, 1)
        grad_low[h] = (probs[h].astype(wide) * (grad_probs - delta)).astype(low)
        turned_query.append(mm(grad_low[h], keys[...], 1, 0))
        turned_keys.append(mm(query_t[h * 64 : (h + 1) * 64, :], grad_low[h], 1, 0))
        turned_values.append(mm(grad_t[h * 64 : (h + 1) * 64, :], probs[h], 1, 0))
    grad_query = jnp.where(lane < 64, turned_query[0], turned_query[1]) * scale
    grad_keys = (jnp.concatenate(turned_keys, axis=0) * scale).T
    grad_values = jnp.concatenate(turned_values, axis=0).T
    at = pl.multiple_of(step * 128, 128)
    for part, value in enumerate((grad_query, grad_keys, grad_values)):
        grad_project[part, :, pl.ds(at, 128)] = value.astype(low)

    @pl.when(step == steps - 1)
    def _():
        for part in range(3):
            if part == 2:
                await_bytes(stage.at[0], out_sems.at[0])
            stage[part % 2] = mm(normed[...], grad_project[part], 0, 0).astype(low)
            store_blocks(
                place,
                stage.at[part % 2],
                buffer,
                out_sems.at[part % 2],
                0,
                3 * side,
                0,
                part * side,
                side,
                side,
            )
        await_bytes(stage.at[1], out_sems.at[1])
        await_bytes(stage.at[0], out_sems.at[0])


def result_kernel(place, whole, active, middle, inside, vectors, result, w_down, total, sems):
    step = pl.program_id(0)
    steps = pl.num_programs(0)
    rows, width = middle.shape
    side = width // 128
    high = 4 * side
    per = CHUNK // 128
    first_down = 4 * side * side + side * high

    def fetch(index, slot):
        start_blocks(
            place, whole, w_down.at[slot], sems.at[slot], first_down, side, index * per, 0, per, side
        )

    @pl.when(step == 0)
    def _():
        total[...] = jnp.zeros_like(total)
        fetch(0, 0)
        fetch(1, 1)

    slot = lax.rem(step, 2)
    await_bytes(w_down.at[slot], sems.at[slot])
    total[...] += mm(active[...], w_down[slot], 1, 0)

    @pl.when(step + 2 < steps)
    def _():
        fetch(step + 2, slot)

    @pl.when(step == steps - 1)
    def _():
        def finish(t, carry):
            at = rows_of(t)
            result[at, :] = (
                middle[at, :] + inside[at, :] * (total[at, :] + vectors[11:12, :])
            ).astype(low)
            return carry

        lax.fori_loop(0, tiles(rows), finish, 0)


def input_kernel(
    place, whole, grad_project, patches, grad_middle, vectors, grad_input, sums, weight, grad_sum, sems
):
    rows, width = patches.shape
    side = width // 128
    for part in range(3):
        start_blocks(
            place, whole, weight.at[part], sems.at[part], 0, 3 * side, 0, part * side, side, side
        )
    for part in range(3):
        await_bytes(weight.at[part], sems.at[part])
    total = mm(grad_project[0], weight[0], 1, 1)
    total = total + mm(grad_project[1], weight[1], 1, 1)
    grad_sum[...] = total + mm(grad_project[2], weight[2], 1, 1)

    def finish(t, carry):
        at = rows_of(t)
        grad = grad_sum[at, :]
        normal, factor = normal_parts(patches[at, :].astype(wide))
        back = norm_back(grad, normal, factor, vectors[0:1, :])
        grad_input[at, :] = (grad_middle[at, :] + back).astype(low)
        gain, shift, bias_query, bias_value = carry
        return (
            gain + jnp.sum(grad * normal, axis=0, keepdims=True),
            shift + jnp.sum(grad, axis=0, keepdims=True),
            bias_query + jnp.sum(grad_project[0, at, :].astype(wide), axis=0, keepdims=True),
            bias_value + jnp.sum(grad_project[2, at, :].astype(wide), axis=0, keepdims=True),
        )

    empty = jnp.zeros((1, width), wide)
    found = lax.fori_loop(0, tiles(rows), finish, (empty, empty, empty, empty))
    for row in range(4):
        sums[row : row + 1, :] = found[row]
    sums[4:8, :] = jnp.zeros((4, width), wide)


VMEM_LIMIT = 60 * 1024 * 1024


def params(count=1):
    return pltpu.CompilerParams(
        dimension_semantics=("arbitrary",) * count, vmem_limit_bytes=VMEM_LIMIT
    )


def whole_spec():
    return pl.BlockSpec(memory_space=pl.ANY)


def full(shape):
    return pl.BlockSpec(shape, lambda *_: (0,) * len(shape))


def shards(
    sizes,
    patches,
    lengths,
    cotangent,
    owners,
    master,
    first_moment,
    second_moment,
    left_basis,
    right_basis,
    vectors,
    vector_first,
    vector_second,
):
    dp, fsdp = sizes
    devices = dp * fsdp
    rows, width = patches.shape
    hidden = 4 * width
    side = width // 128
    pairs = width // 128
    held, size = master.shape[0], master.shape[1]
    slots = held * devices
    shape = jax.ShapeDtypeStruct
    me = lax.axis_index(AXES)
    order = ring_order(dp, fsdp)
    groups = None if order is None else [order]

    def gather(value):
        return lax.all_gather(value, AXES, axis=0, tiled=True, axis_index_groups=groups)

    def scatter(value):
        return lax.psum_scatter(
            value, AXES, scatter_dimension=0, tiled=True, axis_index_groups=groups
        )

    def everywhere(value):
        step = 1
        while step < devices:
            value = value + lax.ppermute(value, AXES, [(d, d ^ step) for d in range(devices)])
            step *= 2
        return value

    whole = gather(master.astype(low))
    if order is None:
        place = owners
    else:
        rank = [0] * devices
        for spot, device in enumerate(order):
            rank[device] = spot
        device = owners // held
        spot = jnp.sum(
            jnp.where(
                device[:, None] == jnp.arange(devices, dtype=jnp.int32)[None, :],
                jnp.array(rank, jnp.int32)[None, :],
                0,
            ),
            axis=1,
        )
        place = spot * held + owners % held
    mine = me * held + jnp.arange(held, dtype=jnp.int32)
    named = jnp.any(mine[:, None] == owners[None, :], axis=1)

    counts = lengths[0]
    ends = jnp.cumsum(counts)
    places = jnp.arange(rows, dtype=jnp.int32)[:, None]
    image = jnp.sum((places >= ends[None, :]).astype(jnp.int32), axis=1, keepdims=True)
    within = places < ends[-1]
    image = jnp.where(within, image, 4)
    inside = within.astype(wide)
    lanes = jnp.arange(128, dtype=jnp.int32)[None, :]
    image_keys = (lanes == image).astype(low)
    image_query = jnp.where((lanes != image) & (lanes < 5), -far, 0.0).astype(low)

    project = pl.pallas_call(
        qkv_kernel,
        grid_spec=pltpu.PrefetchScalarGridSpec(
            num_scalar_prefetch=1,
            grid=(1,),
            in_specs=[whole_spec(), full((rows, width)), full((12, width))],
            out_specs=full((rows, 3 * width)),
            scratch_shapes=[
                pltpu.VMEM((3, width, width), low),
                pltpu.VMEM((rows, width), low),
                pltpu.SemaphoreType.DMA((3,)),
            ],
        ),
        out_shape=shape((rows, 3 * width), low),
        compiler_params=params(),
        name="qkv",
    )(place, whole, patches, vectors)

    def column(offset):
        return pl.BlockSpec((rows, 128), lambda j, *_: (0, j + offset))

    mixed, probs = pl.pallas_call(
        attend_kernel,
        grid=(pairs,),
        in_specs=[
            column(0),
            column(pairs),
            column(2 * pairs),
            full((rows, 128)),
            full((rows, 128)),
        ],
        out_specs=[column(0), pl.BlockSpec((2, rows, rows), lambda j: (j, 0, 0))],
        out_shape=[shape((rows, width), low), shape((HEADS, rows, rows), low)],
        scratch_shapes=[pltpu.VMEM((2, rows, rows), wide)],
        compiler_params=params(),
        name="attend",
    )(project, project, project, image_query, image_keys)

    steps = hidden // CHUNK
    middle, active, grad_middle, grad_mixed, sums_two, sums_up, buffer = pl.pallas_call(
        feed_kernel,
        grid_spec=pltpu.PrefetchScalarGridSpec(
            num_scalar_prefetch=1,
            grid=(steps,),
            in_specs=[
                whole_spec(),
                full((rows, width)),
                full((rows, width)),
                full((rows, width)),
                full((rows, 1)),
                full((12, width)),
                pl.BlockSpec((1, 1, CHUNK), lambda c, *_: (c, 0, 0)),
            ],
            out_specs=[
                full((rows, width)),
                pl.BlockSpec((rows, CHUNK), lambda c, *_: (0, c)),
                full((rows, width)),
                full((rows, width)),
                full((8, width)),
                pl.BlockSpec((1, 1, CHUNK), lambda c, *_: (c, 0, 0)),
                whole_spec(),
            ],
            scratch_shapes=[
                pltpu.VMEM((width, width), low),
                pltpu.VMEM((2, width, CHUNK), low),
                pltpu.VMEM((2, CHUNK, width), low),
                pltpu.VMEM((rows, width), wide),
                pltpu.VMEM((rows, 1), wide),
                pltpu.VMEM((rows, width), low),
                pltpu.VMEM((width, rows), low),
                pltpu.VMEM((rows, width), low),
                pltpu.VMEM((rows, width), wide),
                pltpu.VMEM((rows, width), wide),
                pltpu.VMEM((2, width, CHUNK), low),
                pltpu.VMEM((2, CHUNK, width), low),
                pltpu.VMEM((width, width), low),
                pltpu.VMEM((rows, CHUNK), low),
                pltpu.SemaphoreType.DMA((5,)),
                pltpu.SemaphoreType.DMA((5,)),
            ],
        ),
        out_shape=[
            shape((rows, width), wide),
            shape((rows, hidden), low),
            shape((rows, width), wide),
            shape((rows, width), low),
            shape((8, width), wide),
            shape((steps, 1, CHUNK), wide),
            shape((slots, size, size), low),
        ],
        compiler_params=params(),
        name="feed",
    )(
        place,
        whole,
        patches,
        cotangent,
        mixed,
        inside,
        vectors,
        vectors[7:11].reshape(steps, 1, CHUNK),
    )

    grad_project, buffer = pl.pallas_call(
        back_kernel,
        grid_spec=pltpu.PrefetchScalarGridSpec(
            num_scalar_prefetch=1,
            grid=(pairs,),
            in_specs=[
                whole_spec(),
                column(0),
                column(pairs),
                column(2 * pairs),
                pl.BlockSpec((2, rows, rows), lambda j, *_: (j, 0, 0)),
                column(0),
                column(0),
                full((rows, width)),
                full((12, width)),
            ],
            out_specs=[full((3, rows, width)), whole_spec()],
            scratch_shapes=[
                pltpu.VMEM((2, rows, rows), low),
                pltpu.VMEM((rows, width), low),
                pltpu.VMEM((2, width, width), low),
                pltpu.SemaphoreType.DMA((2,)),
            ],
        ),
        out_shape=[
            shape((3, rows, width), low),
            shape((slots, size, size), low),
        ],
        input_output_aliases={1: 1},
        compiler_params=params(),
        name="back",
    )(
        place,
        buffer,
        project,
        project,
        project,
        probs,
        grad_mixed,
        mixed,
        patches,
        vectors,
    )
    owned = scatter(buffer)

    grad_input, sums_one = pl.pallas_call(
        input_kernel,
        grid_spec=pltpu.PrefetchScalarGridSpec(
            num_scalar_prefetch=1,
            grid=(1,),
            in_specs=[
                whole_spec(),
                full((3, rows, width)),
                full((rows, width)),
                full((rows, width)),
                full((12, width)),
            ],
            out_specs=[full((rows, width)), full((8, width))],
            scratch_shapes=[
                pltpu.VMEM((3, width, width), low),
                pltpu.VMEM((rows, width), wide),
                pltpu.SemaphoreType.DMA((3,)),
            ],
        ),
        out_shape=[shape((rows, width), low), shape((8, width), wide)],
        compiler_params=params(),
        name="input",
    )(place, whole, grad_project, patches, grad_middle, vectors)
    result = pl.pallas_call(
        result_kernel,
        grid_spec=pltpu.PrefetchScalarGridSpec(
            num_scalar_prefetch=1,
            grid=(steps,),
            in_specs=[
                whole_spec(),
                pl.BlockSpec((rows, CHUNK), lambda c, *_: (0, c)),
                full((rows, width)),
                full((rows, 1)),
                full((12, width)),
            ],
            out_specs=full((rows, width)),
            scratch_shapes=[
                pltpu.VMEM((2, CHUNK, width), low),
                pltpu.VMEM((rows, width), wide),
                pltpu.SemaphoreType.DMA((2,)),
            ],
        ),
        out_shape=shape((rows, width), low),
        compiler_params=params(),
        name="result",
    )(place, whole, active, middle, inside, vectors)
    vector_grad = jnp.concatenate(
        [sums_one[0:4], sums_two[0:3], sums_up.reshape(4, width), sums_two[3:4]], axis=0
    )
    vector_sum = everywhere(vector_grad)

    owned, vector_sum, result = lax.optimization_barrier((owned, vector_sum, result))

    owned = jnp.where(named[:, None, None], owned.astype(wide), 0.0)
    squares = jnp.broadcast_to(jnp.sum(owned * owned), (devices, 128))
    total_blocks = jnp.sum(lax.all_to_all(squares, AXES, 0, 0, tiled=True)[:, 0])
    clip_norm = jnp.sqrt(total_blocks + jnp.sum(vector_sum * vector_sum))
    count = owners.shape[0] * size * size + vectors.shape[0] * width
    factor = jnp.minimum(1.0, 0.5 * math.sqrt(count) / clip_norm)
    turned = jnp.einsum("sji,sjk->sik", left_basis, owned, precision=highest)
    rotated = factor * jnp.einsum("sik,skl->sil", turned, right_basis, precision=highest)
    new_first = beta * first_moment + (1.0 - beta) * rotated
    new_second = beta * second_moment + (1.0 - beta) * rotated * rotated
    correction = 1.0 - beta**STEP
    direction = new_first / correction / (jnp.sqrt(new_second / correction) + adam_eps)
    back_turn = jnp.einsum("sij,sjk->sik", left_basis, direction, precision=highest)
    update = jnp.einsum("sik,slk->sil", back_turn, right_basis, precision=highest)
    new_master = master - rate_matrix * (update + decay_weight * master)
    vector_clip = factor * vector_sum
    new_vector_first = beta * vector_first + (1.0 - beta) * vector_clip
    new_vector_second = beta * vector_second + (1.0 - beta) * vector_clip * vector_clip
    vector_step = (
        new_vector_first / correction / (jnp.sqrt(new_vector_second / correction) + adam_eps)
    )
    new_vectors = vectors - rate_vector * vector_step
    return (
        result,
        grad_input,
        clip_norm,
        new_master,
        new_first,
        new_second,
        new_vectors,
        new_vector_first,
        new_vector_second,
    )


def solution(mesh):
    sizes = (mesh.shape["dp"], mesh.shape["fsdp"])
    rows = P(AXES, None)
    blocks = P(AXES, None, None)
    return jax.shard_map(
        functools.partial(shards, sizes),
        mesh=mesh,
        in_specs=(rows, rows, rows, P(), blocks, blocks, blocks, blocks, blocks, P(), P(), P()),
        out_specs=(rows, rows, P(), blocks, blocks, blocks, P(), P(), P()),
        check_vma=False,
    )
```

```python
import functools
import math

import jax
import jax.numpy as jnp
from jax import lax
from jax.experimental import pallas as pl
from jax.experimental.pallas import tpu as pltpu
from jax.sharding import PartitionSpec as P

HEADS = 12
STEP = 2
AXES = ("dp", "fsdp")

norm_eps = 1e-06
adam_eps = 1e-08
beta = 0.5
rate_matrix = 0.03
rate_vector = 0.05
decay_weight = 0.01
highest = lax.Precision.HIGHEST
far = 2.0**30
low = jnp.bfloat16
wide = jnp.float32

CHUNK = 512


def ring_order(dp, fsdp):
    if (dp, fsdp) != (8, 4):
        return None
    order = []
    for turn, (x, y) in enumerate(((0, 0), (1, 0), (1, 1), (0, 1))):
        places = range(4) if turn % 2 == 0 else range(3, -1, -1)
        for z in places:
            order += [(z * 2 + x) * 4 + y * 2 + core for core in (0, 1)]
    return order


def mm(a, b, ca, cb):
    return lax.dot_general(a, b, (((ca,), (cb,)), ((), ())), preferred_element_type=wide)


def normal_parts(values):
    center = values - jnp.mean(values, axis=-1, keepdims=True)
    factor = lax.rsqrt(jnp.mean(center * center, axis=-1, keepdims=True) + norm_eps)
    return center * factor, factor


def norm_back(grad, normal, factor, gain):
    inner = grad * gain
    return factor * (
        inner
        - jnp.mean(inner, axis=-1, keepdims=True)
        - normal * jnp.mean(inner * normal, axis=-1, keepdims=True)
    )


def start_blocks(place, whole, target, sem, first, across, row0, col0, height, breadth):
    def one(r, carry):
        at = first + (row0 + r) * across + col0
        down = pl.ds(pl.multiple_of(r * 128, 128), 128)
        for c in range(breadth):
            pltpu.make_async_copy(
                whole.at[place[at + c]], target.at[down, pl.ds(c * 128, 128)], sem
            ).start()
        return carry

    lax.fori_loop(0, height, one, 0)


def store_blocks(place, source, buffer, sem, first, across, row0, col0, height, breadth):
    def one(r, carry):
        at = first + (row0 + r) * across + col0
        down = pl.ds(pl.multiple_of(r * 128, 128), 128)
        for c in range(breadth):
            pltpu.make_async_copy(
                source.at[down, pl.ds(c * 128, 128)], buffer.at[place[at + c]], sem
            ).start()
        return carry

    lax.fori_loop(0, height, one, 0)


def await_bytes(ref, sem):
    pltpu.make_async_copy(ref, ref, sem).wait()


TILE = 112


def tiles(rows):
    return rows // TILE


def rows_of(t):
    return pl.ds(pl.multiple_of(t * TILE, 16), TILE)


def ready_kernel(patches, cotangent, inside, vectors, normed, normed_t, grad_two, bias_down):
    rows, width = patches.shape

    def norm(t, total):
        at = rows_of(t)
        normal, _ = normal_parts(patches[at, :].astype(wide))
        normed[at, :] = (normal * vectors[0:1, :] + vectors[1:2, :]).astype(low)
        two = (inside[at, :] * cotangent[at, :].astype(wide)).astype(low)
        grad_two[at, :] = two
        return total + jnp.sum(two.astype(wide), axis=0, keepdims=True)

    bias_down[...] = lax.fori_loop(0, tiles(rows), norm, jnp.zeros((1, width), wide))
    normed_t[...] = normed[...].T


def qkv_kernel(place, whole, normed, vectors, project, weight, sems):
    rows, width = normed.shape
    side = width // 128
    for part in range(3):
        start_blocks(
            place, whole, weight.at[part], sems.at[part], 0, 3 * side, 0, part * side, side, side
        )
    for part in range(3):
        await_bytes(weight.at[part], sems.at[part])
        out = mm(normed[...], weight[part], 1, 0)
        if part == 0:
            out = out + vectors[2:3, :]
        if part == 2:
            out = out + vectors[3:4, :]
        project[:, part * width : (part + 1) * width] = out.astype(low)


def attend_kernel(query, keys, values, image_query, image_keys, mixed, probs, scores):
    rows = query.shape[0]
    lane = lax.broadcasted_iota(jnp.int32, (rows, 128), 1)
    wide_keys = jnp.concatenate([keys[...], image_keys[...]], axis=1)
    scaled = query[...] * jnp.asarray(0.125, low)
    outs = []
    for h in range(2):
        part = jnp.where(lane // 64 == h, scaled, jnp.zeros_like(scaled))
        scores[h] = mm(jnp.concatenate([part, image_query[...]], axis=1), wide_keys, 1, 1)
    for h in range(2):
        for t in range(tiles(rows)):
            at = slice(t * TILE, (t + 1) * TILE)
            s = scores[h, at, :]
            e = jnp.exp(s - jnp.max(s, axis=-1, keepdims=True))
            total = jnp.sum(e, axis=-1, keepdims=True)
            probs[h, at, :] = (e * (1.0 / total)).astype(low)
        outs.append(mm(probs[h], values[...], 1, 0))
    mixed[...] = jnp.where(lane < 64, outs[0], outs[1]).astype(low)


def feed_kernel(
    place,
    whole,
    patches,
    cotangent,
    grad_two,
    mixed,
    inside,
    vectors,
    bias_up,
    middle,
    active,
    grad_middle,
    grad_mixed,
    sums,
    sums_up,
    buffer,
    w_out,
    w_up,
    w_down,
    normal,
    factor,
    second,
    second_t,
    out_sum,
    back_sum,
    stage_up,
    stage_down,
    stage_out,
    grad_pre,
    sems,
    out_sems,
):
    step = pl.program_id(0)
    steps = pl.num_programs(0)
    rows, width = patches.shape
    side = width // 128
    hidden = 4 * width
    high = hidden // 128
    per = CHUNK // 128
    first_out = 3 * side * side
    first_up = 4 * side * side
    first_down = first_up + side * high

    def fetch(index, slot):
        start_blocks(
            place, whole, w_up.at[slot], sems.at[slot], first_up, high, 0, index * per, side, per
        )
        start_blocks(
            place, whole, w_down.at[slot], sems.at[2 + slot], first_down, side, index * per, 0, per, side
        )

    @pl.when(step == 0)
    def _():
        start_blocks(place, whole, w_out, sems.at[4], first_out, side, 0, 0, side, side)
        fetch(0, 0)
        fetch(1, 1)
        await_bytes(w_out, sems.at[4])
        out_sum[...] = mm(mixed[...], w_out[...], 1, 0)

        def norm(t, carry):
            at = rows_of(t)
            keep = inside[at, :]
            mid = patches[at, :].astype(wide) + keep * (out_sum[at, :] + vectors[4:5, :])
            middle[at, :] = mid
            scaled, q = normal_parts(mid)
            normal[at, :] = scaled
            factor[at, :] = q
            second[at, :] = (scaled * vectors[5:6, :] + vectors[6:7, :]).astype(low)
            return carry

        lax.fori_loop(0, tiles(rows), norm, 0)
        second_t[...] = second[...].T
        back_sum[...] = jnp.zeros_like(back_sum)

    slot = lax.rem(step, 2)
    await_bytes(w_up.at[slot], sems.at[slot])
    await_bytes(w_down.at[slot], sems.at[2 + slot])

    @pl.when(step >= 2)
    def _():
        await_bytes(stage_up.at[slot], out_sems.at[slot])
        await_bytes(stage_down.at[slot], out_sems.at[2 + slot])

    parts = [slice(h * (CHUNK // 2), (h + 1) * (CHUNK // 2)) for h in range(2)]
    pres = [mm(second[...], w_up[slot, :, p], 1, 0) + bias_up[0, :, p] for p in parts]
    grads = [mm(grad_two[...], w_down[slot, p, :], 1, 1) for p in parts]
    for p, pre, grad in zip(parts, pres, grads):
        half = 0.5 * (1.0 + lax.erf(pre * math.sqrt(0.5)))
        active[:, p] = (pre * half).astype(low)
        slope = half + pre * (jnp.exp(-0.5 * pre * pre) * (1.0 / math.sqrt(2.0 * math.pi)))
        back = (grad * slope).astype(low)
        grad_pre[:, p] = back
        sums_up[0, :, p] = jnp.sum(back.astype(wide), axis=0, keepdims=True)
        stage_up[slot, :, p] = mm(second_t[...], grad_pre[:, p], 1, 0).astype(low)
        stage_down[slot, p, :] = mm(active[:, p], grad_two[...], 0, 0).astype(low)
    back_sum[...] += mm(grad_pre[...], w_up[slot], 1, 1)
    store_blocks(
        place, stage_up.at[slot], buffer, out_sems.at[slot], first_up, high, 0, step * per, side, per
    )
    store_blocks(
        place, stage_down.at[slot], buffer, out_sems.at[2 + slot], first_down, side, step * per, 0, per, side
    )

    @pl.when(step + 2 < steps)
    def _():
        fetch(step + 2, slot)

    @pl.when(step == steps - 1)
    def _():
        def finish(t, total):
            at = rows_of(t)
            keep = inside[at, :]
            grad = back_sum[at, :]
            scaled = normal[at, :]
            mid = cotangent[at, :].astype(wide) + norm_back(
                grad, scaled, factor[at, :], vectors[5:6, :]
            )
            grad_middle[at, :] = mid
            one = (keep * mid).astype(low)
            second[at, :] = one
            gain, shift, bias = total
            return (
                gain + jnp.sum(grad * scaled, axis=0, keepdims=True),
                shift + jnp.sum(grad, axis=0, keepdims=True),
                bias + jnp.sum(one.astype(wide), axis=0, keepdims=True),
            )

        empty = jnp.zeros((1, width), wide)
        gain, shift, bias = lax.fori_loop(0, tiles(rows), finish, (empty, empty, empty))
        sums[0:1, :] = bias
        sums[1:2, :] = gain
        sums[2:3, :] = shift
        sums[3:8, :] = jnp.zeros((5, width), wide)
        stage_out[...] = mm(mixed[...], second[...], 0, 0).astype(low)
        store_blocks(place, stage_out, buffer, out_sems.at[4], first_out, side, 0, 0, side, side)
        grad_mixed[...] = mm(second[...], w_out[...], 1, 1).astype(low)
        for other in range(2):
            await_bytes(stage_up.at[other], out_sems.at[other])
            await_bytes(stage_down.at[other], out_sems.at[2 + other])
        await_bytes(stage_out, out_sems.at[4])


def back_kernel(
    place,
    held,
    query,
    keys,
    values,
    probs,
    grad_mixed,
    mixed,
    normed_t,
    grad_project,
    buffer,
    grad_low,
    stage,
    out_sems,
):
    del held
    step = pl.program_id(0)
    steps = pl.num_programs(0)
    width, rows = normed_t.shape
    side = width // 128
    scale = 0.125
    lane = lax.broadcasted_iota(jnp.int32, (rows, 128), 1)
    grad = grad_mixed[...]
    grad_t = grad.T
    query_t = query[...].T
    outer = grad.astype(wide) * mixed[...].astype(wide)
    mine = [lane // 64 == h for h in range(2)]
    grad_probs = [
        mm(jnp.where(mine[h], grad, jnp.zeros_like(grad)), values[...], 1, 1) for h in range(2)
    ]
    turned_values = [mm(grad_t[h * 64 : (h + 1) * 64, :], probs[h], 1, 0) for h in range(2)]
    turned_query = []
    turned_keys = []
    for h in range(2):
        delta = jnp.sum(jnp.where(mine[h], outer, 0.0), axis=-1, keepdims=True)
        grad_low[h] = (probs[h].astype(wide) * (grad_probs[h] - delta)).astype(low)
        turned_query.append(mm(grad_low[h], keys[...], 1, 0))
        turned_keys.append(mm(query_t[h * 64 : (h + 1) * 64, :], grad_low[h], 1, 0))
    grad_query = jnp.where(lane < 64, turned_query[0], turned_query[1]) * scale
    grad_keys = (jnp.concatenate(turned_keys, axis=0) * scale).T
    grad_values = jnp.concatenate(turned_values, axis=0).T
    at = pl.multiple_of(step * 128, 128)
    for part, value in enumerate((grad_query, grad_keys, grad_values)):
        grad_project[part, :, pl.ds(at, 128)] = value.astype(low)

    @pl.when(step == steps - 1)
    def _():
        for part in range(3):
            if part == 2:
                await_bytes(stage.at[0], out_sems.at[0])
            stage[part % 2] = mm(normed_t[...], grad_project[part], 1, 0).astype(low)
            store_blocks(
                place,
                stage.at[part % 2],
                buffer,
                out_sems.at[part % 2],
                0,
                3 * side,
                0,
                part * side,
                side,
                side,
            )
        await_bytes(stage.at[1], out_sems.at[1])
        await_bytes(stage.at[0], out_sems.at[0])


def result_kernel(place, whole, active, middle, inside, vectors, result, w_down, total, sems):
    step = pl.program_id(0)
    steps = pl.num_programs(0)
    rows, width = middle.shape
    side = width // 128
    high = 4 * side
    per = CHUNK // 128
    first_down = 4 * side * side + side * high

    def fetch(index, slot):
        start_blocks(
            place, whole, w_down.at[slot], sems.at[slot], first_down, side, index * per, 0, per, side
        )

    @pl.when(step == 0)
    def _():
        total[...] = jnp.zeros_like(total)
        fetch(0, 0)
        fetch(1, 1)

    slot = lax.rem(step, 2)
    await_bytes(w_down.at[slot], sems.at[slot])
    total[...] += mm(active[...], w_down[slot], 1, 0)

    @pl.when(step + 2 < steps)
    def _():
        fetch(step + 2, slot)

    @pl.when(step == steps - 1)
    def _():
        def finish(t, carry):
            at = rows_of(t)
            result[at, :] = (
                middle[at, :] + inside[at, :] * (total[at, :] + vectors[11:12, :])
            ).astype(low)
            return carry

        lax.fori_loop(0, tiles(rows), finish, 0)


def input_kernel(
    place, whole, grad_project, patches, grad_middle, vectors, grad_input, sums, weight, grad_sum, sems
):
    rows, width = patches.shape
    side = width // 128
    for part in range(3):
        start_blocks(
            place, whole, weight.at[part], sems.at[part], 0, 3 * side, 0, part * side, side, side
        )
    for part in range(3):
        await_bytes(weight.at[part], sems.at[part])
    total = mm(grad_project[0], weight[0], 1, 1)
    total = total + mm(grad_project[1], weight[1], 1, 1)
    grad_sum[...] = total + mm(grad_project[2], weight[2], 1, 1)

    def finish(t, carry):
        at = rows_of(t)
        grad = grad_sum[at, :]
        normal, factor = normal_parts(patches[at, :].astype(wide))
        back = norm_back(grad, normal, factor, vectors[0:1, :])
        grad_input[at, :] = (grad_middle[at, :] + back).astype(low)
        gain, shift, bias_query, bias_value = carry
        return (
            gain + jnp.sum(grad * normal, axis=0, keepdims=True),
            shift + jnp.sum(grad, axis=0, keepdims=True),
            bias_query + jnp.sum(grad_project[0, at, :].astype(wide), axis=0, keepdims=True),
            bias_value + jnp.sum(grad_project[2, at, :].astype(wide), axis=0, keepdims=True),
        )

    empty = jnp.zeros((1, width), wide)
    found = lax.fori_loop(0, tiles(rows), finish, (empty, empty, empty, empty))
    for row in range(4):
        sums[row : row + 1, :] = found[row]
    sums[4:8, :] = jnp.zeros((4, width), wide)


VMEM_LIMIT = 60 * 1024 * 1024


def params(count=1):
    return pltpu.CompilerParams(
        dimension_semantics=("arbitrary",) * count, vmem_limit_bytes=VMEM_LIMIT
    )


def whole_spec():
    return pl.BlockSpec(memory_space=pl.ANY)


def full(shape):
    return pl.BlockSpec(shape, lambda *_: (0,) * len(shape))


def shards(
    sizes,
    patches,
    lengths,
    cotangent,
    owners,
    master,
    first_moment,
    second_moment,
    left_basis,
    right_basis,
    vectors,
    vector_first,
    vector_second,
):
    dp, fsdp = sizes
    devices = dp * fsdp
    rows, width = patches.shape
    hidden = 4 * width
    side = width // 128
    pairs = width // 128
    held, size = master.shape[0], master.shape[1]
    slots = held * devices
    shape = jax.ShapeDtypeStruct
    me = lax.axis_index(AXES)
    order = ring_order(dp, fsdp)
    groups = None if order is None else [order]

    def gather(value):
        return lax.all_gather(value, AXES, axis=0, tiled=True, axis_index_groups=groups)

    def scatter(value):
        return lax.psum_scatter(
            value, AXES, scatter_dimension=0, tiled=True, axis_index_groups=groups
        )

    def everywhere(value):
        step = 1
        while step < devices:
            value = value + lax.ppermute(value, AXES, [(d, d ^ step) for d in range(devices)])
            step *= 2
        return value

    whole = gather(master.astype(low))
    if order is None:
        place = owners
    else:
        rank = [0] * devices
        for spot, device in enumerate(order):
            rank[device] = spot
        device = owners // held
        spot = jnp.sum(
            jnp.where(
                device[:, None] == jnp.arange(devices, dtype=jnp.int32)[None, :],
                jnp.array(rank, jnp.int32)[None, :],
                0,
            ),
            axis=1,
        )
        place = spot * held + owners % held
    mine = me * held + jnp.arange(held, dtype=jnp.int32)
    named = jnp.any(mine[:, None] == owners[None, :], axis=1)

    counts = lengths[0]
    ends = jnp.cumsum(counts)
    places = jnp.arange(rows, dtype=jnp.int32)[:, None]
    image = jnp.sum((places >= ends[None, :]).astype(jnp.int32), axis=1, keepdims=True)
    within = places < ends[-1]
    image = jnp.where(within, image, 4)
    inside = within.astype(wide)
    lanes = jnp.arange(128, dtype=jnp.int32)[None, :]
    image_keys = (lanes == image).astype(low)
    image_query = jnp.where((lanes != image) & (lanes < 5), -far, 0.0).astype(low)

    normed, normed_t, grad_two, bias_down = pl.pallas_call(
        ready_kernel,
        out_shape=[
            shape((rows, width), low),
            shape((width, rows), low),
            shape((rows, width), low),
            shape((1, width), wide),
        ],
        compiler_params=pltpu.CompilerParams(vmem_limit_bytes=VMEM_LIMIT),
        name="ready",
    )(patches, cotangent, inside, vectors)

    project = pl.pallas_call(
        qkv_kernel,
        grid_spec=pltpu.PrefetchScalarGridSpec(
            num_scalar_prefetch=1,
            grid=(1,),
            in_specs=[whole_spec(), full((rows, width)), full((12, width))],
            out_specs=full((rows, 3 * width)),
            scratch_shapes=[
                pltpu.VMEM((3, width, width), low),
                pltpu.SemaphoreType.DMA((3,)),
            ],
        ),
        out_shape=shape((rows, 3 * width), low),
        compiler_params=params(),
        name="qkv",
    )(place, whole, normed, vectors)

    def column(offset):
        return pl.BlockSpec((rows, 128), lambda j, *_: (0, j + offset))

    mixed, probs = pl.pallas_call(
        attend_kernel,
        grid=(pairs,),
        in_specs=[
            column(0),
            column(pairs),
            column(2 * pairs),
            full((rows, 128)),
            full((rows, 128)),
        ],
        out_specs=[column(0), pl.BlockSpec((2, rows, rows), lambda j: (j, 0, 0))],
        out_shape=[shape((rows, width), low), shape((HEADS, rows, rows), low)],
        scratch_shapes=[pltpu.VMEM((2, rows, rows), wide)],
        compiler_params=params(),
        name="attend",
    )(project, project, project, image_query, image_keys)

    steps = hidden // CHUNK
    middle, active, grad_middle, grad_mixed, sums_two, sums_up, buffer = pl.pallas_call(
        feed_kernel,
        grid_spec=pltpu.PrefetchScalarGridSpec(
            num_scalar_prefetch=1,
            grid=(steps,),
            in_specs=[
                whole_spec(),
                full((rows, width)),
                full((rows, width)),
                full((rows, width)),
                full((rows, width)),
                full((rows, 1)),
                full((12, width)),
                pl.BlockSpec((1, 1, CHUNK), lambda c, *_: (c, 0, 0)),
            ],
            out_specs=[
                full((rows, width)),
                pl.BlockSpec((rows, CHUNK), lambda c, *_: (0, c)),
                full((rows, width)),
                full((rows, width)),
                full((8, width)),
                pl.BlockSpec((1, 1, CHUNK), lambda c, *_: (c, 0, 0)),
                whole_spec(),
            ],
            scratch_shapes=[
                pltpu.VMEM((width, width), low),
                pltpu.VMEM((2, width, CHUNK), low),
                pltpu.VMEM((2, CHUNK, width), low),
                pltpu.VMEM((rows, width), wide),
                pltpu.VMEM((rows, 1), wide),
                pltpu.VMEM((rows, width), low),
                pltpu.VMEM((width, rows), low),
                pltpu.VMEM((rows, width), wide),
                pltpu.VMEM((rows, width), wide),
                pltpu.VMEM((2, width, CHUNK), low),
                pltpu.VMEM((2, CHUNK, width), low),
                pltpu.VMEM((width, width), low),
                pltpu.VMEM((rows, CHUNK), low),
                pltpu.SemaphoreType.DMA((5,)),
                pltpu.SemaphoreType.DMA((5,)),
            ],
        ),
        out_shape=[
            shape((rows, width), wide),
            shape((rows, hidden), low),
            shape((rows, width), wide),
            shape((rows, width), low),
            shape((8, width), wide),
            shape((steps, 1, CHUNK), wide),
            shape((slots, size, size), low),
        ],
        compiler_params=params(),
        name="feed",
    )(
        place,
        whole,
        patches,
        cotangent,
        grad_two,
        mixed,
        inside,
        vectors,
        vectors[7:11].reshape(steps, 1, CHUNK),
    )

    grad_project, buffer = pl.pallas_call(
        back_kernel,
        grid_spec=pltpu.PrefetchScalarGridSpec(
            num_scalar_prefetch=1,
            grid=(pairs,),
            in_specs=[
                whole_spec(),
                column(0),
                column(pairs),
                column(2 * pairs),
                pl.BlockSpec((2, rows, rows), lambda j, *_: (j, 0, 0)),
                column(0),
                column(0),
                full((width, rows)),
            ],
            out_specs=[full((3, rows, width)), whole_spec()],
            scratch_shapes=[
                pltpu.VMEM((2, rows, rows), low),
                pltpu.VMEM((2, width, width), low),
                pltpu.SemaphoreType.DMA((2,)),
            ],
        ),
        out_shape=[
            shape((3, rows, width), low),
            shape((slots, size, size), low),
        ],
        input_output_aliases={1: 1},
        compiler_params=params(),
        name="back",
    )(
        place,
        buffer,
        project,
        project,
        project,
        probs,
        grad_mixed,
        mixed,
        normed_t,
    )
    owned = scatter(buffer)

    grad_input, sums_one = pl.pallas_call(
        input_kernel,
        grid_spec=pltpu.PrefetchScalarGridSpec(
            num_scalar_prefetch=1,
            grid=(1,),
            in_specs=[
                whole_spec(),
                full((3, rows, width)),
                full((rows, width)),
                full((rows, width)),
                full((12, width)),
            ],
            out_specs=[full((rows, width)), full((8, width))],
            scratch_shapes=[
                pltpu.VMEM((3, width, width), low),
                pltpu.VMEM((rows, width), wide),
                pltpu.SemaphoreType.DMA((3,)),
            ],
        ),
        out_shape=[shape((rows, width), low), shape((8, width), wide)],
        compiler_params=params(),
        name="input",
    )(place, whole, grad_project, patches, grad_middle, vectors)
    result = pl.pallas_call(
        result_kernel,
        grid_spec=pltpu.PrefetchScalarGridSpec(
            num_scalar_prefetch=1,
            grid=(steps,),
            in_specs=[
                whole_spec(),
                pl.BlockSpec((rows, CHUNK), lambda c, *_: (0, c)),
                full((rows, width)),
                full((rows, 1)),
                full((12, width)),
            ],
            out_specs=full((rows, width)),
            scratch_shapes=[
                pltpu.VMEM((2, CHUNK, width), low),
                pltpu.VMEM((rows, width), wide),
                pltpu.SemaphoreType.DMA((2,)),
            ],
        ),
        out_shape=shape((rows, width), low),
        compiler_params=params(),
        name="result",
    )(place, whole, active, middle, inside, vectors)
    vector_grad = jnp.concatenate(
        [sums_one[0:4], sums_two[0:3], sums_up.reshape(4, width), bias_down], axis=0
    )
    vector_sum = everywhere(vector_grad)

    owned, vector_sum, result = lax.optimization_barrier((owned, vector_sum, result))

    owned = jnp.where(named[:, None, None], owned.astype(wide), 0.0)
    squares = jnp.broadcast_to(jnp.sum(owned * owned), (devices, 128))
    total_blocks = jnp.sum(lax.all_to_all(squares, AXES, 0, 0, tiled=True)[:, 0])
    clip_norm = jnp.sqrt(total_blocks + jnp.sum(vector_sum * vector_sum))
    count = owners.shape[0] * size * size + vectors.shape[0] * width
    factor = jnp.minimum(1.0, 0.5 * math.sqrt(count) / clip_norm)
    turned = jnp.einsum("sji,sjk->sik", left_basis, owned, precision=highest)
    rotated = factor * jnp.einsum("sik,skl->sil", turned, right_basis, precision=highest)
    new_first = beta * first_moment + (1.0 - beta) * rotated
    new_second = beta * second_moment + (1.0 - beta) * rotated * rotated
    correction = 1.0 - beta**STEP
    direction = new_first / correction / (jnp.sqrt(new_second / correction) + adam_eps)
    back_turn = jnp.einsum("sij,sjk->sik", left_basis, direction, precision=highest)
    update = jnp.einsum("sik,slk->sil", back_turn, right_basis, precision=highest)
    new_master = master - rate_matrix * (update + decay_weight * master)
    vector_clip = factor * vector_sum
    new_vector_first = beta * vector_first + (1.0 - beta) * vector_clip
    new_vector_second = beta * vector_second + (1.0 - beta) * vector_clip * vector_clip
    vector_step = (
        new_vector_first / correction / (jnp.sqrt(new_vector_second / correction) + adam_eps)
    )
    new_vectors = vectors - rate_vector * vector_step
    return (
        result,
        grad_input,
        clip_norm,
        new_master,
        new_first,
        new_second,
        new_vectors,
        new_vector_first,
        new_vector_second,
    )


def solution(mesh):
    sizes = (mesh.shape["dp"], mesh.shape["fsdp"])
    rows = P(AXES, None)
    blocks = P(AXES, None, None)
    return jax.shard_map(
        functools.partial(shards, sizes),
        mesh=mesh,
        in_specs=(rows, rows, rows, P(), blocks, blocks, blocks, blocks, blocks, P(), P(), P()),
        out_specs=(rows, rows, P(), blocks, blocks, blocks, P(), P(), P()),
        check_vma=False,
    )
```

```python
import functools
import math

import jax
import jax.numpy as jnp
from jax import lax
from jax.experimental import pallas as pl
from jax.experimental.pallas import tpu as pltpu
from jax.sharding import PartitionSpec as P

HEADS = 12
STEP = 2
AXES = ("dp", "fsdp")

norm_eps = 1e-06
adam_eps = 1e-08
beta = 0.5
rate_matrix = 0.03
rate_vector = 0.05
decay_weight = 0.01
high = lax.Precision.HIGH
far = 2.0**30
low = jnp.bfloat16
wide = jnp.float32

CHUNK = 512


def ring_order(dp, fsdp):
    if (dp, fsdp) != (8, 4):
        return None
    order = []
    for turn, (x, y) in enumerate(((0, 0), (1, 0), (1, 1), (0, 1))):
        places = range(4) if turn % 2 == 0 else range(3, -1, -1)
        for z in places:
            order += [(z * 2 + x) * 4 + y * 2 + core for core in (0, 1)]
    return order


def mm(a, b, ca, cb):
    return lax.dot_general(a, b, (((ca,), (cb,)), ((), ())), preferred_element_type=wide)


def normal_parts(values):
    center = values - jnp.mean(values, axis=-1, keepdims=True)
    factor = lax.rsqrt(jnp.mean(center * center, axis=-1, keepdims=True) + norm_eps)
    return center * factor, factor


def norm_back(grad, normal, factor, gain):
    inner = grad * gain
    return factor * (
        inner
        - jnp.mean(inner, axis=-1, keepdims=True)
        - normal * jnp.mean(inner * normal, axis=-1, keepdims=True)
    )


def start_blocks(place, whole, target, sem, first, across, row0, col0, height, breadth):
    def one(r, carry):
        at = first + (row0 + r) * across + col0
        down = pl.ds(pl.multiple_of(r * 128, 128), 128)
        for c in range(breadth):
            pltpu.make_async_copy(
                whole.at[place[at + c]], target.at[down, pl.ds(c * 128, 128)], sem
            ).start()
        return carry

    lax.fori_loop(0, height, one, 0)


def store_blocks(place, source, buffer, sem, first, across, row0, col0, height, breadth):
    def one(r, carry):
        at = first + (row0 + r) * across + col0
        down = pl.ds(pl.multiple_of(r * 128, 128), 128)
        for c in range(breadth):
            pltpu.make_async_copy(
                source.at[down, pl.ds(c * 128, 128)], buffer.at[place[at + c]], sem
            ).start()
        return carry

    lax.fori_loop(0, height, one, 0)


def await_bytes(ref, sem):
    pltpu.make_async_copy(ref, ref, sem).wait()


TILE = 112


def tiles(rows):
    return rows // TILE


def rows_of(t):
    return pl.ds(pl.multiple_of(t * TILE, 16), TILE)


def ready_kernel(patches, cotangent, inside, vectors, normed, normed_t, grad_two, bias_down):
    rows, width = patches.shape

    def norm(t, total):
        at = rows_of(t)
        normal, _ = normal_parts(patches[at, :].astype(wide))
        normed[at, :] = (normal * vectors[0:1, :] + vectors[1:2, :]).astype(low)
        two = (inside[at, :] * cotangent[at, :].astype(wide)).astype(low)
        grad_two[at, :] = two
        return total + jnp.sum(two.astype(wide), axis=0, keepdims=True)

    bias_down[...] = lax.fori_loop(0, tiles(rows), norm, jnp.zeros((1, width), wide))
    normed_t[...] = normed[...].T


def qkv_kernel(place, whole, normed, vectors, project, weight, sems):
    rows, width = normed.shape
    side = width // 128
    for part in range(3):
        start_blocks(
            place, whole, weight.at[part], sems.at[part], 0, 3 * side, 0, part * side, side, side
        )
    for part in range(3):
        await_bytes(weight.at[part], sems.at[part])
        out = mm(normed[...], weight[part], 1, 0)
        if part == 0:
            out = out + vectors[2:3, :]
        if part == 2:
            out = out + vectors[3:4, :]
        project[:, part * width : (part + 1) * width] = out.astype(low)


def attend_kernel(query, keys, values, image_query, image_keys, mixed, probs, scores):
    rows = query.shape[0]
    lane = lax.broadcasted_iota(jnp.int32, (rows, 128), 1)
    wide_keys = jnp.concatenate([keys[...], image_keys[...]], axis=1)
    scaled = query[...] * jnp.asarray(0.125, low)
    outs = []
    for h in range(2):
        part = jnp.where(lane // 64 == h, scaled, jnp.zeros_like(scaled))
        scores[h] = mm(jnp.concatenate([part, image_query[...]], axis=1), wide_keys, 1, 1)
    for h in range(2):
        for t in range(tiles(rows)):
            at = slice(t * TILE, (t + 1) * TILE)
            s = scores[h, at, :]
            e = jnp.exp(s - jnp.max(s, axis=-1, keepdims=True))
            total = jnp.sum(e, axis=-1, keepdims=True)
            probs[h, at, :] = (e * (1.0 / total)).astype(low)
        outs.append(mm(probs[h], values[...], 1, 0))
    mixed[...] = jnp.where(lane < 64, outs[0], outs[1]).astype(low)


def feed_kernel(
    place,
    whole,
    patches,
    cotangent,
    grad_two,
    mixed,
    inside,
    vectors,
    bias_up,
    middle,
    active,
    grad_middle,
    grad_mixed,
    sums,
    sums_up,
    buffer,
    w_out,
    w_up,
    w_down,
    normal,
    factor,
    second,
    second_t,
    out_sum,
    back_sum,
    stage_up,
    stage_down,
    stage_out,
    grad_pre,
    sems,
    out_sems,
):
    step = pl.program_id(0)
    steps = pl.num_programs(0)
    rows, width = patches.shape
    side = width // 128
    hidden = 4 * width
    high = hidden // 128
    per = CHUNK // 128
    first_out = 3 * side * side
    first_up = 4 * side * side
    first_down = first_up + side * high

    def fetch(index, slot):
        start_blocks(
            place, whole, w_up.at[slot], sems.at[slot], first_up, high, 0, index * per, side, per
        )
        start_blocks(
            place, whole, w_down.at[slot], sems.at[2 + slot], first_down, side, index * per, 0, per, side
        )

    @pl.when(step == 0)
    def _():
        start_blocks(place, whole, w_out, sems.at[4], first_out, side, 0, 0, side, side)
        fetch(0, 0)
        fetch(1, 1)
        await_bytes(w_out, sems.at[4])
        out_sum[...] = mm(mixed[...], w_out[...], 1, 0)

        def norm(t, carry):
            at = rows_of(t)
            keep = inside[at, :]
            mid = patches[at, :].astype(wide) + keep * (out_sum[at, :] + vectors[4:5, :])
            middle[at, :] = mid
            scaled, q = normal_parts(mid)
            normal[at, :] = scaled
            factor[at, :] = q
            second[at, :] = (scaled * vectors[5:6, :] + vectors[6:7, :]).astype(low)
            return carry

        lax.fori_loop(0, tiles(rows), norm, 0)
        second_t[...] = second[...].T
        back_sum[...] = jnp.zeros_like(back_sum)

    slot = lax.rem(step, 2)
    await_bytes(w_up.at[slot], sems.at[slot])
    await_bytes(w_down.at[slot], sems.at[2 + slot])

    @pl.when(step >= 2)
    def _():
        await_bytes(stage_up.at[slot], out_sems.at[slot])
        await_bytes(stage_down.at[slot], out_sems.at[2 + slot])

    parts = [slice(h * (CHUNK // 2), (h + 1) * (CHUNK // 2)) for h in range(2)]
    pres = [mm(second[...], w_up[slot, :, p], 1, 0) + bias_up[0, :, p] for p in parts]
    grads = [mm(grad_two[...], w_down[slot, p, :], 1, 1) for p in parts]
    for p, pre, grad in zip(parts, pres, grads):
        half = 0.5 * (1.0 + lax.erf(pre * math.sqrt(0.5)))
        active[:, p] = (pre * half).astype(low)
        slope = half + pre * (jnp.exp(-0.5 * pre * pre) * (1.0 / math.sqrt(2.0 * math.pi)))
        back = (grad * slope).astype(low)
        grad_pre[:, p] = back
        sums_up[0, :, p] = jnp.sum(back.astype(wide), axis=0, keepdims=True)
        stage_up[slot, :, p] = mm(second_t[...], grad_pre[:, p], 1, 0).astype(low)
        stage_down[slot, p, :] = mm(active[:, p], grad_two[...], 0, 0).astype(low)
    back_sum[...] += mm(grad_pre[...], w_up[slot], 1, 1)
    store_blocks(
        place, stage_up.at[slot], buffer, out_sems.at[slot], first_up, high, 0, step * per, side, per
    )
    store_blocks(
        place, stage_down.at[slot], buffer, out_sems.at[2 + slot], first_down, side, step * per, 0, per, side
    )

    @pl.when(step + 2 < steps)
    def _():
        fetch(step + 2, slot)

    @pl.when(step == steps - 1)
    def _():
        def finish(t, total):
            at = rows_of(t)
            keep = inside[at, :]
            grad = back_sum[at, :]
            scaled = normal[at, :]
            mid = cotangent[at, :].astype(wide) + norm_back(
                grad, scaled, factor[at, :], vectors[5:6, :]
            )
            grad_middle[at, :] = mid
            one = (keep * mid).astype(low)
            second[at, :] = one
            gain, shift, bias = total
            return (
                gain + jnp.sum(grad * scaled, axis=0, keepdims=True),
                shift + jnp.sum(grad, axis=0, keepdims=True),
                bias + jnp.sum(one.astype(wide), axis=0, keepdims=True),
            )

        empty = jnp.zeros((1, width), wide)
        gain, shift, bias = lax.fori_loop(0, tiles(rows), finish, (empty, empty, empty))
        sums[0:1, :] = bias
        sums[1:2, :] = gain
        sums[2:3, :] = shift
        sums[3:8, :] = jnp.zeros((5, width), wide)
        stage_out[...] = mm(mixed[...], second[...], 0, 0).astype(low)
        store_blocks(place, stage_out, buffer, out_sems.at[4], first_out, side, 0, 0, side, side)
        grad_mixed[...] = mm(second[...], w_out[...], 1, 1).astype(low)
        for other in range(2):
            await_bytes(stage_up.at[other], out_sems.at[other])
            await_bytes(stage_down.at[other], out_sems.at[2 + other])
        await_bytes(stage_out, out_sems.at[4])


def back_kernel(
    place,
    held,
    query,
    keys,
    values,
    probs,
    grad_mixed,
    mixed,
    normed_t,
    grad_project,
    buffer,
    grad_low,
    stage,
    out_sems,
):
    del held
    step = pl.program_id(0)
    steps = pl.num_programs(0)
    width, rows = normed_t.shape
    side = width // 128
    scale = 0.125
    lane = lax.broadcasted_iota(jnp.int32, (rows, 128), 1)
    grad = grad_mixed[...]
    grad_t = grad.T
    query_t = query[...].T
    outer = grad.astype(wide) * mixed[...].astype(wide)
    mine = [lane // 64 == h for h in range(2)]
    grad_probs = [
        mm(jnp.where(mine[h], grad, jnp.zeros_like(grad)), values[...], 1, 1) for h in range(2)
    ]
    turned_values = [mm(grad_t[h * 64 : (h + 1) * 64, :], probs[h], 1, 0) for h in range(2)]
    turned_query = []
    turned_keys = []
    for h in range(2):
        delta = jnp.sum(jnp.where(mine[h], outer, 0.0), axis=-1, keepdims=True)
        grad_low[h] = (probs[h].astype(wide) * (grad_probs[h] - delta)).astype(low)
        turned_query.append(mm(grad_low[h], keys[...], 1, 0))
        turned_keys.append(mm(query_t[h * 64 : (h + 1) * 64, :], grad_low[h], 1, 0))
    grad_query = jnp.where(lane < 64, turned_query[0], turned_query[1]) * scale
    grad_keys = (jnp.concatenate(turned_keys, axis=0) * scale).T
    grad_values = jnp.concatenate(turned_values, axis=0).T
    at = pl.multiple_of(step * 128, 128)
    for part, value in enumerate((grad_query, grad_keys, grad_values)):
        grad_project[part, :, pl.ds(at, 128)] = value.astype(low)

    @pl.when(step == steps - 1)
    def _():
        for part in range(3):
            if part == 2:
                await_bytes(stage.at[0], out_sems.at[0])
            stage[part % 2] = mm(normed_t[...], grad_project[part], 1, 0).astype(low)
            store_blocks(
                place,
                stage.at[part % 2],
                buffer,
                out_sems.at[part % 2],
                0,
                3 * side,
                0,
                part * side,
                side,
                side,
            )
        await_bytes(stage.at[1], out_sems.at[1])
        await_bytes(stage.at[0], out_sems.at[0])


def result_kernel(place, whole, active, middle, inside, vectors, result, w_down, total, sems):
    step = pl.program_id(0)
    steps = pl.num_programs(0)
    rows, width = middle.shape
    side = width // 128
    high = 4 * side
    per = CHUNK // 128
    first_down = 4 * side * side + side * high

    def fetch(index, slot):
        start_blocks(
            place, whole, w_down.at[slot], sems.at[slot], first_down, side, index * per, 0, per, side
        )

    @pl.when(step == 0)
    def _():
        total[...] = jnp.zeros_like(total)
        fetch(0, 0)
        fetch(1, 1)

    slot = lax.rem(step, 2)
    await_bytes(w_down.at[slot], sems.at[slot])
    total[...] += mm(active[...], w_down[slot], 1, 0)

    @pl.when(step + 2 < steps)
    def _():
        fetch(step + 2, slot)

    @pl.when(step == steps - 1)
    def _():
        def finish(t, carry):
            at = rows_of(t)
            result[at, :] = (
                middle[at, :] + inside[at, :] * (total[at, :] + vectors[11:12, :])
            ).astype(low)
            return carry

        lax.fori_loop(0, tiles(rows), finish, 0)


def input_kernel(
    place, whole, grad_project, patches, grad_middle, vectors, grad_input, sums, weight, grad_sum, sems
):
    rows, width = patches.shape
    side = width // 128
    for part in range(3):
        start_blocks(
            place, whole, weight.at[part], sems.at[part], 0, 3 * side, 0, part * side, side, side
        )
    for part in range(3):
        await_bytes(weight.at[part], sems.at[part])
    total = mm(grad_project[0], weight[0], 1, 1)
    total = total + mm(grad_project[1], weight[1], 1, 1)
    grad_sum[...] = total + mm(grad_project[2], weight[2], 1, 1)

    def finish(t, carry):
        at = rows_of(t)
        grad = grad_sum[at, :]
        normal, factor = normal_parts(patches[at, :].astype(wide))
        back = norm_back(grad, normal, factor, vectors[0:1, :])
        grad_input[at, :] = (grad_middle[at, :] + back).astype(low)
        gain, shift, bias_query, bias_value = carry
        return (
            gain + jnp.sum(grad * normal, axis=0, keepdims=True),
            shift + jnp.sum(grad, axis=0, keepdims=True),
            bias_query + jnp.sum(grad_project[0, at, :].astype(wide), axis=0, keepdims=True),
            bias_value + jnp.sum(grad_project[2, at, :].astype(wide), axis=0, keepdims=True),
        )

    empty = jnp.zeros((1, width), wide)
    found = lax.fori_loop(0, tiles(rows), finish, (empty, empty, empty, empty))
    for row in range(4):
        sums[row : row + 1, :] = found[row]
    sums[4:8, :] = jnp.zeros((4, width), wide)


def squares_kernel(named, grads, spread):
    total = jnp.zeros((128, 128), wide)
    for s in range(grads.shape[0]):
        block = jnp.where(named[s] > 0, grads[s].astype(wide), 0.0)
        total = total + block * block
    spread[...] = jnp.broadcast_to(jnp.sum(total), spread.shape)


VMEM_LIMIT = 60 * 1024 * 1024


def params(count=1):
    return pltpu.CompilerParams(
        dimension_semantics=("arbitrary",) * count, vmem_limit_bytes=VMEM_LIMIT
    )


def whole_spec():
    return pl.BlockSpec(memory_space=pl.ANY)


def full(shape):
    return pl.BlockSpec(shape, lambda *_: (0,) * len(shape))


def shards(
    sizes,
    patches,
    lengths,
    cotangent,
    owners,
    master,
    first_moment,
    second_moment,
    left_basis,
    right_basis,
    vectors,
    vector_first,
    vector_second,
):
    dp, fsdp = sizes
    devices = dp * fsdp
    rows, width = patches.shape
    hidden = 4 * width
    side = width // 128
    pairs = width // 128
    held, size = master.shape[0], master.shape[1]
    slots = held * devices
    shape = jax.ShapeDtypeStruct
    me = lax.axis_index(AXES)
    order = ring_order(dp, fsdp)
    groups = None if order is None else [order]

    def gather(value):
        return lax.all_gather(value, AXES, axis=0, tiled=True, axis_index_groups=groups)

    def scatter(value):
        return lax.psum_scatter(
            value, AXES, scatter_dimension=0, tiled=True, axis_index_groups=groups
        )

    def everywhere(value):
        step = 1
        while step < devices:
            value = value + lax.ppermute(value, AXES, [(d, d ^ step) for d in range(devices)])
            step *= 2
        return value

    whole = gather(master.astype(low))
    if order is None:
        place = owners
    else:
        rank = [0] * devices
        for spot, device in enumerate(order):
            rank[device] = spot
        device = owners // held
        spot = jnp.sum(
            jnp.where(
                device[:, None] == jnp.arange(devices, dtype=jnp.int32)[None, :],
                jnp.array(rank, jnp.int32)[None, :],
                0,
            ),
            axis=1,
        )
        place = spot * held + owners % held
    mine = me * held + jnp.arange(held, dtype=jnp.int32)
    named = jnp.any(mine[:, None] == owners[None, :], axis=1)

    counts = lengths[0]
    ends = jnp.cumsum(counts)
    places = jnp.arange(rows, dtype=jnp.int32)[:, None]
    image = jnp.sum((places >= ends[None, :]).astype(jnp.int32), axis=1, keepdims=True)
    within = places < ends[-1]
    image = jnp.where(within, image, 4)
    inside = within.astype(wide)
    lanes = jnp.arange(128, dtype=jnp.int32)[None, :]
    image_keys = (lanes == image).astype(low)
    image_query = jnp.where((lanes != image) & (lanes < 5), -far, 0.0).astype(low)

    normed, normed_t, grad_two, bias_down = pl.pallas_call(
        ready_kernel,
        out_shape=[
            shape((rows, width), low),
            shape((width, rows), low),
            shape((rows, width), low),
            shape((1, width), wide),
        ],
        compiler_params=pltpu.CompilerParams(vmem_limit_bytes=VMEM_LIMIT),
        name="ready",
    )(patches, cotangent, inside, vectors)

    project = pl.pallas_call(
        qkv_kernel,
        grid_spec=pltpu.PrefetchScalarGridSpec(
            num_scalar_prefetch=1,
            grid=(1,),
            in_specs=[whole_spec(), full((rows, width)), full((12, width))],
            out_specs=full((rows, 3 * width)),
            scratch_shapes=[
                pltpu.VMEM((3, width, width), low),
                pltpu.SemaphoreType.DMA((3,)),
            ],
        ),
        out_shape=shape((rows, 3 * width), low),
        compiler_params=params(),
        name="qkv",
    )(place, whole, normed, vectors)

    def column(offset):
        return pl.BlockSpec((rows, 128), lambda j, *_: (0, j + offset))

    mixed, probs = pl.pallas_call(
        attend_kernel,
        grid=(pairs,),
        in_specs=[
            column(0),
            column(pairs),
            column(2 * pairs),
            full((rows, 128)),
            full((rows, 128)),
        ],
        out_specs=[column(0), pl.BlockSpec((2, rows, rows), lambda j: (j, 0, 0))],
        out_shape=[shape((rows, width), low), shape((HEADS, rows, rows), low)],
        scratch_shapes=[pltpu.VMEM((2, rows, rows), wide)],
        compiler_params=params(),
        name="attend",
    )(project, project, project, image_query, image_keys)

    steps = hidden // CHUNK
    middle, active, grad_middle, grad_mixed, sums_two, sums_up, buffer = pl.pallas_call(
        feed_kernel,
        grid_spec=pltpu.PrefetchScalarGridSpec(
            num_scalar_prefetch=1,
            grid=(steps,),
            in_specs=[
                whole_spec(),
                full((rows, width)),
                full((rows, width)),
                full((rows, width)),
                full((rows, width)),
                full((rows, 1)),
                full((12, width)),
                pl.BlockSpec((1, 1, CHUNK), lambda c, *_: (c, 0, 0)),
            ],
            out_specs=[
                full((rows, width)),
                pl.BlockSpec((rows, CHUNK), lambda c, *_: (0, c)),
                full((rows, width)),
                full((rows, width)),
                full((8, width)),
                pl.BlockSpec((1, 1, CHUNK), lambda c, *_: (c, 0, 0)),
                whole_spec(),
            ],
            scratch_shapes=[
                pltpu.VMEM((width, width), low),
                pltpu.VMEM((2, width, CHUNK), low),
                pltpu.VMEM((2, CHUNK, width), low),
                pltpu.VMEM((rows, width), wide),
                pltpu.VMEM((rows, 1), wide),
                pltpu.VMEM((rows, width), low),
                pltpu.VMEM((width, rows), low),
                pltpu.VMEM((rows, width), wide),
                pltpu.VMEM((rows, width), wide),
                pltpu.VMEM((2, width, CHUNK), low),
                pltpu.VMEM((2, CHUNK, width), low),
                pltpu.VMEM((width, width), low),
                pltpu.VMEM((rows, CHUNK), low),
                pltpu.SemaphoreType.DMA((5,)),
                pltpu.SemaphoreType.DMA((5,)),
            ],
        ),
        out_shape=[
            shape((rows, width), wide),
            shape((rows, hidden), low),
            shape((rows, width), wide),
            shape((rows, width), low),
            shape((8, width), wide),
            shape((steps, 1, CHUNK), wide),
            shape((slots, size, size), low),
        ],
        compiler_params=params(),
        name="feed",
    )(
        place,
        whole,
        patches,
        cotangent,
        grad_two,
        mixed,
        inside,
        vectors,
        vectors[7:11].reshape(steps, 1, CHUNK),
    )

    grad_project, buffer = pl.pallas_call(
        back_kernel,
        grid_spec=pltpu.PrefetchScalarGridSpec(
            num_scalar_prefetch=1,
            grid=(pairs,),
            in_specs=[
                whole_spec(),
                column(0),
                column(pairs),
                column(2 * pairs),
                pl.BlockSpec((2, rows, rows), lambda j, *_: (j, 0, 0)),
                column(0),
                column(0),
                full((width, rows)),
            ],
            out_specs=[full((3, rows, width)), whole_spec()],
            scratch_shapes=[
                pltpu.VMEM((2, rows, rows), low),
                pltpu.VMEM((2, width, width), low),
                pltpu.SemaphoreType.DMA((2,)),
            ],
        ),
        out_shape=[
            shape((3, rows, width), low),
            shape((slots, size, size), low),
        ],
        input_output_aliases={1: 1},
        compiler_params=params(),
        name="back",
    )(
        place,
        buffer,
        project,
        project,
        project,
        probs,
        grad_mixed,
        mixed,
        normed_t,
    )
    owned = scatter(buffer)

    grad_input, sums_one = pl.pallas_call(
        input_kernel,
        grid_spec=pltpu.PrefetchScalarGridSpec(
            num_scalar_prefetch=1,
            grid=(1,),
            in_specs=[
                whole_spec(),
                full((3, rows, width)),
                full((rows, width)),
                full((rows, width)),
                full((12, width)),
            ],
            out_specs=[full((rows, width)), full((8, width))],
            scratch_shapes=[
                pltpu.VMEM((3, width, width), low),
                pltpu.VMEM((rows, width), wide),
                pltpu.SemaphoreType.DMA((3,)),
            ],
        ),
        out_shape=[shape((rows, width), low), shape((8, width), wide)],
        compiler_params=params(),
        name="input",
    )(place, whole, grad_project, patches, grad_middle, vectors)
    result = pl.pallas_call(
        result_kernel,
        grid_spec=pltpu.PrefetchScalarGridSpec(
            num_scalar_prefetch=1,
            grid=(steps,),
            in_specs=[
                whole_spec(),
                pl.BlockSpec((rows, CHUNK), lambda c, *_: (0, c)),
                full((rows, width)),
                full((rows, 1)),
                full((12, width)),
            ],
            out_specs=full((rows, width)),
            scratch_shapes=[
                pltpu.VMEM((2, CHUNK, width), low),
                pltpu.VMEM((rows, width), wide),
                pltpu.SemaphoreType.DMA((2,)),
            ],
        ),
        out_shape=shape((rows, width), low),
        compiler_params=params(),
        name="result",
    )(place, whole, active, middle, inside, vectors)
    vector_grad = jnp.concatenate(
        [sums_one[0:4], sums_two[0:3], sums_up.reshape(4, width), bias_down], axis=0
    )
    vector_sum = everywhere(vector_grad)

    owned, vector_sum, result = lax.optimization_barrier((owned, vector_sum, result))

    received = owned
    owned = jnp.where(named[:, None, None], owned.astype(wide), 0.0)
    squares = pl.pallas_call(
        squares_kernel,
        in_specs=[pl.BlockSpec(memory_space=pltpu.SMEM), full((held, size, size))],
        out_specs=full((devices, 128)),
        out_shape=shape((devices, 128), wide),
        grid=(),
        name="squares",
    )(named.astype(jnp.int32), received)
    total_blocks = jnp.sum(lax.all_to_all(squares, AXES, 0, 0, tiled=True)[:, 0])
    clip_norm = jnp.sqrt(total_blocks + jnp.sum(vector_sum * vector_sum))
    count = owners.shape[0] * size * size + vectors.shape[0] * width
    factor = jnp.minimum(1.0, 0.5 * math.sqrt(count) / clip_norm)
    turned = jnp.einsum("sji,sjk->sik", left_basis, owned, precision=high)
    rotated = factor * jnp.einsum("sik,skl->sil", turned, right_basis, precision=high)
    new_first = beta * first_moment + (1.0 - beta) * rotated
    new_second = beta * second_moment + (1.0 - beta) * rotated * rotated
    correction = 1.0 - beta**STEP
    direction = new_first / correction / (jnp.sqrt(new_second / correction) + adam_eps)
    back_turn = jnp.einsum("sij,sjk->sik", left_basis, direction, precision=high)
    update = jnp.einsum("sik,slk->sil", back_turn, right_basis, precision=high)
    new_master = master - rate_matrix * (update + decay_weight * master)
    vector_clip = factor * vector_sum
    new_vector_first = beta * vector_first + (1.0 - beta) * vector_clip
    new_vector_second = beta * vector_second + (1.0 - beta) * vector_clip * vector_clip
    vector_step = (
        new_vector_first / correction / (jnp.sqrt(new_vector_second / correction) + adam_eps)
    )
    new_vectors = vectors - rate_vector * vector_step
    return (
        result,
        grad_input,
        clip_norm,
        new_master,
        new_first,
        new_second,
        new_vectors,
        new_vector_first,
        new_vector_second,
    )


def solution(mesh):
    sizes = (mesh.shape["dp"], mesh.shape["fsdp"])
    rows = P(AXES, None)
    blocks = P(AXES, None, None)
    return jax.shard_map(
        functools.partial(shards, sizes),
        mesh=mesh,
        in_specs=(rows, rows, rows, P(), blocks, blocks, blocks, blocks, blocks, P(), P(), P()),
        out_specs=(rows, rows, P(), blocks, blocks, blocks, P(), P(), P()),
        check_vma=False,
    )
```

```python
import functools
import math

import jax
import jax.numpy as jnp
from jax import lax
from jax.experimental import pallas as pl
from jax.experimental.pallas import tpu as pltpu
from jax.sharding import PartitionSpec as P

HEADS = 12
STEP = 2
AXES = ("dp", "fsdp")

norm_eps = 1e-06
adam_eps = 1e-08
beta = 0.5
rate_matrix = 0.03
rate_vector = 0.05
decay_weight = 0.01
high = lax.Precision.HIGH
far = 2.0**30
low = jnp.bfloat16
wide = jnp.float32

CHUNK = 1024


def ring_order(dp, fsdp):
    if (dp, fsdp) != (8, 4):
        return None
    order = []
    for turn, (x, y) in enumerate(((0, 0), (1, 0), (1, 1), (0, 1))):
        places = range(4) if turn % 2 == 0 else range(3, -1, -1)
        for z in places:
            order += [(z * 2 + x) * 4 + y * 2 + core for core in (0, 1)]
    return order


def mm(a, b, ca, cb):
    return lax.dot_general(a, b, (((ca,), (cb,)), ((), ())), preferred_element_type=wide)


def normal_parts(values):
    center = values - jnp.mean(values, axis=-1, keepdims=True)
    factor = lax.rsqrt(jnp.mean(center * center, axis=-1, keepdims=True) + norm_eps)
    return center * factor, factor


def norm_back(grad, normal, factor, gain):
    inner = grad * gain
    return factor * (
        inner
        - jnp.mean(inner, axis=-1, keepdims=True)
        - normal * jnp.mean(inner * normal, axis=-1, keepdims=True)
    )


def start_blocks(place, whole, target, sem, first, across, row0, col0, height, breadth):
    def one(r, carry):
        at = first + (row0 + r) * across + col0
        down = pl.ds(pl.multiple_of(r * 128, 128), 128)
        for c in range(breadth):
            pltpu.make_async_copy(
                whole.at[place[at + c]], target.at[down, pl.ds(c * 128, 128)], sem
            ).start()
        return carry

    lax.fori_loop(0, height, one, 0)


def store_blocks(place, source, buffer, sem, first, across, row0, col0, height, breadth):
    def one(r, carry):
        at = first + (row0 + r) * across + col0
        down = pl.ds(pl.multiple_of(r * 128, 128), 128)
        for c in range(breadth):
            pltpu.make_async_copy(
                source.at[down, pl.ds(c * 128, 128)], buffer.at[place[at + c]], sem
            ).start()
        return carry

    lax.fori_loop(0, height, one, 0)


def await_bytes(ref, sem):
    pltpu.make_async_copy(ref, ref, sem).wait()


TILE = 112


def tiles(rows):
    return rows // TILE


def rows_of(t):
    return pl.ds(pl.multiple_of(t * TILE, 16), TILE)


def ready_kernel(patches, cotangent, inside, vectors, normed, normed_t, grad_two, bias_down):
    rows, width = patches.shape

    def norm(t, total):
        at = rows_of(t)
        normal, _ = normal_parts(patches[at, :].astype(wide))
        normed[at, :] = (normal * vectors[0:1, :] + vectors[1:2, :]).astype(low)
        two = (inside[at, :] * cotangent[at, :].astype(wide)).astype(low)
        grad_two[at, :] = two
        return total + jnp.sum(two.astype(wide), axis=0, keepdims=True)

    bias_down[...] = lax.fori_loop(0, tiles(rows), norm, jnp.zeros((1, width), wide))
    normed_t[...] = normed[...].T


def qkv_kernel(place, whole, normed, vectors, project, weight, sems):
    rows, width = normed.shape
    side = width // 128
    for part in range(3):
        start_blocks(
            place, whole, weight.at[part], sems.at[part], 0, 3 * side, 0, part * side, side, side
        )
    for part in range(3):
        await_bytes(weight.at[part], sems.at[part])
        out = mm(normed[...], weight[part], 1, 0)
        if part == 0:
            out = out + vectors[2:3, :]
        if part == 2:
            out = out + vectors[3:4, :]
        project[:, part * width : (part + 1) * width] = out.astype(low)


def attend_kernel(query, keys, values, image_query, image_keys, mixed, probs, scores):
    rows = query.shape[0]
    lane = lax.broadcasted_iota(jnp.int32, (rows, 128), 1)
    wide_keys = jnp.concatenate([keys[...], image_keys[...]], axis=1)
    scaled = query[...] * jnp.asarray(0.125, low)
    outs = []
    for h in range(2):
        part = jnp.where(lane // 64 == h, scaled, jnp.zeros_like(scaled))
        scores[h] = mm(jnp.concatenate([part, image_query[...]], axis=1), wide_keys, 1, 1)
    for h in range(2):
        for t in range(tiles(rows)):
            at = slice(t * TILE, (t + 1) * TILE)
            s = scores[h, at, :]
            e = jnp.exp(s - jnp.max(s, axis=-1, keepdims=True))
            total = jnp.sum(e, axis=-1, keepdims=True)
            probs[h, at, :] = (e * (1.0 / total)).astype(low)
        outs.append(mm(probs[h], values[...], 1, 0))
    mixed[...] = jnp.where(lane < 64, outs[0], outs[1]).astype(low)


def feed_kernel(
    place,
    whole,
    patches,
    cotangent,
    grad_two,
    mixed,
    inside,
    vectors,
    bias_up,
    middle,
    active,
    grad_middle,
    grad_mixed,
    sums,
    sums_up,
    buffer,
    w_out,
    w_up,
    w_down,
    normal,
    factor,
    second,
    second_t,
    out_sum,
    back_sum,
    stage_up,
    stage_down,
    stage_out,
    grad_pre,
    sems,
    out_sems,
):
    step = pl.program_id(0)
    steps = pl.num_programs(0)
    rows, width = patches.shape
    side = width // 128
    hidden = 4 * width
    high = hidden // 128
    per = CHUNK // 128
    first_out = 3 * side * side
    first_up = 4 * side * side
    first_down = first_up + side * high

    def fetch(index, slot):
        start_blocks(
            place, whole, w_up.at[slot], sems.at[slot], first_up, high, 0, index * per, side, per
        )
        start_blocks(
            place, whole, w_down.at[slot], sems.at[2 + slot], first_down, side, index * per, 0, per, side
        )

    @pl.when(step == 0)
    def _():
        start_blocks(place, whole, w_out, sems.at[4], first_out, side, 0, 0, side, side)
        fetch(0, 0)
        fetch(1, 1)
        await_bytes(w_out, sems.at[4])
        out_sum[...] = mm(mixed[...], w_out[...], 1, 0)

        def norm(t, carry):
            at = rows_of(t)
            keep = inside[at, :]
            mid = patches[at, :].astype(wide) + keep * (out_sum[at, :] + vectors[4:5, :])
            middle[at, :] = mid
            scaled, q = normal_parts(mid)
            normal[at, :] = scaled
            factor[at, :] = q
            second[at, :] = (scaled * vectors[5:6, :] + vectors[6:7, :]).astype(low)
            return carry

        lax.fori_loop(0, tiles(rows), norm, 0)
        second_t[...] = second[...].T
        back_sum[...] = jnp.zeros_like(back_sum)

    slot = lax.rem(step, 2)
    await_bytes(w_up.at[slot], sems.at[slot])
    await_bytes(w_down.at[slot], sems.at[2 + slot])

    @pl.when(step >= 2)
    def _():
        await_bytes(stage_up.at[slot], out_sems.at[slot])
        await_bytes(stage_down.at[slot], out_sems.at[2 + slot])

    parts = [slice(h * 256, (h + 1) * 256) for h in range(CHUNK // 256)]
    pres = [mm(second[...], w_up[slot, :, p], 1, 0) + bias_up[0, :, p] for p in parts]
    grads = [mm(grad_two[...], w_down[slot, p, :], 1, 1) for p in parts]
    for p, pre, grad in zip(parts, pres, grads):
        half = 0.5 * (1.0 + lax.erf(pre * math.sqrt(0.5)))
        active[:, p] = (pre * half).astype(low)
        slope = half + pre * (jnp.exp(-0.5 * pre * pre) * (1.0 / math.sqrt(2.0 * math.pi)))
        back = (grad * slope).astype(low)
        grad_pre[:, p] = back
        sums_up[0, :, p] = jnp.sum(back.astype(wide), axis=0, keepdims=True)
        stage_up[slot, :, p] = mm(second_t[...], grad_pre[:, p], 1, 0).astype(low)
        stage_down[slot, p, :] = mm(active[:, p], grad_two[...], 0, 0).astype(low)
    back_sum[...] += mm(grad_pre[...], w_up[slot], 1, 1)
    store_blocks(
        place, stage_up.at[slot], buffer, out_sems.at[slot], first_up, high, 0, step * per, side, per
    )
    store_blocks(
        place, stage_down.at[slot], buffer, out_sems.at[2 + slot], first_down, side, step * per, 0, per, side
    )

    @pl.when(step + 2 < steps)
    def _():
        fetch(step + 2, slot)

    @pl.when(step == steps - 1)
    def _():
        def finish(t, total):
            at = rows_of(t)
            keep = inside[at, :]
            grad = back_sum[at, :]
            scaled = normal[at, :]
            mid = cotangent[at, :].astype(wide) + norm_back(
                grad, scaled, factor[at, :], vectors[5:6, :]
            )
            grad_middle[at, :] = mid
            one = (keep * mid).astype(low)
            second[at, :] = one
            gain, shift, bias = total
            return (
                gain + jnp.sum(grad * scaled, axis=0, keepdims=True),
                shift + jnp.sum(grad, axis=0, keepdims=True),
                bias + jnp.sum(one.astype(wide), axis=0, keepdims=True),
            )

        empty = jnp.zeros((1, width), wide)
        gain, shift, bias = lax.fori_loop(0, tiles(rows), finish, (empty, empty, empty))
        sums[0:1, :] = bias
        sums[1:2, :] = gain
        sums[2:3, :] = shift
        sums[3:8, :] = jnp.zeros((5, width), wide)
        stage_out[...] = mm(mixed[...], second[...], 0, 0).astype(low)
        store_blocks(place, stage_out, buffer, out_sems.at[4], first_out, side, 0, 0, side, side)
        grad_mixed[...] = mm(second[...], w_out[...], 1, 1).astype(low)
        for other in range(2):
            await_bytes(stage_up.at[other], out_sems.at[other])
            await_bytes(stage_down.at[other], out_sems.at[2 + other])
        await_bytes(stage_out, out_sems.at[4])


def back_kernel(
    place,
    held,
    query,
    keys,
    values,
    probs,
    grad_mixed,
    mixed,
    normed_t,
    grad_project,
    buffer,
    grad_low,
    stage,
    out_sems,
):
    del held
    step = pl.program_id(0)
    steps = pl.num_programs(0)
    width, rows = normed_t.shape
    side = width // 128
    scale = 0.125
    lane = lax.broadcasted_iota(jnp.int32, (rows, 128), 1)
    grad = grad_mixed[...]
    grad_t = grad.T
    query_t = query[...].T
    outer = grad.astype(wide) * mixed[...].astype(wide)
    mine = [lane // 64 == h for h in range(2)]
    grad_probs = [
        mm(jnp.where(mine[h], grad, jnp.zeros_like(grad)), values[...], 1, 1) for h in range(2)
    ]
    turned_values = [mm(grad_t[h * 64 : (h + 1) * 64, :], probs[h], 1, 0) for h in range(2)]
    turned_query = []
    turned_keys = []
    for h in range(2):
        delta = jnp.sum(jnp.where(mine[h], outer, 0.0), axis=-1, keepdims=True)
        grad_low[h] = (probs[h].astype(wide) * (grad_probs[h] - delta)).astype(low)
        turned_query.append(mm(grad_low[h], keys[...], 1, 0))
        turned_keys.append(mm(query_t[h * 64 : (h + 1) * 64, :], grad_low[h], 1, 0))
    grad_query = jnp.where(lane < 64, turned_query[0], turned_query[1]) * scale
    grad_keys = (jnp.concatenate(turned_keys, axis=0) * scale).T
    grad_values = jnp.concatenate(turned_values, axis=0).T
    at = pl.multiple_of(step * 128, 128)
    for part, value in enumerate((grad_query, grad_keys, grad_values)):
        grad_project[part, :, pl.ds(at, 128)] = value.astype(low)

    @pl.when(step == steps - 1)
    def _():
        for part in range(3):
            if part == 2:
                await_bytes(stage.at[0], out_sems.at[0])
            stage[part % 2] = mm(normed_t[...], grad_project[part], 1, 0).astype(low)
            store_blocks(
                place,
                stage.at[part % 2],
                buffer,
                out_sems.at[part % 2],
                0,
                3 * side,
                0,
                part * side,
                side,
                side,
            )
        await_bytes(stage.at[1], out_sems.at[1])
        await_bytes(stage.at[0], out_sems.at[0])


def result_kernel(place, whole, active, middle, inside, vectors, result, w_down, total, sems):
    step = pl.program_id(0)
    steps = pl.num_programs(0)
    rows, width = middle.shape
    side = width // 128
    high = 4 * side
    per = CHUNK // 128
    first_down = 4 * side * side + side * high

    def fetch(index, slot):
        start_blocks(
            place, whole, w_down.at[slot], sems.at[slot], first_down, side, index * per, 0, per, side
        )

    @pl.when(step == 0)
    def _():
        total[...] = jnp.zeros_like(total)
        fetch(0, 0)
        fetch(1, 1)

    slot = lax.rem(step, 2)
    await_bytes(w_down.at[slot], sems.at[slot])
    total[...] += mm(active[...], w_down[slot], 1, 0)

    @pl.when(step + 2 < steps)
    def _():
        fetch(step + 2, slot)

    @pl.when(step == steps - 1)
    def _():
        def finish(t, carry):
            at = rows_of(t)
            result[at, :] = (
                middle[at, :] + inside[at, :] * (total[at, :] + vectors[11:12, :])
            ).astype(low)
            return carry

        lax.fori_loop(0, tiles(rows), finish, 0)


def input_kernel(
    place, whole, grad_project, patches, grad_middle, vectors, grad_input, sums, weight, grad_sum, sems
):
    rows, width = patches.shape
    side = width // 128
    for part in range(3):
        start_blocks(
            place, whole, weight.at[part], sems.at[part], 0, 3 * side, 0, part * side, side, side
        )
    for part in range(3):
        await_bytes(weight.at[part], sems.at[part])
    total = mm(grad_project[0], weight[0], 1, 1)
    total = total + mm(grad_project[1], weight[1], 1, 1)
    grad_sum[...] = total + mm(grad_project[2], weight[2], 1, 1)

    def finish(t, carry):
        at = rows_of(t)
        grad = grad_sum[at, :]
        normal, factor = normal_parts(patches[at, :].astype(wide))
        back = norm_back(grad, normal, factor, vectors[0:1, :])
        grad_input[at, :] = (grad_middle[at, :] + back).astype(low)
        gain, shift, bias_query, bias_value = carry
        return (
            gain + jnp.sum(grad * normal, axis=0, keepdims=True),
            shift + jnp.sum(grad, axis=0, keepdims=True),
            bias_query + jnp.sum(grad_project[0, at, :].astype(wide), axis=0, keepdims=True),
            bias_value + jnp.sum(grad_project[2, at, :].astype(wide), axis=0, keepdims=True),
        )

    empty = jnp.zeros((1, width), wide)
    found = lax.fori_loop(0, tiles(rows), finish, (empty, empty, empty, empty))
    for row in range(4):
        sums[row : row + 1, :] = found[row]
    sums[4:8, :] = jnp.zeros((4, width), wide)


def squares_kernel(named, grads, spread):
    total = jnp.zeros((128, 128), wide)
    for s in range(grads.shape[0]):
        block = jnp.where(named[s] > 0, grads[s].astype(wide), 0.0)
        total = total + block * block
    spread[...] = jnp.broadcast_to(jnp.sum(total), spread.shape)


VMEM_LIMIT = 60 * 1024 * 1024


def params(count=1):
    return pltpu.CompilerParams(
        dimension_semantics=("arbitrary",) * count, vmem_limit_bytes=VMEM_LIMIT
    )


def whole_spec():
    return pl.BlockSpec(memory_space=pl.ANY)


def full(shape):
    return pl.BlockSpec(shape, lambda *_: (0,) * len(shape))


def shards(
    sizes,
    patches,
    lengths,
    cotangent,
    owners,
    master,
    first_moment,
    second_moment,
    left_basis,
    right_basis,
    vectors,
    vector_first,
    vector_second,
):
    dp, fsdp = sizes
    devices = dp * fsdp
    rows, width = patches.shape
    hidden = 4 * width
    side = width // 128
    pairs = width // 128
    held, size = master.shape[0], master.shape[1]
    slots = held * devices
    shape = jax.ShapeDtypeStruct
    me = lax.axis_index(AXES)
    order = ring_order(dp, fsdp)
    groups = None if order is None else [order]

    def gather(value):
        return lax.all_gather(value, AXES, axis=0, tiled=True, axis_index_groups=groups)

    def scatter(value):
        return lax.psum_scatter(
            value, AXES, scatter_dimension=0, tiled=True, axis_index_groups=groups
        )

    def everywhere(value):
        step = 1
        while step < devices:
            value = value + lax.ppermute(value, AXES, [(d, d ^ step) for d in range(devices)])
            step *= 2
        return value

    whole = gather(master.astype(low))
    if order is None:
        place = owners
    else:
        rank = [0] * devices
        for spot, device in enumerate(order):
            rank[device] = spot
        device = owners // held
        spot = jnp.sum(
            jnp.where(
                device[:, None] == jnp.arange(devices, dtype=jnp.int32)[None, :],
                jnp.array(rank, jnp.int32)[None, :],
                0,
            ),
            axis=1,
        )
        place = spot * held + owners % held
    mine = me * held + jnp.arange(held, dtype=jnp.int32)
    named = jnp.any(mine[:, None] == owners[None, :], axis=1)

    counts = lengths[0]
    ends = jnp.cumsum(counts)
    places = jnp.arange(rows, dtype=jnp.int32)[:, None]
    image = jnp.sum((places >= ends[None, :]).astype(jnp.int32), axis=1, keepdims=True)
    within = places < ends[-1]
    image = jnp.where(within, image, 4)
    inside = within.astype(wide)
    lanes = jnp.arange(128, dtype=jnp.int32)[None, :]
    image_keys = (lanes == image).astype(low)
    image_query = jnp.where((lanes != image) & (lanes < 5), -far, 0.0).astype(low)

    normed, normed_t, grad_two, bias_down = pl.pallas_call(
        ready_kernel,
        out_shape=[
            shape((rows, width), low),
            shape((width, rows), low),
            shape((rows, width), low),
            shape((1, width), wide),
        ],
        compiler_params=pltpu.CompilerParams(vmem_limit_bytes=VMEM_LIMIT),
        name="ready",
    )(patches, cotangent, inside, vectors)

    project = pl.pallas_call(
        qkv_kernel,
        grid_spec=pltpu.PrefetchScalarGridSpec(
            num_scalar_prefetch=1,
            grid=(1,),
            in_specs=[whole_spec(), full((rows, width)), full((12, width))],
            out_specs=full((rows, 3 * width)),
            scratch_shapes=[
                pltpu.VMEM((3, width, width), low),
                pltpu.SemaphoreType.DMA((3,)),
            ],
        ),
        out_shape=shape((rows, 3 * width), low),
        compiler_params=params(),
        name="qkv",
    )(place, whole, normed, vectors)

    def column(offset):
        return pl.BlockSpec((rows, 128), lambda j, *_: (0, j + offset))

    mixed, probs = pl.pallas_call(
        attend_kernel,
        grid=(pairs,),
        in_specs=[
            column(0),
            column(pairs),
            column(2 * pairs),
            full((rows, 128)),
            full((rows, 128)),
        ],
        out_specs=[column(0), pl.BlockSpec((2, rows, rows), lambda j: (j, 0, 0))],
        out_shape=[shape((rows, width), low), shape((HEADS, rows, rows), low)],
        scratch_shapes=[pltpu.VMEM((2, rows, rows), wide)],
        compiler_params=params(),
        name="attend",
    )(project, project, project, image_query, image_keys)

    steps = hidden // CHUNK
    middle, active, grad_middle, grad_mixed, sums_two, sums_up, buffer = pl.pallas_call(
        feed_kernel,
        grid_spec=pltpu.PrefetchScalarGridSpec(
            num_scalar_prefetch=1,
            grid=(steps,),
            in_specs=[
                whole_spec(),
                full((rows, width)),
                full((rows, width)),
                full((rows, width)),
                full((rows, width)),
                full((rows, 1)),
                full((12, width)),
                pl.BlockSpec((1, 1, CHUNK), lambda c, *_: (c, 0, 0)),
            ],
            out_specs=[
                full((rows, width)),
                pl.BlockSpec((rows, CHUNK), lambda c, *_: (0, c)),
                full((rows, width)),
                full((rows, width)),
                full((8, width)),
                pl.BlockSpec((1, 1, CHUNK), lambda c, *_: (c, 0, 0)),
                whole_spec(),
            ],
            scratch_shapes=[
                pltpu.VMEM((width, width), low),
                pltpu.VMEM((2, width, CHUNK), low),
                pltpu.VMEM((2, CHUNK, width), low),
                pltpu.VMEM((rows, width), wide),
                pltpu.VMEM((rows, 1), wide),
                pltpu.VMEM((rows, width), low),
                pltpu.VMEM((width, rows), low),
                pltpu.VMEM((rows, width), wide),
                pltpu.VMEM((rows, width), wide),
                pltpu.VMEM((2, width, CHUNK), low),
                pltpu.VMEM((2, CHUNK, width), low),
                pltpu.VMEM((width, width), low),
                pltpu.VMEM((rows, CHUNK), low),
                pltpu.SemaphoreType.DMA((5,)),
                pltpu.SemaphoreType.DMA((5,)),
            ],
        ),
        out_shape=[
            shape((rows, width), wide),
            shape((rows, hidden), low),
            shape((rows, width), wide),
            shape((rows, width), low),
            shape((8, width), wide),
            shape((steps, 1, CHUNK), wide),
            shape((slots, size, size), low),
        ],
        compiler_params=params(),
        name="feed",
    )(
        place,
        whole,
        patches,
        cotangent,
        grad_two,
        mixed,
        inside,
        vectors,
        vectors[7:11].reshape(steps, 1, CHUNK),
    )

    grad_project, buffer = pl.pallas_call(
        back_kernel,
        grid_spec=pltpu.PrefetchScalarGridSpec(
            num_scalar_prefetch=1,
            grid=(pairs,),
            in_specs=[
                whole_spec(),
                column(0),
                column(pairs),
                column(2 * pairs),
                pl.BlockSpec((2, rows, rows), lambda j, *_: (j, 0, 0)),
                column(0),
                column(0),
                full((width, rows)),
            ],
            out_specs=[full((3, rows, width)), whole_spec()],
            scratch_shapes=[
                pltpu.VMEM((2, rows, rows), low),
                pltpu.VMEM((2, width, width), low),
                pltpu.SemaphoreType.DMA((2,)),
            ],
        ),
        out_shape=[
            shape((3, rows, width), low),
            shape((slots, size, size), low),
        ],
        input_output_aliases={1: 1},
        compiler_params=params(),
        name="back",
    )(
        place,
        buffer,
        project,
        project,
        project,
        probs,
        grad_mixed,
        mixed,
        normed_t,
    )
    owned = scatter(buffer)

    grad_input, sums_one = pl.pallas_call(
        input_kernel,
        grid_spec=pltpu.PrefetchScalarGridSpec(
            num_scalar_prefetch=1,
            grid=(1,),
            in_specs=[
                whole_spec(),
                full((3, rows, width)),
                full((rows, width)),
                full((rows, width)),
                full((12, width)),
            ],
            out_specs=[full((rows, width)), full((8, width))],
            scratch_shapes=[
                pltpu.VMEM((3, width, width), low),
                pltpu.VMEM((rows, width), wide),
                pltpu.SemaphoreType.DMA((3,)),
            ],
        ),
        out_shape=[shape((rows, width), low), shape((8, width), wide)],
        compiler_params=params(),
        name="input",
    )(place, whole, grad_project, patches, grad_middle, vectors)
    result = pl.pallas_call(
        result_kernel,
        grid_spec=pltpu.PrefetchScalarGridSpec(
            num_scalar_prefetch=1,
            grid=(steps,),
            in_specs=[
                whole_spec(),
                pl.BlockSpec((rows, CHUNK), lambda c, *_: (0, c)),
                full((rows, width)),
                full((rows, 1)),
                full((12, width)),
            ],
            out_specs=full((rows, width)),
            scratch_shapes=[
                pltpu.VMEM((2, CHUNK, width), low),
                pltpu.VMEM((rows, width), wide),
                pltpu.SemaphoreType.DMA((2,)),
            ],
        ),
        out_shape=shape((rows, width), low),
        compiler_params=params(),
        name="result",
    )(place, whole, active, middle, inside, vectors)
    vector_grad = jnp.concatenate(
        [sums_one[0:4], sums_two[0:3], sums_up.reshape(4, width), bias_down], axis=0
    )
    vector_sum = everywhere(vector_grad)

    owned, vector_sum, result = lax.optimization_barrier((owned, vector_sum, result))

    received = owned
    owned = jnp.where(named[:, None, None], owned.astype(wide), 0.0)
    squares = pl.pallas_call(
        squares_kernel,
        in_specs=[pl.BlockSpec(memory_space=pltpu.SMEM), full((held, size, size))],
        out_specs=full((devices, 128)),
        out_shape=shape((devices, 128), wide),
        grid=(),
        name="squares",
    )(named.astype(jnp.int32), received)
    total_blocks = jnp.sum(lax.all_to_all(squares, AXES, 0, 0, tiled=True)[:, 0])
    clip_norm = jnp.sqrt(total_blocks + jnp.sum(vector_sum * vector_sum))
    count = owners.shape[0] * size * size + vectors.shape[0] * width
    factor = jnp.minimum(1.0, 0.5 * math.sqrt(count) / clip_norm)
    turned = jnp.einsum("sji,sjk->sik", left_basis, owned, precision=high)
    rotated = factor * jnp.einsum("sik,skl->sil", turned, right_basis, precision=high)
    new_first = beta * first_moment + (1.0 - beta) * rotated
    new_second = beta * second_moment + (1.0 - beta) * rotated * rotated
    correction = 1.0 - beta**STEP
    direction = new_first / correction / (jnp.sqrt(new_second / correction) + adam_eps)
    back_turn = jnp.einsum("sij,sjk->sik", left_basis, direction, precision=high)
    update = jnp.einsum("sik,slk->sil", back_turn, right_basis, precision=high)
    new_master = master - rate_matrix * (update + decay_weight * master)
    vector_clip = factor * vector_sum
    new_vector_first = beta * vector_first + (1.0 - beta) * vector_clip
    new_vector_second = beta * vector_second + (1.0 - beta) * vector_clip * vector_clip
    vector_step = (
        new_vector_first / correction / (jnp.sqrt(new_vector_second / correction) + adam_eps)
    )
    new_vectors = vectors - rate_vector * vector_step
    return (
        result,
        grad_input,
        clip_norm,
        new_master,
        new_first,
        new_second,
        new_vectors,
        new_vector_first,
        new_vector_second,
    )


def solution(mesh):
    sizes = (mesh.shape["dp"], mesh.shape["fsdp"])
    rows = P(AXES, None)
    blocks = P(AXES, None, None)
    return jax.shard_map(
        functools.partial(shards, sizes),
        mesh=mesh,
        in_specs=(rows, rows, rows, P(), blocks, blocks, blocks, blocks, blocks, P(), P(), P()),
        out_specs=(rows, rows, P(), blocks, blocks, blocks, P(), P(), P()),
        check_vma=False,
    )
```

```python
import functools
import math

import jax
import jax.numpy as jnp
from jax import lax
from jax.experimental import pallas as pl
from jax.experimental.pallas import tpu as pltpu
from jax.sharding import PartitionSpec as P

HEADS = 12
STEP = 2
AXES = ("dp", "fsdp")

norm_eps = 1e-06
adam_eps = 1e-08
beta = 0.5
rate_matrix = 0.03
rate_vector = 0.05
decay_weight = 0.01
high = lax.Precision.HIGH
far = 2.0**30
low = jnp.bfloat16
wide = jnp.float32

CHUNK = 1024
PIECE = 256


def ring_order(dp, fsdp):
    if (dp, fsdp) != (8, 4):
        return None
    order = []
    for turn, (x, y) in enumerate(((0, 0), (1, 0), (1, 1), (0, 1))):
        places = range(4) if turn % 2 == 0 else range(3, -1, -1)
        for z in places:
            order += [(z * 2 + x) * 4 + y * 2 + core for core in (0, 1)]
    return order


def mm(a, b, ca, cb):
    return lax.dot_general(a, b, (((ca,), (cb,)), ((), ())), preferred_element_type=wide)


def normal_parts(values):
    center = values - jnp.mean(values, axis=-1, keepdims=True)
    factor = lax.rsqrt(jnp.mean(center * center, axis=-1, keepdims=True) + norm_eps)
    return center * factor, factor


def norm_back(grad, normal, factor, gain):
    inner = grad * gain
    return factor * (
        inner
        - jnp.mean(inner, axis=-1, keepdims=True)
        - normal * jnp.mean(inner * normal, axis=-1, keepdims=True)
    )


def start_blocks(place, whole, target, sem, first, across, row0, col0, height, breadth):
    def one(r, carry):
        at = first + (row0 + r) * across + col0
        down = pl.ds(pl.multiple_of(r * 128, 128), 128)
        for c in range(breadth):
            pltpu.make_async_copy(
                whole.at[place[at + c]], target.at[down, pl.ds(c * 128, 128)], sem
            ).start()
        return carry

    lax.fori_loop(0, height, one, 0)


def store_blocks(place, source, buffer, sem, first, across, row0, col0, height, breadth):
    def one(r, carry):
        at = first + (row0 + r) * across + col0
        down = pl.ds(pl.multiple_of(r * 128, 128), 128)
        for c in range(breadth):
            pltpu.make_async_copy(
                source.at[down, pl.ds(c * 128, 128)], buffer.at[place[at + c]], sem
            ).start()
        return carry

    lax.fori_loop(0, height, one, 0)


def await_bytes(ref, sem):
    pltpu.make_async_copy(ref, ref, sem).wait()


TILE = 112


def tiles(rows):
    return rows // TILE


def rows_of(t):
    return pl.ds(pl.multiple_of(t * TILE, 16), TILE)


def ready_kernel(patches, cotangent, inside, vectors, normed, normed_t, grad_two, bias_down):
    rows, width = patches.shape

    def norm(t, total):
        at = rows_of(t)
        normal, _ = normal_parts(patches[at, :].astype(wide))
        normed[at, :] = (normal * vectors[0:1, :] + vectors[1:2, :]).astype(low)
        two = (inside[at, :] * cotangent[at, :].astype(wide)).astype(low)
        grad_two[at, :] = two
        return total + jnp.sum(two.astype(wide), axis=0, keepdims=True)

    bias_down[...] = lax.fori_loop(0, tiles(rows), norm, jnp.zeros((1, width), wide))
    normed_t[...] = normed[...].T


def qkv_kernel(place, whole, normed, vectors, project, weight, sems):
    rows, width = normed.shape
    side = width // 128
    for part in range(3):
        start_blocks(
            place, whole, weight.at[part], sems.at[part], 0, 3 * side, 0, part * side, side, side
        )
    for part in range(3):
        await_bytes(weight.at[part], sems.at[part])
        out = mm(normed[...], weight[part], 1, 0)
        if part == 0:
            out = out + vectors[2:3, :]
        if part == 2:
            out = out + vectors[3:4, :]
        project[:, part * width : (part + 1) * width] = out.astype(low)


def attend_kernel(query, keys, values, image_query, image_keys, mixed, probs, scores):
    rows = query.shape[0]
    lane = lax.broadcasted_iota(jnp.int32, (rows, 128), 1)
    wide_keys = jnp.concatenate([keys[...], image_keys[...]], axis=1)
    scaled = query[...] * jnp.asarray(0.125, low)
    outs = []
    for h in range(2):
        part = jnp.where(lane // 64 == h, scaled, jnp.zeros_like(scaled))
        scores[h] = mm(jnp.concatenate([part, image_query[...]], axis=1), wide_keys, 1, 1)
    for h in range(2):
        for t in range(tiles(rows)):
            at = slice(t * TILE, (t + 1) * TILE)
            s = scores[h, at, :]
            e = jnp.exp(s - jnp.max(s, axis=-1, keepdims=True))
            total = jnp.sum(e, axis=-1, keepdims=True)
            probs[h, at, :] = (e * (1.0 / total)).astype(low)
        outs.append(mm(probs[h], values[...], 1, 0))
    mixed[...] = jnp.where(lane < 64, outs[0], outs[1]).astype(low)


def feed_kernel(
    place,
    whole,
    patches,
    cotangent,
    grad_two,
    mixed,
    inside,
    vectors,
    bias_up,
    middle,
    active,
    grad_middle,
    grad_mixed,
    sums,
    sums_up,
    buffer,
    w_out,
    w_up,
    w_down,
    normal,
    factor,
    second,
    second_t,
    out_sum,
    back_sum,
    stage_up,
    stage_down,
    stage_out,
    grad_pre,
    sems,
    out_sems,
):
    step = pl.program_id(0)
    steps = pl.num_programs(0)
    rows, width = patches.shape
    side = width // 128
    hidden = 4 * width
    high = hidden // 128
    per = CHUNK // 128
    first_out = 3 * side * side
    first_up = 4 * side * side
    first_down = first_up + side * high

    def fetch(index, slot):
        start_blocks(
            place, whole, w_up.at[slot], sems.at[slot], first_up, high, 0, index * per, side, per
        )
        start_blocks(
            place, whole, w_down.at[slot], sems.at[2 + slot], first_down, side, index * per, 0, per, side
        )

    @pl.when(step == 0)
    def _():
        start_blocks(place, whole, w_out, sems.at[4], first_out, side, 0, 0, side, side)
        fetch(0, 0)
        fetch(1, 1)
        await_bytes(w_out, sems.at[4])
        out_sum[...] = mm(mixed[...], w_out[...], 1, 0)

        def norm(t, carry):
            at = rows_of(t)
            keep = inside[at, :]
            mid = patches[at, :].astype(wide) + keep * (out_sum[at, :] + vectors[4:5, :])
            middle[at, :] = mid
            scaled, q = normal_parts(mid)
            normal[at, :] = scaled
            factor[at, :] = q
            second[at, :] = (scaled * vectors[5:6, :] + vectors[6:7, :]).astype(low)
            return carry

        lax.fori_loop(0, tiles(rows), norm, 0)
        second_t[...] = second[...].T
        back_sum[...] = jnp.zeros_like(back_sum)

    slot = lax.rem(step, 2)
    await_bytes(w_up.at[slot], sems.at[slot])
    await_bytes(w_down.at[slot], sems.at[2 + slot])

    @pl.when(step >= 2)
    def _():
        await_bytes(stage_up.at[slot], out_sems.at[slot])
        await_bytes(stage_down.at[slot], out_sems.at[2 + slot])

    parts = [slice(h * 256, (h + 1) * 256) for h in range(CHUNK // 256)]
    pres = [mm(second[...], w_up[slot, :, p], 1, 0) + bias_up[0, :, p] for p in parts]
    grads = [mm(grad_two[...], w_down[slot, p, :], 1, 1) for p in parts]
    for p, pre, grad in zip(parts, pres, grads):
        half = 0.5 * (1.0 + lax.erf(pre * math.sqrt(0.5)))
        active[:, p] = (pre * half).astype(low)
        slope = half + pre * (jnp.exp(-0.5 * pre * pre) * (1.0 / math.sqrt(2.0 * math.pi)))
        back = (grad * slope).astype(low)
        grad_pre[:, p] = back
        sums_up[0, :, p] = jnp.sum(back.astype(wide), axis=0, keepdims=True)
        stage_up[slot, :, p] = mm(second_t[...], grad_pre[:, p], 1, 0).astype(low)
        stage_down[slot, p, :] = mm(active[:, p], grad_two[...], 0, 0).astype(low)
    back_sum[...] += mm(grad_pre[...], w_up[slot], 1, 1)
    store_blocks(
        place, stage_up.at[slot], buffer, out_sems.at[slot], first_up, high, 0, step * per, side, per
    )
    store_blocks(
        place, stage_down.at[slot], buffer, out_sems.at[2 + slot], first_down, side, step * per, 0, per, side
    )

    @pl.when(step + 2 < steps)
    def _():
        fetch(step + 2, slot)

    @pl.when(step == steps - 1)
    def _():
        def finish(t, total):
            at = rows_of(t)
            keep = inside[at, :]
            grad = back_sum[at, :]
            scaled = normal[at, :]
            mid = cotangent[at, :].astype(wide) + norm_back(
                grad, scaled, factor[at, :], vectors[5:6, :]
            )
            grad_middle[at, :] = mid
            one = (keep * mid).astype(low)
            second[at, :] = one
            gain, shift, bias = total
            return (
                gain + jnp.sum(grad * scaled, axis=0, keepdims=True),
                shift + jnp.sum(grad, axis=0, keepdims=True),
                bias + jnp.sum(one.astype(wide), axis=0, keepdims=True),
            )

        empty = jnp.zeros((1, width), wide)
        gain, shift, bias = lax.fori_loop(0, tiles(rows), finish, (empty, empty, empty))
        sums[0:1, :] = bias
        sums[1:2, :] = gain
        sums[2:3, :] = shift
        sums[3:8, :] = jnp.zeros((5, width), wide)
        stage_out[...] = mm(mixed[...], second[...], 0, 0).astype(low)
        store_blocks(place, stage_out, buffer, out_sems.at[4], first_out, side, 0, 0, side, side)
        grad_mixed[...] = mm(second[...], w_out[...], 1, 1).astype(low)
        for other in range(2):
            await_bytes(stage_up.at[other], out_sems.at[other])
            await_bytes(stage_down.at[other], out_sems.at[2 + other])
        await_bytes(stage_out, out_sems.at[4])


def back_kernel(
    place,
    held,
    query,
    keys,
    values,
    probs,
    grad_mixed,
    mixed,
    normed_t,
    grad_project,
    buffer,
    grad_low,
    stage,
    out_sems,
):
    del held
    step = pl.program_id(0)
    steps = pl.num_programs(0)
    width, rows = normed_t.shape
    side = width // 128
    scale = 0.125
    lane = lax.broadcasted_iota(jnp.int32, (rows, 128), 1)
    grad = grad_mixed[...]
    grad_t = grad.T
    query_t = query[...].T
    outer = grad.astype(wide) * mixed[...].astype(wide)
    mine = [lane // 64 == h for h in range(2)]
    grad_probs = [
        mm(jnp.where(mine[h], grad, jnp.zeros_like(grad)), values[...], 1, 1) for h in range(2)
    ]
    turned_values = [mm(grad_t[h * 64 : (h + 1) * 64, :], probs[h], 1, 0) for h in range(2)]
    turned_query = []
    turned_keys = []
    for h in range(2):
        delta = jnp.sum(jnp.where(mine[h], outer, 0.0), axis=-1, keepdims=True)
        grad_low[h] = (probs[h].astype(wide) * (grad_probs[h] - delta)).astype(low)
        turned_query.append(mm(grad_low[h], keys[...], 1, 0))
        turned_keys.append(mm(query_t[h * 64 : (h + 1) * 64, :], grad_low[h], 1, 0))
    grad_query = jnp.where(lane < 64, turned_query[0], turned_query[1]) * scale
    grad_keys = (jnp.concatenate(turned_keys, axis=0) * scale).T
    grad_values = jnp.concatenate(turned_values, axis=0).T
    at = pl.multiple_of(step * 128, 128)
    for part, value in enumerate((grad_query, grad_keys, grad_values)):
        grad_project[part, :, pl.ds(at, 128)] = value.astype(low)

    @pl.when(step == steps - 1)
    def _():
        for part in range(3):
            if part == 2:
                await_bytes(stage.at[0], out_sems.at[0])
            stage[part % 2] = mm(normed_t[...], grad_project[part], 1, 0).astype(low)
            store_blocks(
                place,
                stage.at[part % 2],
                buffer,
                out_sems.at[part % 2],
                0,
                3 * side,
                0,
                part * side,
                side,
                side,
            )
        await_bytes(stage.at[1], out_sems.at[1])
        await_bytes(stage.at[0], out_sems.at[0])


def result_kernel(place, whole, active, middle, inside, vectors, result, w_down, total, sems):
    step = pl.program_id(0)
    steps = pl.num_programs(0)
    rows, width = middle.shape
    side = width // 128
    high = 4 * side
    per = PIECE // 128
    first_down = 4 * side * side + side * high

    def fetch(index, slot):
        start_blocks(
            place, whole, w_down.at[slot], sems.at[slot], first_down, side, index * per, 0, per, side
        )

    @pl.when(step == 0)
    def _():
        total[...] = jnp.zeros_like(total)
        fetch(0, 0)
        fetch(1, 1)

    slot = lax.rem(step, 2)
    await_bytes(w_down.at[slot], sems.at[slot])
    total[...] += mm(active[...], w_down[slot], 1, 0)

    @pl.when(step + 2 < steps)
    def _():
        fetch(step + 2, slot)

    @pl.when(step == steps - 1)
    def _():
        def finish(t, carry):
            at = rows_of(t)
            result[at, :] = (
                middle[at, :] + inside[at, :] * (total[at, :] + vectors[11:12, :])
            ).astype(low)
            return carry

        lax.fori_loop(0, tiles(rows), finish, 0)


def input_kernel(
    place, whole, grad_project, patches, grad_middle, vectors, grad_input, sums, weight, grad_sum, sems
):
    rows, width = patches.shape
    side = width // 128
    for part in range(3):
        start_blocks(
            place, whole, weight.at[part], sems.at[part], 0, 3 * side, 0, part * side, side, side
        )
    grad_sum[...] = jnp.zeros_like(grad_sum)

    def product(part, carry):
        await_bytes(weight.at[part], sems.at[part])
        grad_sum[...] += mm(grad_project[part], weight[part], 1, 1)
        return carry

    lax.fori_loop(0, 3, product, 0)

    def finish(t, carry):
        at = rows_of(t)
        grad = grad_sum[at, :]
        normal, factor = normal_parts(patches[at, :].astype(wide))
        back = norm_back(grad, normal, factor, vectors[0:1, :])
        grad_input[at, :] = (grad_middle[at, :] + back).astype(low)
        gain, shift, bias_query, bias_value = carry
        return (
            gain + jnp.sum(grad * normal, axis=0, keepdims=True),
            shift + jnp.sum(grad, axis=0, keepdims=True),
            bias_query + jnp.sum(grad_project[0, at, :].astype(wide), axis=0, keepdims=True),
            bias_value + jnp.sum(grad_project[2, at, :].astype(wide), axis=0, keepdims=True),
        )

    empty = jnp.zeros((1, width), wide)
    found = lax.fori_loop(0, tiles(rows), finish, (empty, empty, empty, empty))
    for row in range(4):
        sums[row : row + 1, :] = found[row]
    sums[4:8, :] = jnp.zeros((4, width), wide)


def squares_kernel(named, grads, spread):
    total = jnp.zeros((128, 128), wide)
    for s in range(grads.shape[0]):
        block = jnp.where(named[s] > 0, grads[s].astype(wide), 0.0)
        total = total + block * block
    spread[...] = jnp.broadcast_to(jnp.sum(total), spread.shape)


VMEM_LIMIT = 60 * 1024 * 1024


def params(count=1):
    return pltpu.CompilerParams(
        dimension_semantics=("arbitrary",) * count, vmem_limit_bytes=VMEM_LIMIT
    )


def whole_spec():
    return pl.BlockSpec(memory_space=pl.ANY)


def full(shape):
    return pl.BlockSpec(shape, lambda *_: (0,) * len(shape))


def shards(
    sizes,
    patches,
    lengths,
    cotangent,
    owners,
    master,
    first_moment,
    second_moment,
    left_basis,
    right_basis,
    vectors,
    vector_first,
    vector_second,
):
    dp, fsdp = sizes
    devices = dp * fsdp
    rows, width = patches.shape
    hidden = 4 * width
    side = width // 128
    pairs = width // 128
    held, size = master.shape[0], master.shape[1]
    slots = held * devices
    shape = jax.ShapeDtypeStruct
    me = lax.axis_index(AXES)
    order = ring_order(dp, fsdp)
    groups = None if order is None else [order]

    def gather(value):
        return lax.all_gather(value, AXES, axis=0, tiled=True, axis_index_groups=groups)

    def scatter(value):
        return lax.psum_scatter(
            value, AXES, scatter_dimension=0, tiled=True, axis_index_groups=groups
        )

    def everywhere(value):
        step = 1
        while step < devices:
            value = value + lax.ppermute(value, AXES, [(d, d ^ step) for d in range(devices)])
            step *= 2
        return value

    whole = gather(master.astype(low))
    if order is None:
        place = owners
    else:
        rank = [0] * devices
        for spot, device in enumerate(order):
            rank[device] = spot
        device = owners // held
        spot = jnp.sum(
            jnp.where(
                device[:, None] == jnp.arange(devices, dtype=jnp.int32)[None, :],
                jnp.array(rank, jnp.int32)[None, :],
                0,
            ),
            axis=1,
        )
        place = spot * held + owners % held
    mine = me * held + jnp.arange(held, dtype=jnp.int32)
    named = jnp.any(mine[:, None] == owners[None, :], axis=1)

    counts = lengths[0]
    ends = jnp.cumsum(counts)
    places = jnp.arange(rows, dtype=jnp.int32)[:, None]
    image = jnp.sum((places >= ends[None, :]).astype(jnp.int32), axis=1, keepdims=True)
    within = places < ends[-1]
    image = jnp.where(within, image, 4)
    inside = within.astype(wide)
    lanes = jnp.arange(128, dtype=jnp.int32)[None, :]
    image_keys = (lanes == image).astype(low)
    image_query = jnp.where((lanes != image) & (lanes < 5), -far, 0.0).astype(low)

    normed, normed_t, grad_two, bias_down = pl.pallas_call(
        ready_kernel,
        out_shape=[
            shape((rows, width), low),
            shape((width, rows), low),
            shape((rows, width), low),
            shape((1, width), wide),
        ],
        compiler_params=pltpu.CompilerParams(vmem_limit_bytes=VMEM_LIMIT),
        name="ready",
    )(patches, cotangent, inside, vectors)

    project = pl.pallas_call(
        qkv_kernel,
        grid_spec=pltpu.PrefetchScalarGridSpec(
            num_scalar_prefetch=1,
            grid=(1,),
            in_specs=[whole_spec(), full((rows, width)), full((12, width))],
            out_specs=full((rows, 3 * width)),
            scratch_shapes=[
                pltpu.VMEM((3, width, width), low),
                pltpu.SemaphoreType.DMA((3,)),
            ],
        ),
        out_shape=shape((rows, 3 * width), low),
        compiler_params=params(),
        name="qkv",
    )(place, whole, normed, vectors)

    def column(offset):
        return pl.BlockSpec((rows, 128), lambda j, *_: (0, j + offset))

    mixed, probs = pl.pallas_call(
        attend_kernel,
        grid=(pairs,),
        in_specs=[
            column(0),
            column(pairs),
            column(2 * pairs),
            full((rows, 128)),
            full((rows, 128)),
        ],
        out_specs=[column(0), pl.BlockSpec((2, rows, rows), lambda j: (j, 0, 0))],
        out_shape=[shape((rows, width), low), shape((HEADS, rows, rows), low)],
        scratch_shapes=[pltpu.VMEM((2, rows, rows), wide)],
        compiler_params=params(),
        name="attend",
    )(project, project, project, image_query, image_keys)

    steps = hidden // CHUNK
    middle, active, grad_middle, grad_mixed, sums_two, sums_up, buffer = pl.pallas_call(
        feed_kernel,
        grid_spec=pltpu.PrefetchScalarGridSpec(
            num_scalar_prefetch=1,
            grid=(steps,),
            in_specs=[
                whole_spec(),
                full((rows, width)),
                full((rows, width)),
                full((rows, width)),
                full((rows, width)),
                full((rows, 1)),
                full((12, width)),
                pl.BlockSpec((1, 1, CHUNK), lambda c, *_: (c, 0, 0)),
            ],
            out_specs=[
                full((rows, width)),
                pl.BlockSpec((rows, CHUNK), lambda c, *_: (0, c)),
                full((rows, width)),
                full((rows, width)),
                full((8, width)),
                pl.BlockSpec((1, 1, CHUNK), lambda c, *_: (c, 0, 0)),
                whole_spec(),
            ],
            scratch_shapes=[
                pltpu.VMEM((width, width), low),
                pltpu.VMEM((2, width, CHUNK), low),
                pltpu.VMEM((2, CHUNK, width), low),
                pltpu.VMEM((rows, width), wide),
                pltpu.VMEM((rows, 1), wide),
                pltpu.VMEM((rows, width), low),
                pltpu.VMEM((width, rows), low),
                pltpu.VMEM((rows, width), wide),
                pltpu.VMEM((rows, width), wide),
                pltpu.VMEM((2, width, CHUNK), low),
                pltpu.VMEM((2, CHUNK, width), low),
                pltpu.VMEM((width, width), low),
                pltpu.VMEM((rows, CHUNK), low),
                pltpu.SemaphoreType.DMA((5,)),
                pltpu.SemaphoreType.DMA((5,)),
            ],
        ),
        out_shape=[
            shape((rows, width), wide),
            shape((rows, hidden), low),
            shape((rows, width), wide),
            shape((rows, width), low),
            shape((8, width), wide),
            shape((steps, 1, CHUNK), wide),
            shape((slots, size, size), low),
        ],
        compiler_params=params(),
        name="feed",
    )(
        place,
        whole,
        patches,
        cotangent,
        grad_two,
        mixed,
        inside,
        vectors,
        vectors[7:11].reshape(steps, 1, CHUNK),
    )

    grad_project, buffer = pl.pallas_call(
        back_kernel,
        grid_spec=pltpu.PrefetchScalarGridSpec(
            num_scalar_prefetch=1,
            grid=(pairs,),
            in_specs=[
                whole_spec(),
                column(0),
                column(pairs),
                column(2 * pairs),
                pl.BlockSpec((2, rows, rows), lambda j, *_: (j, 0, 0)),
                column(0),
                column(0),
                full((width, rows)),
            ],
            out_specs=[full((3, rows, width)), whole_spec()],
            scratch_shapes=[
                pltpu.VMEM((2, rows, rows), low),
                pltpu.VMEM((2, width, width), low),
                pltpu.SemaphoreType.DMA((2,)),
            ],
        ),
        out_shape=[
            shape((3, rows, width), low),
            shape((slots, size, size), low),
        ],
        input_output_aliases={1: 1},
        compiler_params=params(),
        name="back",
    )(
        place,
        buffer,
        project,
        project,
        project,
        probs,
        grad_mixed,
        mixed,
        normed_t,
    )
    owned = scatter(buffer)

    grad_input, sums_one = pl.pallas_call(
        input_kernel,
        grid_spec=pltpu.PrefetchScalarGridSpec(
            num_scalar_prefetch=1,
            grid=(1,),
            in_specs=[
                whole_spec(),
                full((3, rows, width)),
                full((rows, width)),
                full((rows, width)),
                full((12, width)),
            ],
            out_specs=[full((rows, width)), full((8, width))],
            scratch_shapes=[
                pltpu.VMEM((3, width, width), low),
                pltpu.VMEM((rows, width), wide),
                pltpu.SemaphoreType.DMA((3,)),
            ],
        ),
        out_shape=[shape((rows, width), low), shape((8, width), wide)],
        compiler_params=params(),
        name="input",
    )(place, whole, grad_project, patches, grad_middle, vectors)
    result = pl.pallas_call(
        result_kernel,
        grid_spec=pltpu.PrefetchScalarGridSpec(
            num_scalar_prefetch=1,
            grid=(hidden // PIECE,),
            in_specs=[
                whole_spec(),
                pl.BlockSpec((rows, PIECE), lambda c, *_: (0, c)),
                full((rows, width)),
                full((rows, 1)),
                full((12, width)),
            ],
            out_specs=full((rows, width)),
            scratch_shapes=[
                pltpu.VMEM((2, PIECE, width), low),
                pltpu.VMEM((rows, width), wide),
                pltpu.SemaphoreType.DMA((2,)),
            ],
        ),
        out_shape=shape((rows, width), low),
        compiler_params=params(),
        name="result",
    )(place, whole, active, middle, inside, vectors)
    vector_grad = jnp.concatenate(
        [sums_one[0:4], sums_two[0:3], sums_up.reshape(4, width), bias_down], axis=0
    )
    vector_sum = everywhere(vector_grad)

    owned, vector_sum, result = lax.optimization_barrier((owned, vector_sum, result))

    received = owned
    owned = jnp.where(named[:, None, None], owned.astype(wide), 0.0)
    squares = pl.pallas_call(
        squares_kernel,
        in_specs=[pl.BlockSpec(memory_space=pltpu.SMEM), full((held, size, size))],
        out_specs=full((devices, 128)),
        out_shape=shape((devices, 128), wide),
        grid=(),
        name="squares",
    )(named.astype(jnp.int32), received)
    total_blocks = jnp.sum(lax.all_to_all(squares, AXES, 0, 0, tiled=True)[:, 0])
    clip_norm = jnp.sqrt(total_blocks + jnp.sum(vector_sum * vector_sum))
    count = owners.shape[0] * size * size + vectors.shape[0] * width
    factor = jnp.minimum(1.0, 0.5 * math.sqrt(count) / clip_norm)
    turned = jnp.einsum("sji,sjk->sik", left_basis, owned, precision=high)
    rotated = factor * jnp.einsum("sik,skl->sil", turned, right_basis, precision=high)
    new_first = beta * first_moment + (1.0 - beta) * rotated
    new_second = beta * second_moment + (1.0 - beta) * rotated * rotated
    correction = 1.0 - beta**STEP
    direction = new_first / correction / (jnp.sqrt(new_second / correction) + adam_eps)
    back_turn = jnp.einsum("sij,sjk->sik", left_basis, direction, precision=high)
    update = jnp.einsum("sik,slk->sil", back_turn, right_basis, precision=high)
    new_master = master - rate_matrix * (update + decay_weight * master)
    vector_clip = factor * vector_sum
    new_vector_first = beta * vector_first + (1.0 - beta) * vector_clip
    new_vector_second = beta * vector_second + (1.0 - beta) * vector_clip * vector_clip
    vector_step = (
        new_vector_first / correction / (jnp.sqrt(new_vector_second / correction) + adam_eps)
    )
    new_vectors = vectors - rate_vector * vector_step
    return (
        result,
        grad_input,
        clip_norm,
        new_master,
        new_first,
        new_second,
        new_vectors,
        new_vector_first,
        new_vector_second,
    )


def solution(mesh):
    sizes = (mesh.shape["dp"], mesh.shape["fsdp"])
    rows = P(AXES, None)
    blocks = P(AXES, None, None)
    return jax.shard_map(
        functools.partial(shards, sizes),
        mesh=mesh,
        in_specs=(rows, rows, rows, P(), blocks, blocks, blocks, blocks, blocks, P(), P(), P()),
        out_specs=(rows, rows, P(), blocks, blocks, blocks, P(), P(), P()),
        check_vma=False,
    )
```

```python
import functools
import math

import jax
import jax.numpy as jnp
from jax import lax
from jax.experimental import pallas as pl
from jax.experimental.pallas import tpu as pltpu
from jax.sharding import PartitionSpec as P

HEADS = 12
STEP = 2
AXES = ("dp", "fsdp")

norm_eps = 1e-06
adam_eps = 1e-08
beta = 0.5
rate_matrix = 0.03
rate_vector = 0.05
decay_weight = 0.01
high = lax.Precision.HIGH
far = 2.0**30
low = jnp.bfloat16
wide = jnp.float32

CHUNK = 1024
PIECE = 256


def ring_order(dp, fsdp):
    if (dp, fsdp) != (8, 4):
        return None
    order = []
    for turn, (x, y) in enumerate(((0, 0), (1, 0), (1, 1), (0, 1))):
        places = range(4) if turn % 2 == 0 else range(3, -1, -1)
        for z in places:
            order += [(z * 2 + x) * 4 + y * 2 + core for core in (0, 1)]
    return order


def mm(a, b, ca, cb):
    return lax.dot_general(a, b, (((ca,), (cb,)), ((), ())), preferred_element_type=wide)


def normal_parts(values):
    center = values - jnp.mean(values, axis=-1, keepdims=True)
    factor = lax.rsqrt(jnp.mean(center * center, axis=-1, keepdims=True) + norm_eps)
    return center * factor, factor


def norm_back(grad, normal, factor, gain):
    inner = grad * gain
    return factor * (
        inner
        - jnp.mean(inner, axis=-1, keepdims=True)
        - normal * jnp.mean(inner * normal, axis=-1, keepdims=True)
    )


def start_blocks(place, whole, target, sem, first, across, row0, col0, height, breadth):
    def one(r, carry):
        at = first + (row0 + r) * across + col0
        down = pl.ds(pl.multiple_of(r * 128, 128), 128)
        for c in range(breadth):
            pltpu.make_async_copy(
                whole.at[place[at + c]], target.at[down, pl.ds(c * 128, 128)], sem
            ).start()
        return carry

    lax.fori_loop(0, height, one, 0)


def store_blocks(place, source, buffer, sem, first, across, row0, col0, height, breadth):
    def one(r, carry):
        at = first + (row0 + r) * across + col0
        down = pl.ds(pl.multiple_of(r * 128, 128), 128)
        for c in range(breadth):
            pltpu.make_async_copy(
                source.at[down, pl.ds(c * 128, 128)], buffer.at[place[at + c]], sem
            ).start()
        return carry

    lax.fori_loop(0, height, one, 0)


def await_bytes(ref, sem):
    pltpu.make_async_copy(ref, ref, sem).wait()


TILE = 112


def tiles(rows):
    return rows // TILE


def rows_of(t):
    return pl.ds(pl.multiple_of(t * TILE, 16), TILE)


def ready_kernel(patches, cotangent, inside, vectors, normed, normed_t, grad_two, bias_down):
    rows, width = patches.shape

    def norm(t, total):
        at = rows_of(t)
        normal, _ = normal_parts(patches[at, :].astype(wide))
        normed[at, :] = (normal * vectors[0:1, :] + vectors[1:2, :]).astype(low)
        two = (inside[at, :] * cotangent[at, :].astype(wide)).astype(low)
        grad_two[at, :] = two
        return total + jnp.sum(two.astype(wide), axis=0, keepdims=True)

    bias_down[...] = lax.fori_loop(0, tiles(rows), norm, jnp.zeros((1, width), wide))
    normed_t[...] = normed[...].T


def qkv_kernel(place, whole, normed, vectors, project, weight, sems):
    rows, width = normed.shape
    side = width // 128
    for part in range(3):
        start_blocks(
            place, whole, weight.at[part], sems.at[part], 0, 3 * side, 0, part * side, side, side
        )
    for part in range(3):
        await_bytes(weight.at[part], sems.at[part])
        out = mm(normed[...], weight[part], 1, 0)
        if part == 0:
            out = out + vectors[2:3, :]
        if part == 2:
            out = out + vectors[3:4, :]
        project[:, part * width : (part + 1) * width] = out.astype(low)


def attend_kernel(query, keys, values, image_query, image_keys, mixed, probs, scores):
    rows = query.shape[0]
    lane = lax.broadcasted_iota(jnp.int32, (rows, 128), 1)
    wide_keys = jnp.concatenate([keys[...], image_keys[...]], axis=1)
    scaled = query[...] * jnp.asarray(0.125, low)
    outs = []
    for h in range(2):
        part = jnp.where(lane // 64 == h, scaled, jnp.zeros_like(scaled))
        scores[h] = mm(jnp.concatenate([part, image_query[...]], axis=1), wide_keys, 1, 1)
    for h in range(2):
        for t in range(tiles(rows)):
            at = slice(t * TILE, (t + 1) * TILE)
            s = scores[h, at, :]
            e = jnp.exp(s - jnp.max(s, axis=-1, keepdims=True))
            total = jnp.sum(e, axis=-1, keepdims=True)
            probs[h, at, :] = (e * (1.0 / total)).astype(low)
        outs.append(mm(probs[h], values[...], 1, 0))
    mixed[...] = jnp.where(lane < 64, outs[0], outs[1]).astype(low)


def feed_kernel(
    place,
    whole,
    patches,
    cotangent,
    grad_two,
    mixed,
    inside,
    vectors,
    bias_up,
    middle,
    active,
    grad_middle,
    grad_mixed,
    sums,
    sums_up,
    buffer,
    w_out,
    w_up,
    w_down,
    normal,
    factor,
    second,
    second_t,
    out_sum,
    back_sum,
    stage_up,
    stage_down,
    stage_out,
    grad_pre,
    sems,
    out_sems,
):
    step = pl.program_id(0)
    steps = pl.num_programs(0)
    rows, width = patches.shape
    side = width // 128
    hidden = 4 * width
    high = hidden // 128
    per = CHUNK // 128
    first_out = 3 * side * side
    first_up = 4 * side * side
    first_down = first_up + side * high

    def fetch(index, slot):
        start_blocks(
            place, whole, w_up.at[slot], sems.at[slot], first_up, high, 0, index * per, side, per
        )
        start_blocks(
            place, whole, w_down.at[slot], sems.at[2 + slot], first_down, side, index * per, 0, per, side
        )

    @pl.when(step == 0)
    def _():
        start_blocks(place, whole, w_out, sems.at[4], first_out, side, 0, 0, side, side)
        fetch(0, 0)
        await_bytes(w_out, sems.at[4])
        out_sum[...] = mm(mixed[...], w_out[...], 1, 0)

        def norm(t, carry):
            at = rows_of(t)
            keep = inside[at, :]
            mid = patches[at, :].astype(wide) + keep * (out_sum[at, :] + vectors[4:5, :])
            middle[at, :] = mid
            scaled, q = normal_parts(mid)
            normal[at, :] = scaled
            factor[at, :] = q
            second[at, :] = (scaled * vectors[5:6, :] + vectors[6:7, :]).astype(low)
            return carry

        lax.fori_loop(0, tiles(rows), norm, 0)
        second_t[...] = second[...].T
        back_sum[...] = jnp.zeros_like(back_sum)
        fetch(1, 1)

    slot = lax.rem(step, 2)
    await_bytes(w_up.at[slot], sems.at[slot])
    await_bytes(w_down.at[slot], sems.at[2 + slot])

    @pl.when(step >= 2)
    def _():
        await_bytes(stage_up.at[slot], out_sems.at[slot])
        await_bytes(stage_down.at[slot], out_sems.at[2 + slot])

    parts = [slice(h * 256, (h + 1) * 256) for h in range(CHUNK // 256)]
    pres = [mm(second[...], w_up[slot, :, p], 1, 0) + bias_up[0, :, p] for p in parts]
    grads = [mm(grad_two[...], w_down[slot, p, :], 1, 1) for p in parts]
    for p, pre, grad in zip(parts, pres, grads):
        half = 0.5 * (1.0 + lax.erf(pre * math.sqrt(0.5)))
        active[:, p] = (pre * half).astype(low)
        slope = half + pre * (jnp.exp(-0.5 * pre * pre) * (1.0 / math.sqrt(2.0 * math.pi)))
        back = (grad * slope).astype(low)
        grad_pre[:, p] = back
        sums_up[0, :, p] = jnp.sum(back.astype(wide), axis=0, keepdims=True)
        stage_up[slot, :, p] = mm(second_t[...], grad_pre[:, p], 1, 0).astype(low)
        stage_down[slot, p, :] = mm(active[:, p], grad_two[...], 0, 0).astype(low)
    back_sum[...] += mm(grad_pre[...], w_up[slot], 1, 1)
    store_blocks(
        place, stage_up.at[slot], buffer, out_sems.at[slot], first_up, high, 0, step * per, side, per
    )
    store_blocks(
        place, stage_down.at[slot], buffer, out_sems.at[2 + slot], first_down, side, step * per, 0, per, side
    )

    @pl.when(step + 2 < steps)
    def _():
        fetch(step + 2, slot)

    @pl.when(step == steps - 1)
    def _():
        def finish(t, total):
            at = rows_of(t)
            keep = inside[at, :]
            grad = back_sum[at, :]
            scaled = normal[at, :]
            mid = cotangent[at, :].astype(wide) + norm_back(
                grad, scaled, factor[at, :], vectors[5:6, :]
            )
            grad_middle[at, :] = mid
            one = (keep * mid).astype(low)
            second[at, :] = one
            gain, shift, bias = total
            return (
                gain + jnp.sum(grad * scaled, axis=0, keepdims=True),
                shift + jnp.sum(grad, axis=0, keepdims=True),
                bias + jnp.sum(one.astype(wide), axis=0, keepdims=True),
            )

        empty = jnp.zeros((1, width), wide)
        gain, shift, bias = lax.fori_loop(0, tiles(rows), finish, (empty, empty, empty))
        sums[0:1, :] = bias
        sums[1:2, :] = gain
        sums[2:3, :] = shift
        sums[3:8, :] = jnp.zeros((5, width), wide)
        stage_out[...] = mm(mixed[...], second[...], 0, 0).astype(low)
        store_blocks(place, stage_out, buffer, out_sems.at[4], first_out, side, 0, 0, side, side)
        grad_mixed[...] = mm(second[...], w_out[...], 1, 1).astype(low)
        for other in range(2):
            await_bytes(stage_up.at[other], out_sems.at[other])
            await_bytes(stage_down.at[other], out_sems.at[2 + other])
        await_bytes(stage_out, out_sems.at[4])


def back_kernel(
    place,
    held,
    query,
    keys,
    values,
    probs,
    grad_mixed,
    mixed,
    normed_t,
    grad_project,
    buffer,
    grad_low,
    stage,
    out_sems,
):
    del held
    step = pl.program_id(0)
    steps = pl.num_programs(0)
    width, rows = normed_t.shape
    side = width // 128
    scale = 0.125
    lane = lax.broadcasted_iota(jnp.int32, (rows, 128), 1)
    grad = grad_mixed[...]
    grad_t = grad.T
    query_t = query[...].T
    outer = grad.astype(wide) * mixed[...].astype(wide)
    mine = [lane // 64 == h for h in range(2)]
    grad_probs = [
        mm(jnp.where(mine[h], grad, jnp.zeros_like(grad)), values[...], 1, 1) for h in range(2)
    ]
    turned_values = [mm(grad_t[h * 64 : (h + 1) * 64, :], probs[h], 1, 0) for h in range(2)]
    turned_query = []
    turned_keys = []
    for h in range(2):
        delta = jnp.sum(jnp.where(mine[h], outer, 0.0), axis=-1, keepdims=True)
        grad_low[h] = (probs[h].astype(wide) * (grad_probs[h] - delta)).astype(low)
        turned_query.append(mm(grad_low[h], keys[...], 1, 0))
        turned_keys.append(mm(query_t[h * 64 : (h + 1) * 64, :], grad_low[h], 1, 0))
    grad_query = jnp.where(lane < 64, turned_query[0], turned_query[1]) * scale
    grad_keys = (jnp.concatenate(turned_keys, axis=0) * scale).T
    grad_values = jnp.concatenate(turned_values, axis=0).T
    at = pl.multiple_of(step * 128, 128)
    for part, value in enumerate((grad_query, grad_keys, grad_values)):
        grad_project[part, :, pl.ds(at, 128)] = value.astype(low)

    @pl.when(step == steps - 1)
    def _():
        for part in range(3):
            if part == 2:
                await_bytes(stage.at[0], out_sems.at[0])
            stage[part % 2] = mm(normed_t[...], grad_project[part], 1, 0).astype(low)
            store_blocks(
                place,
                stage.at[part % 2],
                buffer,
                out_sems.at[part % 2],
                0,
                3 * side,
                0,
                part * side,
                side,
                side,
            )
        await_bytes(stage.at[1], out_sems.at[1])
        await_bytes(stage.at[0], out_sems.at[0])


def result_kernel(place, whole, active, middle, inside, vectors, result, w_down, total, sems):
    step = pl.program_id(0)
    steps = pl.num_programs(0)
    rows, width = middle.shape
    side = width // 128
    high = 4 * side
    per = PIECE // 128
    first_down = 4 * side * side + side * high

    def fetch(index, slot):
        start_blocks(
            place, whole, w_down.at[slot], sems.at[slot], first_down, side, index * per, 0, per, side
        )

    @pl.when(step == 0)
    def _():
        total[...] = jnp.zeros_like(total)
        fetch(0, 0)
        fetch(1, 1)

    slot = lax.rem(step, 2)
    await_bytes(w_down.at[slot], sems.at[slot])
    total[...] += mm(active[...], w_down[slot], 1, 0)

    @pl.when(step + 2 < steps)
    def _():
        fetch(step + 2, slot)

    @pl.when(step == steps - 1)
    def _():
        def finish(t, carry):
            at = rows_of(t)
            result[at, :] = (
                middle[at, :] + inside[at, :] * (total[at, :] + vectors[11:12, :])
            ).astype(low)
            return carry

        lax.fori_loop(0, tiles(rows), finish, 0)


def input_kernel(
    place, whole, grad_project, patches, grad_middle, vectors, grad_input, sums, weight, grad_sum, sems
):
    rows, width = patches.shape
    side = width // 128
    for part in range(3):
        start_blocks(
            place, whole, weight.at[part], sems.at[part], 0, 3 * side, 0, part * side, side, side
        )
    grad_sum[...] = jnp.zeros_like(grad_sum)

    def product(part, carry):
        await_bytes(weight.at[part], sems.at[part])
        grad_sum[...] += mm(grad_project[part], weight[part], 1, 1)
        return carry

    lax.fori_loop(0, 3, product, 0)

    def finish(t, carry):
        at = rows_of(t)
        grad = grad_sum[at, :]
        normal, factor = normal_parts(patches[at, :].astype(wide))
        back = norm_back(grad, normal, factor, vectors[0:1, :])
        grad_input[at, :] = (grad_middle[at, :] + back).astype(low)
        gain, shift, bias_query, bias_value = carry
        return (
            gain + jnp.sum(grad * normal, axis=0, keepdims=True),
            shift + jnp.sum(grad, axis=0, keepdims=True),
            bias_query + jnp.sum(grad_project[0, at, :].astype(wide), axis=0, keepdims=True),
            bias_value + jnp.sum(grad_project[2, at, :].astype(wide), axis=0, keepdims=True),
        )

    empty = jnp.zeros((1, width), wide)
    found = lax.fori_loop(0, tiles(rows), finish, (empty, empty, empty, empty))
    for row in range(4):
        sums[row : row + 1, :] = found[row]
    sums[4:8, :] = jnp.zeros((4, width), wide)


def squares_kernel(named, grads, spread):
    total = jnp.zeros((128, 128), wide)
    for s in range(grads.shape[0]):
        block = jnp.where(named[s] > 0, grads[s].astype(wide), 0.0)
        total = total + block * block
    spread[...] = jnp.broadcast_to(jnp.sum(total), spread.shape)


VMEM_LIMIT = 60 * 1024 * 1024


def params(count=1):
    return pltpu.CompilerParams(
        dimension_semantics=("arbitrary",) * count, vmem_limit_bytes=VMEM_LIMIT
    )


def whole_spec():
    return pl.BlockSpec(memory_space=pl.ANY)


def full(shape):
    return pl.BlockSpec(shape, lambda *_: (0,) * len(shape))


def shards(
    sizes,
    patches,
    lengths,
    cotangent,
    owners,
    master,
    first_moment,
    second_moment,
    left_basis,
    right_basis,
    vectors,
    vector_first,
    vector_second,
):
    dp, fsdp = sizes
    devices = dp * fsdp
    rows, width = patches.shape
    hidden = 4 * width
    side = width // 128
    pairs = width // 128
    held, size = master.shape[0], master.shape[1]
    slots = held * devices
    shape = jax.ShapeDtypeStruct
    me = lax.axis_index(AXES)
    order = ring_order(dp, fsdp)
    groups = None if order is None else [order]

    def gather(value):
        return lax.all_gather(value, AXES, axis=0, tiled=True, axis_index_groups=groups)

    def scatter(value):
        return lax.psum_scatter(
            value, AXES, scatter_dimension=0, tiled=True, axis_index_groups=groups
        )

    def everywhere(value):
        step = 1
        while step < devices:
            value = value + lax.ppermute(value, AXES, [(d, d ^ step) for d in range(devices)])
            step *= 2
        return value

    whole = gather(master.astype(low))
    if order is None:
        place = owners
    else:
        rank = [0] * devices
        for spot, device in enumerate(order):
            rank[device] = spot
        device = owners // held
        spot = jnp.sum(
            jnp.where(
                device[:, None] == jnp.arange(devices, dtype=jnp.int32)[None, :],
                jnp.array(rank, jnp.int32)[None, :],
                0,
            ),
            axis=1,
        )
        place = spot * held + owners % held
    mine = me * held + jnp.arange(held, dtype=jnp.int32)
    named = jnp.any(mine[:, None] == owners[None, :], axis=1)

    counts = lengths[0]
    ends = jnp.cumsum(counts)
    places = jnp.arange(rows, dtype=jnp.int32)[:, None]
    image = jnp.sum((places >= ends[None, :]).astype(jnp.int32), axis=1, keepdims=True)
    within = places < ends[-1]
    image = jnp.where(within, image, 4)
    inside = within.astype(wide)
    lanes = jnp.arange(128, dtype=jnp.int32)[None, :]
    image_keys = (lanes == image).astype(low)
    image_query = jnp.where((lanes != image) & (lanes < 5), -far, 0.0).astype(low)

    normed, normed_t, grad_two, bias_down = pl.pallas_call(
        ready_kernel,
        out_shape=[
            shape((rows, width), low),
            shape((width, rows), low),
            shape((rows, width), low),
            shape((1, width), wide),
        ],
        compiler_params=pltpu.CompilerParams(vmem_limit_bytes=VMEM_LIMIT),
        name="ready",
    )(patches, cotangent, inside, vectors)

    project = pl.pallas_call(
        qkv_kernel,
        grid_spec=pltpu.PrefetchScalarGridSpec(
            num_scalar_prefetch=1,
            grid=(1,),
            in_specs=[whole_spec(), full((rows, width)), full((12, width))],
            out_specs=full((rows, 3 * width)),
            scratch_shapes=[
                pltpu.VMEM((3, width, width), low),
                pltpu.SemaphoreType.DMA((3,)),
            ],
        ),
        out_shape=shape((rows, 3 * width), low),
        compiler_params=params(),
        name="qkv",
    )(place, whole, normed, vectors)

    def column(offset):
        return pl.BlockSpec((rows, 128), lambda j, *_: (0, j + offset))

    mixed, probs = pl.pallas_call(
        attend_kernel,
        grid=(pairs,),
        in_specs=[
            column(0),
            column(pairs),
            column(2 * pairs),
            full((rows, 128)),
            full((rows, 128)),
        ],
        out_specs=[column(0), pl.BlockSpec((2, rows, rows), lambda j: (j, 0, 0))],
        out_shape=[shape((rows, width), low), shape((HEADS, rows, rows), low)],
        scratch_shapes=[pltpu.VMEM((2, rows, rows), wide)],
        compiler_params=params(),
        name="attend",
    )(project, project, project, image_query, image_keys)

    steps = hidden // CHUNK
    middle, active, grad_middle, grad_mixed, sums_two, sums_up, buffer = pl.pallas_call(
        feed_kernel,
        grid_spec=pltpu.PrefetchScalarGridSpec(
            num_scalar_prefetch=1,
            grid=(steps,),
            in_specs=[
                whole_spec(),
                full((rows, width)),
                full((rows, width)),
                full((rows, width)),
                full((rows, width)),
                full((rows, 1)),
                full((12, width)),
                pl.BlockSpec((1, 1, CHUNK), lambda c, *_: (c, 0, 0)),
            ],
            out_specs=[
                full((rows, width)),
                pl.BlockSpec((rows, CHUNK), lambda c, *_: (0, c)),
                full((rows, width)),
                full((rows, width)),
                full((8, width)),
                pl.BlockSpec((1, 1, CHUNK), lambda c, *_: (c, 0, 0)),
                whole_spec(),
            ],
            scratch_shapes=[
                pltpu.VMEM((width, width), low),
                pltpu.VMEM((2, width, CHUNK), low),
                pltpu.VMEM((2, CHUNK, width), low),
                pltpu.VMEM((rows, width), wide),
                pltpu.VMEM((rows, 1), wide),
                pltpu.VMEM((rows, width), low),
                pltpu.VMEM((width, rows), low),
                pltpu.VMEM((rows, width), wide),
                pltpu.VMEM((rows, width), wide),
                pltpu.VMEM((2, width, CHUNK), low),
                pltpu.VMEM((2, CHUNK, width), low),
                pltpu.VMEM((width, width), low),
                pltpu.VMEM((rows, CHUNK), low),
                pltpu.SemaphoreType.DMA((5,)),
                pltpu.SemaphoreType.DMA((5,)),
            ],
        ),
        out_shape=[
            shape((rows, width), wide),
            shape((rows, hidden), low),
            shape((rows, width), wide),
            shape((rows, width), low),
            shape((8, width), wide),
            shape((steps, 1, CHUNK), wide),
            shape((slots, size, size), low),
        ],
        compiler_params=params(),
        name="feed",
    )(
        place,
        whole,
        patches,
        cotangent,
        grad_two,
        mixed,
        inside,
        vectors,
        vectors[7:11].reshape(steps, 1, CHUNK),
    )

    grad_project, buffer = pl.pallas_call(
        back_kernel,
        grid_spec=pltpu.PrefetchScalarGridSpec(
            num_scalar_prefetch=1,
            grid=(pairs,),
            in_specs=[
                whole_spec(),
                column(0),
                column(pairs),
                column(2 * pairs),
                pl.BlockSpec((2, rows, rows), lambda j, *_: (j, 0, 0)),
                column(0),
                column(0),
                full((width, rows)),
            ],
            out_specs=[full((3, rows, width)), whole_spec()],
            scratch_shapes=[
                pltpu.VMEM((2, rows, rows), low),
                pltpu.VMEM((2, width, width), low),
                pltpu.SemaphoreType.DMA((2,)),
            ],
        ),
        out_shape=[
            shape((3, rows, width), low),
            shape((slots, size, size), low),
        ],
        input_output_aliases={1: 1},
        compiler_params=params(),
        name="back",
    )(
        place,
        buffer,
        project,
        project,
        project,
        probs,
        grad_mixed,
        mixed,
        normed_t,
    )
    owned = scatter(buffer)

    grad_input, sums_one = pl.pallas_call(
        input_kernel,
        grid_spec=pltpu.PrefetchScalarGridSpec(
            num_scalar_prefetch=1,
            grid=(1,),
            in_specs=[
                whole_spec(),
                full((3, rows, width)),
                full((rows, width)),
                full((rows, width)),
                full((12, width)),
            ],
            out_specs=[full((rows, width)), full((8, width))],
            scratch_shapes=[
                pltpu.VMEM((3, width, width), low),
                pltpu.VMEM((rows, width), wide),
                pltpu.SemaphoreType.DMA((3,)),
            ],
        ),
        out_shape=[shape((rows, width), low), shape((8, width), wide)],
        compiler_params=params(),
        name="input",
    )(place, whole, grad_project, patches, grad_middle, vectors)
    result = pl.pallas_call(
        result_kernel,
        grid_spec=pltpu.PrefetchScalarGridSpec(
            num_scalar_prefetch=1,
            grid=(hidden // PIECE,),
            in_specs=[
                whole_spec(),
                pl.BlockSpec((rows, PIECE), lambda c, *_: (0, c)),
                full((rows, width)),
                full((rows, 1)),
                full((12, width)),
            ],
            out_specs=full((rows, width)),
            scratch_shapes=[
                pltpu.VMEM((2, PIECE, width), low),
                pltpu.VMEM((rows, width), wide),
                pltpu.SemaphoreType.DMA((2,)),
            ],
        ),
        out_shape=shape((rows, width), low),
        compiler_params=params(),
        name="result",
    )(place, whole, active, middle, inside, vectors)
    vector_grad = jnp.concatenate(
        [sums_one[0:4], sums_two[0:3], sums_up.reshape(4, width), bias_down], axis=0
    )
    vector_sum = everywhere(vector_grad)

    owned, vector_sum, result = lax.optimization_barrier((owned, vector_sum, result))

    received = owned
    owned = jnp.where(named[:, None, None], owned.astype(wide), 0.0)
    squares = pl.pallas_call(
        squares_kernel,
        in_specs=[pl.BlockSpec(memory_space=pltpu.SMEM), full((held, size, size))],
        out_specs=full((devices, 128)),
        out_shape=shape((devices, 128), wide),
        grid=(),
        name="squares",
    )(named.astype(jnp.int32), received)
    total_blocks = jnp.sum(lax.all_to_all(squares, AXES, 0, 0, tiled=True)[:, 0])
    clip_norm = jnp.sqrt(total_blocks + jnp.sum(vector_sum * vector_sum))
    count = owners.shape[0] * size * size + vectors.shape[0] * width
    factor = jnp.minimum(1.0, 0.5 * math.sqrt(count) / clip_norm)
    turned = jnp.einsum("sji,sjk->sik", left_basis, owned, precision=high)
    rotated = factor * jnp.einsum("sik,skl->sil", turned, right_basis, precision=high)
    new_first = beta * first_moment + (1.0 - beta) * rotated
    new_second = beta * second_moment + (1.0 - beta) * rotated * rotated
    correction = 1.0 - beta**STEP
    direction = new_first / correction / (jnp.sqrt(new_second / correction) + adam_eps)
    back_turn = jnp.einsum("sij,sjk->sik", left_basis, direction, precision=high)
    update = jnp.einsum("sik,slk->sil", back_turn, right_basis, precision=high)
    new_master = master - rate_matrix * (update + decay_weight * master)
    vector_clip = factor * vector_sum
    new_vector_first = beta * vector_first + (1.0 - beta) * vector_clip
    new_vector_second = beta * vector_second + (1.0 - beta) * vector_clip * vector_clip
    vector_step = (
        new_vector_first / correction / (jnp.sqrt(new_vector_second / correction) + adam_eps)
    )
    new_vectors = vectors - rate_vector * vector_step
    return (
        result,
        grad_input,
        clip_norm,
        new_master,
        new_first,
        new_second,
        new_vectors,
        new_vector_first,
        new_vector_second,
    )


def solution(mesh):
    sizes = (mesh.shape["dp"], mesh.shape["fsdp"])
    rows = P(AXES, None)
    blocks = P(AXES, None, None)
    return jax.shard_map(
        functools.partial(shards, sizes),
        mesh=mesh,
        in_specs=(rows, rows, rows, P(), blocks, blocks, blocks, blocks, blocks, P(), P(), P()),
        out_specs=(rows, rows, P(), blocks, blocks, blocks, P(), P(), P()),
        check_vma=False,
    )
```
